32 devices in a mesh: dp: 8 (over z, y), head: 4 (over x, core).
Axes of the slice: x: 2, y: 2, z: 4, core: 2. Of those that a mesh axis runs over, the one named last changes fastest.
Arguments:
- tokens: bfloat16 [16384, 768], P(('dp', 'head')), may hold values from -12 to 12
- lengths: int32 [8, 8], P('dp'), may hold values from 1 to 512, 1592 in all within a row
- box_cells: int32 [2, 16384], P(None, 'dp'), may hold values from 0 to 63
- bn_gain: float32 [768], replicated, may hold values from 0.1 to 1.9
- bn_shift: float32 [768], replicated, may hold values from -3 to 3
- query_key_value_weight: bfloat16 [3, 768, 768], P(None, None, 'head'), may hold values from -0.21875 to 0.21875
- b_qv: float32 [2, 768], P(None, 'head'), may hold values from -3 to 3
- tab_pos: float32 [12, 32], P('head'), may hold values from -3 to 3
- tab_box: float32 [2, 12, 64], P(None, 'head'), may hold values from -3 to 3
- w_out: bfloat16 [768, 768], P('head'), may hold values from -0.875 to 0.875
- b_out: float32 [768], replicated, may hold values from -3 to 3
- ln1_gain: float32 [768], replicated, may hold values from 0.5 to 1.5
- ln1_shift: float32 [768], replicated, may hold values from -3 to 3
- w_up: bfloat16 [768, 3072], P(None, 'head'), may hold values from -0.21875 to 0.21875
- b_up: float32 [3072], P('head'), may hold values from -3 to 3
- w_down: bfloat16 [3072, 768], P('head'), may hold values from -0.109375 to 0.109375
- b_down: float32 [768], replicated, may hold values from -3 to 3
- ln2_gain: float32 [768], replicated, may hold values from 0.5 to 1.5
- ln2_shift: float32 [768], replicated, may hold values from -3 to 3
- cotangent: bfloat16 [16384, 768], P(('dp', 'head')), may hold values from -6 to 6
Outputs:
- layer_out: bfloat16 [16384, 768], P(('dp', 'head'))
- grad_tokens: float32 [16384, 768], P(('dp', 'head'))
- grad_bn_gain: float32 [768], replicated
- grad_bn_shift: float32 [768], replicated
- projection_weight_gradient: float32 [3, 768, 768], P(None, None, 'head')
- grad_b_qv: float32 [2, 768], P(None, 'head')
- grad_tab_pos: float32 [12, 32], P('head')
- grad_tab_box: float32 [2, 12, 64], P(None, 'head')
- grad_w_out: float32 [768, 768], P('head')
- grad_b_out: float32 [768], replicated
- grad_ln1_gain: float32 [768], replicated
- grad_ln1_shift: float32 [768], replicated
- grad_w_up: float32 [768, 3072], P(None, 'head')
- grad_b_up: float32 [3072], P('head')
- grad_w_down: float32 [3072, 768], P('head')
- grad_b_down: float32 [768], replicated
- grad_ln2_gain: float32 [768], replicated
- grad_ln2_shift: float32 [768], replicated
The draws below stay inside these ranges and needn't reach their ends.
Inputs may be any that keep to these rules, and one draw needn't show every extreme that they name: Each row lists the text lengths of the 8 documents of one group in packing order; a row sums to 1592 and its longest is exactly 512.
All inputs are finite; a program needn't handle non-finite values.
Results may differ from the reference program's by a relative error of at most 0.017.
The reference program's roundings to bfloat16 on the way count: a program that leaves them out, or rounds other values in their place, can miss the bound.
Values may be sent and summed in bfloat16 or wider, within the bound.
A program may use at most 256 MiB of HBM per device.

```python
import math
import jax
import jax.numpy as jnp
import numpy as np
from jax import lax

D = 768
HEADS = 12
DH = 64
FF = 3072
VISUAL = 49
POSB = 32
BOXB = 64
DOCS = 8
GROUP = 2048
TEXT = 1592
MOST = 512
TOKENS = 16384
VIS_ROWS = 3136
N_DP = 8


def draw_tokens(key, part):
    row_pos = jnp.arange(TOKENS, dtype=jnp.float32)[:, None] / TOKENS
    row_scale = 0.5 * jnp.exp(row_pos * math.log(3.0))
    col_scale = jnp.exp(jax.random.uniform(jax.random.fold_in(key, 7), (1, D), jnp.float32, -0.6, 0.6))
    values = jnp.clip(jax.random.normal(jax.random.fold_in(key, 11), (TOKENS, D), jnp.float32), -4.0, 4.0) * row_scale * col_scale
    return values.astype(jnp.bfloat16)


def plant(values, rng, low, largest):
    longest = values.shape.index(max(values.shape))
    spots = []
    for shift in (0, 1):
        where = [jax.random.randint(jax.random.fold_in(rng, axis), (), 0, length) for axis, length in enumerate(values.shape)]
        where[longest] = (where[longest] + shift) % values.shape[longest]
        spots.append(tuple(where))
    return values.at[spots[0]].set(low).at[spots[1]].set(largest)


def steps_of(stream_key, dims, cuts, least, largest):
    def one(dim, shards_of):
        draws = jax.random.uniform(jax.random.fold_in(jax.random.fold_in(stream_key, 6), dim), (shards_of,), jnp.float32, least / len(cuts), largest / len(cuts))
        return jnp.repeat(jnp.exp(draws), dims[dim] // shards_of).reshape((-1,) + (1,) * (len(dims) - dim - 1))

    loudness = one(*cuts[0])
    for cut in cuts[1:]:
        loudness = loudness * one(*cut)
    return loudness


def split_up(number_of, total, limit, slope):
    portions = [(1 << 20) // math.isqrt(grade ** slope) + 1 for grade in range(2, number_of + 1)]
    surplus, counts = total - limit - (number_of - 1), [1] * (number_of - 1)
    while surplus > 0:
        movable = [i for i in range(number_of - 1) if counts[i] < limit]
        pool, budget = sum([portions[i] for i in movable]), surplus
        for i in movable:
            more = min(limit - counts[i], max(1, budget * portions[i] // pool), surplus)
            counts[i] = counts[i] + more
            surplus = surplus - more
    return np.array([limit] + counts)


def ragged_sizes(stream_key, amount, total, reach, skew):
    if amount == 2:
        one = jax.random.randint(stream_key, (), max(1, total - reach), min(reach, total - 1) + 1)
        return jnp.stack([one, total - one])
    tallies = jnp.asarray(split_up(amount, total, reach, skew), jnp.int32)
    pairs = (amount - 1) // 2
    giver, taker = tallies[1:1 + 2 * pairs:2], tallies[2:2 + 2 * pairs:2]
    room = jnp.minimum(giver - 1, reach - taker)
    moved = jax.random.randint(jax.random.fold_in(stream_key, 1), (pairs,), 0, 1 << 20) % (room + 1)
    tallies = tallies.at[1:1 + 2 * pairs:2].set(giver - moved).at[2:2 + 2 * pairs:2].set(taker + moved)
    return tallies[jax.random.permutation(jax.random.fold_in(stream_key, 2), amount)]


def bell_draw(rng, dims, width, most, split=(), kind=jnp.bfloat16):
    level = steps_of(rng, dims, split, -0.22, 0.18) if split else 1.0
    values = jax.random.normal(rng, dims, jnp.float32) * width * level
    return jnp.minimum(jnp.maximum(values, -most), most).astype(kind)


def setup_inputs(seed: int = 0) -> dict:
    key_of = jax.random.split(jax.random.key(seed), 21)
    return {
        "tokens": draw_tokens(jax.random.fold_in(key_of[20], 71), 0),
        "lengths": jax.vmap(lambda own: ragged_sizes(own, DOCS, TEXT, MOST, 2))(jax.random.split(key_of[1], N_DP)).reshape((N_DP, DOCS)).astype(jnp.int32),
        "box_cells": plant(jax.random.randint(key_of[2], (2, TOKENS), 0, BOXB), jax.random.fold_in(key_of[2], 1), 0, BOXB - 1).astype(jnp.int32),
        "bn_gain": jnp.clip(1.0 + 0.18 * jax.random.normal(key_of[3], (D,), jnp.float32), 0.1, 1.9),
        "bn_shift": bell_draw(key_of[4], (D,), 0.5, 3.0, (), jnp.float32),
        "query_key_value_weight": bell_draw(key_of[5], (3, D, D), D ** -0.5, 0.21875, ((2, 4),)),
        "b_qv": bell_draw(key_of[6], (2, D), 0.5, 3.0, ((1, 4),), jnp.float32),
        "tab_pos": bell_draw(key_of[7], (HEADS, POSB), 0.5, 3.0, ((0, 4),), jnp.float32),
        "tab_box": bell_draw(key_of[8], (2, HEADS, BOXB), 0.5, 3.0, ((1, 4),), jnp.float32),
        "w_out": bell_draw(key_of[9], (D, D), (D // 16) ** -0.5, 0.875, ((0, 4),)),
        "b_out": bell_draw(key_of[10], (D,), 0.5, 3.0, (), jnp.float32),
        "ln1_gain": jnp.clip(1.0 + 0.1 * jax.random.normal(key_of[11], (D,), jnp.float32), 0.5, 1.5),
        "ln1_shift": bell_draw(key_of[12], (D,), 0.5, 3.0, (), jnp.float32),
        "w_up": bell_draw(key_of[13], (D, FF), D ** -0.5, 0.21875, ((1, 4),)),
        "b_up": bell_draw(key_of[14], (FF,), 0.5, 3.0, ((0, 4),), jnp.float32),
        "w_down": bell_draw(key_of[15], (FF, D), FF ** -0.5, 0.109375, ((0, 4),)),
        "b_down": bell_draw(key_of[16], (D,), 0.5, 3.0, (), jnp.float32),
        "ln2_gain": jnp.clip(1.0 + 0.1 * jax.random.normal(key_of[17], (D,), jnp.float32), 0.5, 1.5),
        "ln2_shift": bell_draw(key_of[18], (D,), 0.5, 3.0, (), jnp.float32),
        "cotangent": bell_draw(key_of[19], (TOKENS, D), 1.0, 6.0, ((0, 32),)),
    }


norm_eps = 1e-05
batch_eps = 1e-05
neg_big = -1e+30
pos_step = 16

@jax.custom_vjp
def low(v):
    return lax.optimization_barrier(v.astype(jnp.bfloat16)).astype(jnp.float32)

@jax.custom_vjp
def low_back(v):
    return v

def low_keep(v):
    return (low(v), None)

def low_pass(kept, grad):
    return (grad,)

def backward_retained(v):
    return (v, None)

def back_low(kept, grad):
    return (low(grad),)
low.defvjp(low_keep, low_pass)
low_back.defvjp(backward_retained, back_low)

def layout_rows(lengths, group_rows):
    doc_count = lengths.shape[0]
    doc_sizes = (lengths + VISUAL).astype(jnp.int32)
    doc_ends = jnp.cumsum(doc_sizes).astype(jnp.int32)
    starts = (doc_ends - doc_sizes).astype(jnp.int32)
    row_identifiers = jnp.arange(group_rows, dtype=jnp.int32)
    segment = lax.optimization_barrier(jnp.sum((row_identifiers[:, None] >= doc_ends[None, :]).astype(jnp.int32), axis=1)).astype(jnp.int32)
    owned_by = segment[:, None] == jnp.arange(doc_count, dtype=jnp.int32)[None, :]
    first_row = lax.optimization_barrier(jnp.sum(jnp.where(owned_by, starts[None, :], 0), axis=1)).astype(jnp.int32)
    first_row = first_row + jnp.where(segment == doc_count, doc_ends[doc_count - 1], 0).astype(jnp.int32)
    offset = row_identifiers - first_row
    visual = jnp.logical_and(segment < doc_count, offset < VISUAL)
    position = jnp.where(visual, offset, offset - VISUAL)
    bucket = jnp.minimum(jnp.maximum(position, 0) // pos_step, POSB - 1).astype(jnp.int32)
    return (segment, visual, bucket)

def toeplitz_map(buckets):
    bins_ids = jnp.arange(buckets, dtype=jnp.int32)
    relative = jnp.clip(bins_ids[None, :] - bins_ids[:, None], -(buckets // 2), buckets // 2 - 1) + buckets // 2
    return (relative[:, :, None] == bins_ids[None, None, :]).astype(jnp.float32)

def key_features(bucket, box_x, box_y, out_type):
    return jnp.concatenate([(bucket[..., None] == jnp.arange(POSB, dtype=jnp.int32)).astype(out_type), (box_x[..., None] == jnp.arange(BOXB, dtype=jnp.int32)).astype(out_type), (box_y[..., None] == jnp.arange(BOXB, dtype=jnp.int32)).astype(out_type)], axis=-1)

def norm_rows(h, gain_vec, shift_vec):
    row_mean = lax.optimization_barrier(jnp.mean(h, axis=-1, keepdims=True))
    centred = h - row_mean
    variance = lax.optimization_barrier(jnp.mean(centred * centred, axis=-1, keepdims=True))
    return centred * lax.rsqrt(variance + norm_eps) * gain_vec + shift_vec

def reference(tokens, lengths, box_cells, bn_gain, bn_shift, query_key_value_weight, b_qv, tab_pos, tab_box, w_out, b_out, ln1_gain, ln1_shift, w_up, b_up, w_down, b_down, ln2_gain, ln2_shift, cotangent):
    highest = lax.Precision.HIGHEST
    groups = lengths.shape[0]
    segment, visual, bucket = jax.vmap(lambda length_row: layout_rows(length_row, GROUP))(lengths)
    box_x = box_cells[0].reshape(groups, GROUP)
    box_y = box_cells[1].reshape(groups, GROUP)
    key_feat = key_features(bucket, box_x, box_y, jnp.float32)
    vis_rows = visual.reshape(TOKENS, 1)
    pos_map = toeplitz_map(POSB)
    box_map = toeplitz_map(BOXB)
    block_rows = min(512, GROUP)

    def attend_block(query_blk, feat_blk, seg_query, key_grp, value_grp, key_group_features, seg_key):
        scores = jnp.einsum('qhd,khd->hqk', query_blk, key_grp, precision=highest) * 0.125
        scores = scores + jnp.einsum('qhc,kc->hqk', feat_blk, key_group_features, precision=highest)
        scores = low_back(scores)
        scores = jnp.where((seg_query[:, None] == seg_key[None, :])[None], scores, neg_big)
        row_max = lax.optimization_barrier(jnp.max(scores, axis=2, keepdims=True))
        exp_scores = jnp.exp(scores - row_max)
        attn_prob = exp_scores / lax.optimization_barrier(jnp.sum(exp_scores, axis=2, keepdims=True))
        return jnp.einsum('hqk,khd->qhd', low(attn_prob), value_grp, precision=highest)
    attend = jax.checkpoint(attend_block)

    def attend_group(group_items):
        query_grp, key_grp, value_grp, feat_grp, key_group_features, seg_grp = group_items
        pieces = [attend(query_grp[row_start:row_start + block_rows], feat_grp[row_start:row_start + block_rows], seg_grp[row_start:row_start + block_rows], key_grp, value_grp, key_group_features, seg_grp) for row_start in range(0, GROUP, block_rows)]
        return jnp.concatenate(pieces, axis=0)

    def forward(x_val, gain_bn, shift_bn, qkv_w, qv_b, pos_tab, box_tab, out_w, out_b, gain_one, shift_one, up_w, up_b, down_w, down_b, gain_two, shift_two):
        col_sum = lax.optimization_barrier(jnp.sum(jnp.where(vis_rows, x_val, 0.0), axis=0))
        col_sq = lax.optimization_barrier(jnp.sum(jnp.where(vis_rows, x_val * x_val, 0.0), axis=0))
        row_mean = col_sum / VIS_ROWS
        variance = col_sq / VIS_ROWS - row_mean * row_mean
        x_hat = (x_val - row_mean) * lax.rsqrt(variance + batch_eps)
        x_in = jnp.where(vis_rows, x_hat * gain_bn + shift_bn, x_val)
        attention_input = low(x_in)
        query = low_back(low(jnp.dot(attention_input, qkv_w[0], precision=highest) + qv_b[0]))
        key_h = low_back(low(jnp.dot(attention_input, qkv_w[1], precision=highest)))
        value_h = low_back(low(jnp.dot(attention_input, qkv_w[2], precision=highest) + qv_b[1]))
        pos_low = low(pos_tab)
        box_low = low(box_tab)
        map_pos = jnp.einsum('abt,ht->hab', pos_map, pos_low, precision=highest)
        map_x = jnp.einsum('abt,ht->hab', box_map, box_low[0], precision=highest)
        map_y = jnp.einsum('abt,ht->hab', box_map, box_low[1], precision=highest)
        query_feat = jnp.concatenate([jnp.einsum('nga,hab->nghb', key_feat[..., :POSB], map_pos, precision=highest), jnp.einsum('nga,hab->nghb', key_feat[..., POSB:POSB + BOXB], map_x, precision=highest), jnp.einsum('nga,hab->nghb', key_feat[..., POSB + BOXB:], map_y, precision=highest)], axis=-1)
        shape4 = (groups, GROUP, HEADS, DH)
        attn_out = lax.map(attend_group, (query.reshape(shape4), key_h.reshape(shape4), value_h.reshape(shape4), query_feat, key_feat, segment))
        attn_out = low_back(low(attn_out.reshape(TOKENS, D)))
        attn_proj = low_back(jnp.dot(attn_out, out_w, precision=highest)) + out_b
        mid_norm = norm_rows(x_in + attn_proj, gain_one, shift_one)
        ffn_in = low(mid_norm)
        pre_act = low_back(jnp.dot(ffn_in, up_w, precision=highest) + up_b)
        gelu_out = low(jax.nn.gelu(pre_act, approximate=False))
        ffn_proj = low_back(jnp.dot(gelu_out, down_w, precision=highest)) + down_b
        return norm_rows(mid_norm + ffn_proj, gain_two, shift_two)
    primals = (tokens.astype(jnp.float32), bn_gain, bn_shift, query_key_value_weight.astype(jnp.float32), b_qv, tab_pos, tab_box, w_out.astype(jnp.float32), b_out, ln1_gain, ln1_shift, w_up.astype(jnp.float32), b_up, w_down.astype(jnp.float32), b_down, ln2_gain, ln2_shift)
    output, pullback = jax.vjp(forward, *primals)
    gradients = pullback(cotangent.astype(jnp.float32))
    return (output.astype(jnp.bfloat16), gradients[0], gradients[1], gradients[2], gradients[3], gradients[4], gradients[5], gradients[6], gradients[7], gradients[8], gradients[9], gradients[10], gradients[11], gradients[12], gradients[13], gradients[14], gradients[15], gradients[16])
```

```python
import functools

import jax
import jax.numpy as jnp
from jax import lax
from jax.experimental import pallas as pl
from jax.experimental.pallas import tpu as pltpu
from jax.sharding import PartitionSpec as P

DH = 64
VISUAL = 49
POSB = 32
BOXB = 64
POS_STEP = 16
NORM_EPS = 1e-05
BATCH_EPS = 1e-05
BIG = float(2.0**100)
BLK = 256
LANES = 128
SEG0 = 96
LSE0 = 112
VMEM_CAP = 58 << 20

MESH = pl.DeviceIdType.MESH
BF = jnp.bfloat16
F32 = jnp.float32
I32 = jnp.int32
VM = pl.BlockSpec(memory_space=pltpu.VMEM)
SM = pl.BlockSpec(memory_space=pltpu.SMEM)


def iota(shape, dim):
    return lax.broadcasted_iota(I32, shape, dim)


def mm(a, b):
    return jnp.dot(a, b, preferred_element_type=F32)


def mm_nt(a, b):
    return lax.dot_general(a, b, (((1,), (1,)), ((), ())), preferred_element_type=F32)


def mm_tn(a, b):
    return lax.dot_general(a, b, (((0,), (0,)), ((), ())), preferred_element_type=F32)


def head_peers():
    hd = lax.axis_index("head")
    sib = hd + 1 - 2 * lax.rem(hd, 2)
    cross = lax.rem(hd + 2, 4)
    diag = lax.rem(sib + 2, 4)
    return hd, sib, cross, diag


def row_layout(rows, lens):
    seg = jnp.zeros_like(rows)
    first = jnp.zeros_like(rows)
    end = 0
    for size in lens:
        end = end + size + VISUAL
        past = rows >= end
        seg = seg + past.astype(I32)
        first = jnp.where(past, end, first)
    offset = rows - first
    visual = jnp.logical_and(seg < len(lens), offset < VISUAL)
    position = jnp.where(visual, offset, offset - VISUAL)
    bucket = jnp.minimum(lax.shift_right_logical(jnp.maximum(position, 0), 4), POSB - 1)
    return seg, visual, bucket


def block_window(block, lens, group_rows):
    first, last = block * BLK, block * BLK + BLK - 1
    low, high, end = 0, group_rows, 0
    ends = []
    for size in lens:
        end = end + size + VISUAL
        ends.append(end)
        low = jnp.where(first >= end, end, low)
    for end in reversed(ends):
        high = jnp.where(last < end, end, high)
    return low // BLK, (high + BLK - 1) // BLK


def entry_kernel(
    len_ref,
    tok_ref,
    box_ref,
    gain_ref,
    shift_ref,
    w_ref,
    b_ref,
    tp_ref,
    tb_ref,
    xin_ref,
    a_ref,
    q0_ref,
    q1_ref,
    k0_ref,
    k1_ref,
    vx_ref,
    st_ref,
    abuf,
    hbuf,
    dbuf,
    map0,
    map1,
    hsend,
    hrecv,
    dsend,
    drecv,
    asend,
    arecv,
    osem,
):
    n_dp = dbuf.shape[0]
    own = tok_ref.shape[0]
    group = abuf.shape[0]
    docs = len_ref.shape[1]
    heads = w_ref.shape[2] // DH
    hd, sib, cross, diag = head_peers()
    dp = lax.axis_index("dp")
    lens = [len_ref[0, d] for d in range(docs)]

    barrier = pltpu.get_barrier_semaphore()
    for peer in (sib, cross, diag):
        pl.semaphore_signal(barrier, inc=1, device_id={"head": peer}, device_id_type=MESH)

    def greet(j, carry):
        pl.semaphore_signal(
            barrier, inc=1, device_id={"dp": lax.rem(dp + j, n_dp)}, device_id_type=MESH
        )
        return carry

    lax.fori_loop(1, n_dp, greet, 0)

    rows = iota((own, LANES), 0) + hd * own
    _, visual, _ = row_layout(rows, lens)
    vis_f = visual.astype(F32)
    for c in range(0, tok_ref.shape[1], LANES):
        v = tok_ref[:, c : c + LANES].astype(F32) * vis_f
        hbuf[hd, 0:1, c : c + LANES] = jnp.sum(v, axis=0, keepdims=True)
        hbuf[hd, 1:2, c : c + LANES] = jnp.sum(v * v, axis=0, keepdims=True)
    pl.semaphore_wait(barrier, n_dp + 2)

    def hcopy(i, peer):
        return pltpu.make_async_remote_copy(
            src_ref=hbuf.at[hd],
            dst_ref=hbuf.at[hd],
            send_sem=hsend.at[i],
            recv_sem=hrecv.at[i],
            device_id={"head": peer},
            device_id_type=MESH,
        )

    hcopies = [hcopy(i, peer) for i, peer in enumerate((sib, cross, diag))]
    for copy in hcopies:
        copy.start()

    r_i, l_i = iota((LANES, LANES), 0), iota((LANES, LANES), 1)

    def toeplitz(table, count):
        t_i, j_i = iota((count, LANES), 0), iota((count, LANES), 1)
        low = 63 - count // 2
        pick = (t_i == jnp.clip(j_i - low, 0, count - 1)).astype(BF)
        ext = mm(table.astype(BF), pick)
        return [
            pltpu.roll(jnp.broadcast_to(ext[h : h + 1], (LANES, LANES)), 65, 1, stride=1, stride_axis=0)
            for h in range(heads)
        ]

    pos_t = toeplitz(tp_ref[...], POSB)
    x_t = toeplitz(tb_ref[0], BOXB)
    y_t = toeplitz(tb_ref[1], BOXB)

    def within(low, high):
        return (r_i >= low) & (r_i < high) & (l_i >= low) & (l_i < high)

    seg_part = jnp.where(within(SEG0, LSE0) & (r_i != l_i), -BIG, 0.0)
    for h in range(heads):
        map1[h] = jnp.where(
            within(0, 64), x_t[h], jnp.where(within(64, 96), pos_t[h], seg_part)
        ).astype(BF)
        map0[h] = jnp.where(within(64, 128), y_t[h], 0.0).astype(BF)

    for copy in hcopies:
        copy.wait()
    dbuf[dp] = ((hbuf[0] + hbuf[1]) + hbuf[2]) + hbuf[3]

    def dcopy(j):
        return pltpu.make_async_remote_copy(
            src_ref=dbuf.at[dp],
            dst_ref=dbuf.at[dp],
            send_sem=dsend.at[j],
            recv_sem=drecv.at[j],
            device_id={"dp": lax.rem(dp + j, n_dp)},
            device_id_type=MESH,
        )

    def dstart(j, carry):
        dcopy(j).start()
        return carry

    def dwait(j, carry):
        dcopy(j).wait()
        return carry

    lax.fori_loop(1, n_dp, dstart, 0)

    def features(c, carry):
        at = pl.ds(pl.multiple_of(c * LANES, LANES), LANES)
        seg, _, bucket = row_layout(r_i + c * LANES, lens)
        bx = jnp.broadcast_to(box_ref[0:1, at].astype(F32), (LANES, LANES)).T.astype(I32)
        by = jnp.broadcast_to(box_ref[1:2, at].astype(F32), (LANES, LANES)).T.astype(I32)
        hot = (
            (l_i == bx)
            | (l_i == bucket + 64)
            | (l_i == seg + SEG0)
        )
        key1 = hot.astype(F32)
        k1_ref[at] = jnp.where((l_i >= LSE0) & (l_i < LSE0 + 3), 1.0, key1).astype(BF)
        key1 = key1.astype(BF)
        key0 = (l_i == by + 64).astype(F32).astype(BF)
        for h in range(heads):
            q1_ref[h, at] = mm(key1, map1[h]).astype(BF)
            q0_ref[h, at] = mm(key0, map0[h]).astype(BF)
            k0_ref[h, at] = key0
        return carry

    lax.fori_loop(0, group // LANES, features, 0)
    lax.fori_loop(1, n_dp, dwait, 0)

    def dsum(j, total):
        return total + dbuf[j]

    total = lax.fori_loop(1, n_dp, dsum, dbuf[0])
    count = float(VISUAL * docs) * n_dp
    mean = total[0:1] / count
    inv_std = lax.rsqrt(total[1:2] / count - mean * mean + BATCH_EPS)
    st_ref[0:1] = mean
    st_ref[1:2] = inv_std
    pieces = asend.shape[1]
    piece = own // pieces

    def acopy(source, s, i, peer):
        at = pl.ds(pl.multiple_of(source * own + s * piece, piece), piece)
        return pltpu.make_async_remote_copy(
            src_ref=abuf.at[at],
            dst_ref=abuf.at[at],
            send_sem=asend.at[i, s],
            recv_sem=arecv.at[i, s],
            device_id={"head": peer},
            device_id_type=MESH,
        )

    for s in range(pieces):
        at = pl.ds(s * piece, piece)
        v = tok_ref[at].astype(F32)
        vis = vis_f[s * piece : (s + 1) * piece, 0:1] > 0.5
        x_in = jnp.where(vis, (v - mean) * inv_std * gain_ref[...] + shift_ref[...], v)
        xin_ref[at] = x_in
        abuf[pl.ds(pl.multiple_of(hd * own + s * piece, piece), piece)] = x_in.astype(BF)
        acopy(hd, s, 0, cross).start()
        acopy(hd, s, 1, sib).start()

    lane = iota((piece, LANES), 1)

    def project(source, s):
        at = pl.ds(pl.multiple_of(source * own + s * piece, piece), piece)
        a = abuf[at]
        q = ((mm(a, w_ref[0]) + b_ref[0:1]).astype(BF)).astype(F32) * 0.125
        k = mm(a, w_ref[1])
        v = mm(a, w_ref[2]) + b_ref[1:2]
        for h in range(heads):
            cols = slice(h * DH, (h + 1) * DH)
            zero = jnp.zeros((piece, DH), F32)
            q0_ref[h, at] = jnp.where(
                lane < DH, jnp.concatenate([q[:, cols], zero], axis=1), q0_ref[h, at].astype(F32)
            ).astype(BF)
            k0_ref[h, at] = jnp.where(
                lane < DH, jnp.concatenate([k[:, cols], zero], axis=1), k0_ref[h, at].astype(F32)
            ).astype(BF)
            vx_ref[h, at] = jnp.where(
                lane < DH, jnp.concatenate([v[:, cols], zero], axis=1), 1.0
            ).astype(BF)

    def loop_project(source):
        def step(s, carry):
            project(source, s)
            return carry

        lax.fori_loop(0, pieces, step, 0)

    loop_project(hd)
    for s in range(pieces):
        acopy(sib, s, 1, sib).wait_recv()
    loop_project(sib)
    for s in range(pieces):
        acopy(cross, s, 0, cross).wait_recv()
        acopy(cross, s, 2, sib).start()
        project(cross, s)
    for s in range(pieces):
        acopy(diag, s, 2, sib).wait_recv()
        project(diag, s)
    out = pltpu.make_async_copy(abuf, a_ref, osem)
    out.start()
    for s in range(pieces):
        acopy(hd, s, 0, cross).wait_send()
        acopy(hd, s, 1, sib).wait_send()
        acopy(cross, s, 2, sib).wait_send()
    out.wait()


def entry(tokens, lengths, box_cells, bn_gain, bn_shift, w, b_qv, tab_pos, tab_box, n_dp):
    own, width = tokens.shape
    group = box_cells.shape[1]
    heads = w.shape[2] // DH
    pieces = 4
    tile = jax.ShapeDtypeStruct((heads, group, LANES), BF)
    dma = pltpu.SemaphoreType.DMA
    return pl.pallas_call(
        entry_kernel,
        out_shape=(
            jax.ShapeDtypeStruct((own, width), F32),
            jax.ShapeDtypeStruct((group, width), BF),
            tile,
            tile,
            tile,
            jax.ShapeDtypeStruct((group, LANES), BF),
            tile,
            jax.ShapeDtypeStruct((2, width), F32),
        ),
        in_specs=[SM] + [VM] * 8,
        out_specs=(VM, pl.BlockSpec(memory_space=pl.ANY), VM, VM, VM, VM, VM, VM),
        scratch_shapes=[
            pltpu.VMEM((group, width), BF),
            pltpu.VMEM((4, 8, width), F32),
            pltpu.VMEM((n_dp, 8, width), F32),
            pltpu.VMEM((heads, LANES, LANES), BF),
            pltpu.VMEM((heads, LANES, LANES), BF),
            dma((3,)),
            dma((3,)),
            dma((n_dp,)),
            dma((n_dp,)),
            dma((3, pieces)),
            dma((3, pieces)),
            dma,
        ],
        compiler_params=pltpu.CompilerParams(
            collective_id=0, has_side_effects=True, vmem_limit_bytes=VMEM_CAP
        ),
        name="entry",
    )(
        lengths,
        tokens,
        box_cells,
        bn_gain.reshape(1, width),
        bn_shift.reshape(1, width),
        w,
        b_qv,
        tab_pos,
        tab_box,
    )


def attend_kernel(
    len_ref, q0_ref, q1_ref, k0_ref, k1_ref, vx_ref, o_ref, q1b_ref, s_scr, m_scr, acc
):
    heads, group = q0_ref.shape[0], q0_ref.shape[1]
    lens = [len_ref[0, d] for d in range(len_ref.shape[1])]
    lane = iota((BLK, LANES), 1)

    def block(qb, carry):
        low, high = block_window(qb, lens, group)
        at = pl.ds(pl.multiple_of(qb * BLK, BLK), BLK)
        m_scr[...] = jnp.full_like(m_scr, -2.0 * BIG)
        acc[...] = jnp.zeros_like(acc)

        def score(kb, c):
            ks = pl.ds(pl.multiple_of(kb * BLK, BLK), BLK)
            for h in range(heads):
                qa = jnp.concatenate([q0_ref[h, at], q1_ref[h, at]], axis=1)
                ka = jnp.concatenate([k0_ref[h, ks], k1_ref[ks]], axis=1)
                s = mm_nt(qa, ka)
                s_scr[h, kb] = s
                m_scr[h] = jnp.maximum(m_scr[h], jnp.maximum(s[:, :LANES], s[:, LANES:]))
            return c

        lax.fori_loop(low, high, score, 0)
        for h in range(heads):
            m_scr[h] = jnp.broadcast_to(
                jnp.max(m_scr[h], axis=1, keepdims=True), (BLK, LANES)
            )

        def weigh(kb, c):
            ks = pl.ds(pl.multiple_of(kb * BLK, BLK), BLK)
            for h in range(heads):
                m = m_scr[h]
                p = jnp.exp(s_scr[h, kb] - jnp.concatenate([m, m], axis=1)).astype(BF)
                acc[h] += mm(p, vx_ref[h, ks])
            return c

        lax.fori_loop(low, high, weigh, 0)
        for h in range(heads):
            a = acc[h]
            turned = pltpu.roll(a, DH, 1)
            o_ref[at, h * DH : (h + 1) * DH] = (a / turned)[:, :DH].astype(BF)
            total = jnp.where(lane < DH, turned, a)
            rest = -(m_scr[h] + jnp.log(total))
            tile = q1_ref[h, at].astype(F32)
            for i in range(3):
                part = rest.astype(BF).astype(F32)
                tile = jnp.where(lane == LSE0 + i, part, tile)
                rest = rest - part
            q1b_ref[h, at] = tile.astype(BF)
        return carry

    lax.fori_loop(0, group // BLK, block, 0)


def attend(lengths, q0, q1, k0, k1, vx):
    heads, group, _ = q0.shape
    return pl.pallas_call(
        attend_kernel,
        out_shape=(
            jax.ShapeDtypeStruct((group, heads * DH), BF),
            jax.ShapeDtypeStruct(q1.shape, BF),
        ),
        in_specs=[SM] + [VM] * 5,
        out_specs=(VM, VM),
        scratch_shapes=[
            pltpu.VMEM((heads, group // BLK, BLK, BLK), F32),
            pltpu.VMEM((heads, BLK, LANES), F32),
            pltpu.VMEM((heads, BLK, LANES), F32),
        ],
        compiler_params=pltpu.CompilerParams(vmem_limit_bytes=VMEM_CAP),
        name="attend",
    )(lengths, q0, q1, k0, k1, vx)


def attend_back_kernel(
    len_ref,
    q0_ref,
    q1_ref,
    k0_ref,
    k1_ref,
    vx_ref,
    o_ref,
    go_ref,
    dq_ref,
    dk_ref,
    dv_ref,
    gp_ref,
    gb_ref,
    dox,
    kacc,
    vacc,
    qacc,
    map0,
    map1,
):
    heads, group = q0_ref.shape[0], q0_ref.shape[1]
    width = heads * DH
    lens = [len_ref[0, d] for d in range(len_ref.shape[1])]
    lane = iota((BLK, LANES), 1)
    spread = (
        iota((width, heads * LANES), 0) // DH == iota((width, heads * LANES), 1) // LANES
    ).astype(F32).astype(BF)
    map0[...] = jnp.zeros_like(map0)
    map1[...] = jnp.zeros_like(map1)
    kacc[...] = jnp.zeros_like(kacc)
    vacc[...] = jnp.zeros_like(vacc)

    def prepare(qb, carry):
        at = pl.ds(pl.multiple_of(qb * BLK, BLK), BLK)
        g = go_ref[at].astype(F32)
        e = g * o_ref[at].astype(F32)
        e_high = e.astype(BF)
        e_low = (e - e_high.astype(F32)).astype(BF)
        dots = mm(e_high, spread) + mm(e_low, spread)
        for h in range(heads):
            rest = -dots[:, h * LANES : (h + 1) * LANES]
            tile = jnp.where(
                lane < DH,
                jnp.concatenate([g[:, h * DH : (h + 1) * DH], jnp.zeros((BLK, DH), F32)], axis=1),
                0.0,
            )
            for i in range(3):
                part = rest.astype(BF).astype(F32)
                tile = jnp.where(lane == DH + i, part, tile)
                rest = rest - part
            dox[h, at] = tile.astype(BF)
        return carry

    lax.fori_loop(0, group // BLK, prepare, 0)

    def block(qb, carry):
        low, high = block_window(qb, lens, group)
        at = pl.ds(pl.multiple_of(qb * BLK, BLK), BLK)
        qacc[...] = jnp.zeros_like(qacc)

        def pair(kb, c):
            ks = pl.ds(pl.multiple_of(kb * BLK, BLK), BLK)
            for h in range(heads):
                q0 = q0_ref[h, at]
                qa = jnp.concatenate([q0, q1_ref[h, at]], axis=1)
                ka = jnp.concatenate([k0_ref[h, ks], k1_ref[ks]], axis=1)
                g = dox[h, at]
                p = jnp.exp(mm_nt(ka, qa))
                ds = (p * mm_nt(vx_ref[h, ks], g)).astype(BF)
                vacc[h, ks] += mm(p.astype(BF), g)
                kacc[h, ks] += mm(ds, q0)
                qacc[h] += mm_tn(ds, ka)
            return c

        lax.fori_loop(low, high, pair, 0)
        for h in range(heads):
            a = qacc[h]
            dq_ref[at, h * DH : (h + 1) * DH] = (a[:, :DH] * 0.125).astype(BF)
            high_part = a.astype(BF)
            low_part = (a - high_part.astype(F32)).astype(BF)
            for m, hot, cols in (
                (map0, k0_ref[h, at], slice(0, LANES)),
                (map1, k1_ref[at], slice(LANES, 2 * LANES)),
            ):
                both = jnp.concatenate([high_part[:, cols], low_part[:, cols]], axis=1)
                m[h] += mm_tn(hot, both)
        return carry

    lax.fori_loop(0, group // BLK, block, 0)

    def finish(kb, carry):
        at = pl.ds(pl.multiple_of(kb * BLK, BLK), BLK)
        for h in range(heads):
            cols = slice(h * DH, (h + 1) * DH)
            dk_ref[at, cols] = kacc[h, at][:, :DH].astype(BF)
            dv_ref[at, cols] = vacc[h, at][:, :DH].astype(BF)
        return carry

    lax.fori_loop(0, group // BLK, finish, 0)

    r_i, l_i = iota((LANES, LANES), 0), iota((LANES, LANES), 1)

    def exact(a, b):
        return jnp.dot(a, b, precision=lax.Precision.HIGHEST, preferred_element_type=F32)

    def diagonals(block, base, count):
        inside = (r_i >= base) & (r_i < base + count) & (l_i >= base) & (l_i < base + count)
        flip = ((l_i == base + count - 1 - r_i) & (r_i < count)).astype(F32)
        turned = exact(flip, jnp.where(inside, block, 0.0))
        moved = pltpu.roll(turned, 64 - base - count + LANES, 1, stride=1, stride_axis=0)
        return jnp.sum(moved, axis=0, keepdims=True)

    def fold(block, base, count):
        sums = jnp.broadcast_to(diagonals(block, base, count), (8, LANES))
        j_i, t_i = iota((LANES, count), 0), iota((LANES, count), 1)
        low = 63 - count // 2
        pick = (t_i == jnp.clip(j_i - low, 0, count - 1)).astype(F32)
        return exact(sums, pick)[0:1]

    for h in range(heads):
        one = map1[h][:, :LANES] + map1[h][:, LANES:]
        zero = map0[h][:, :LANES] + map0[h][:, LANES:]
        gb_ref[0, h : h + 1] = fold(one, 0, BOXB)
        gp_ref[h : h + 1] = fold(one, 64, POSB)
        gb_ref[1, h : h + 1] = fold(zero, 64, BOXB)


def attend_back(lengths, q0, q1, k0, k1, vx, out, grad_out):
    heads, group, _ = q0.shape
    flat = jax.ShapeDtypeStruct((group, heads * DH), BF)
    return pl.pallas_call(
        attend_back_kernel,
        out_shape=(
            flat,
            flat,
            flat,
            jax.ShapeDtypeStruct((heads, POSB), F32),
            jax.ShapeDtypeStruct((2, heads, BOXB), F32),
        ),
        in_specs=[SM] + [VM] * 7,
        out_specs=(VM,) * 5,
        scratch_shapes=[
            pltpu.VMEM((heads, group, LANES), BF),
            pltpu.VMEM((heads, group, LANES), F32),
            pltpu.VMEM((heads, group, LANES), F32),
            pltpu.VMEM((heads, BLK, 2 * LANES), F32),
            pltpu.VMEM((heads, LANES, 2 * LANES), F32),
            pltpu.VMEM((heads, LANES, 2 * LANES), F32),
        ],
        compiler_params=pltpu.CompilerParams(vmem_limit_bytes=VMEM_CAP),
        name="attend_back",
    )(lengths, q0, q1, k0, k1, vx, out, grad_out)


def norm_rows(h, gain_vec, shift_vec):
    row_mean = jnp.mean(h, axis=-1, keepdims=True)
    centred = h - row_mean
    variance = jnp.mean(centred * centred, axis=-1, keepdims=True)
    return centred * lax.rsqrt(variance + NORM_EPS) * gain_vec + shift_vec


def exact_gelu(pre_val):
    return jax.nn.gelu(pre_val, approximate=False)


def scatter_rows(partial):
    return lax.psum_scatter(
        partial.astype(BF), "head", scatter_dimension=0, tiled=True
    ).astype(F32)


def body(
    n_dp,
    tokens,
    lengths,
    box_cells,
    bn_gain,
    bn_shift,
    query_key_value_weight,
    b_qv,
    tab_pos,
    tab_box,
    w_out,
    b_out,
    ln1_gain,
    ln1_shift,
    w_up,
    b_up,
    w_down,
    b_down,
    ln2_gain,
    ln2_shift,
    cotangent,
):
    own_rows = tokens.shape[0]
    group_rows = box_cells.shape[1]
    x_in, attention_input, q0, q1, k0, k1, vx, stats = entry(
        tokens, lengths, box_cells, bn_gain, bn_shift, query_key_value_weight, b_qv, tab_pos, tab_box, n_dp
    )
    attn_low, q1b = attend(lengths, q0, q1, k0, k1, vx)
    attn_proj = scatter_rows(mm(attn_low, w_out)) + b_out
    mid_norm, norm_one_back = jax.vjp(norm_rows, x_in + attn_proj, ln1_gain, ln1_shift)
    ffn_in = lax.all_gather(mid_norm.astype(BF), "head", axis=0, tiled=True)
    pre_act = mm(ffn_in, w_up) + b_up
    gelu_out, gelu_back = jax.vjp(exact_gelu, pre_act)
    gelu_low = gelu_out.astype(BF)
    ffn_proj = scatter_rows(mm(gelu_low, w_down)) + b_down
    output, norm_two_back = jax.vjp(norm_rows, mid_norm + ffn_proj, ln2_gain, ln2_shift)
    grad_two, grad_gain_two, grad_shift_two = norm_two_back(cotangent.astype(F32))
    ffn_grad = lax.all_gather(grad_two.astype(BF), "head", axis=0, tiled=True)
    grad_gelu = mm_nt(ffn_grad, w_down)
    grad_pre = gelu_back(grad_gelu)[0].astype(BF)
    grad_w_down = mm_tn(gelu_low, ffn_grad)
    grad_w_up = mm_tn(ffn_in, grad_pre)
    grad_b_up = jnp.sum(grad_pre.astype(F32), axis=0)
    grad_mid = grad_two + scatter_rows(mm_nt(grad_pre, w_up))
    grad_one, grad_gain_one, grad_shift_one = norm_one_back(grad_mid)
    attn_grad = lax.all_gather(grad_one.astype(BF), "head", axis=0, tiled=True)
    grad_w_out = mm_tn(attn_low, attn_grad)
    grad_heads = mm_nt(attn_grad, w_out).astype(BF)
    dq, dk, dv, grad_tab_pos, grad_tab_box = attend_back(
        lengths, q0, q1b, k0, k1, vx, attn_low, grad_heads
    )
    grads = jnp.stack([dq, dk, dv], axis=1)
    projection_weight_gradient = jnp.einsum(
        "pj,peq->ejq", attention_input, grads, preferred_element_type=F32
    )
    grad_b_qv = jnp.stack(
        [jnp.sum(dq.astype(F32), axis=0), jnp.sum(dv.astype(F32), axis=0)]
    )
    grad_in = grad_one + scatter_rows(
        jnp.einsum("ajm,jwm->aw", grads, query_key_value_weight, preferred_element_type=F32)
    )
    segment, visual, bucket = row_layout(
        jnp.arange(group_rows, dtype=I32), [lengths[0, d] for d in range(lengths.shape[1])]
    )
    first_own = lax.axis_index("head") * own_rows
    vis_own = lax.dynamic_slice_in_dim(visual, first_own, own_rows, 0)[:, None]
    x_hat = (tokens.astype(F32) - stats[0]) * stats[1]
    vis_count = VISUAL * lengths.shape[1] * n_dp
    vis_grad = jnp.where(vis_own, grad_in, 0.0)
    small_sums = lax.psum(
        (
            jnp.sum(vis_grad, axis=0),
            jnp.sum(vis_grad * x_hat, axis=0),
            grad_gain_one,
            grad_shift_one,
            grad_gain_two,
            grad_shift_two,
            jnp.sum(grad_one, axis=0),
            jnp.sum(grad_two, axis=0),
        ),
        ("dp", "head"),
    )
    grad_bn_shift = small_sums[0]
    grad_bn_gain = small_sums[1]
    batch_term = bn_gain * (grad_bn_shift + x_hat * grad_bn_gain) / vis_count
    grad_tokens = jnp.where(vis_own, stats[1] * (grad_in * bn_gain - batch_term), grad_in)
    small = lax.psum((grad_b_qv, grad_tab_pos, grad_tab_box, grad_b_up), "dp")
    weights = lax.psum(
        (
            projection_weight_gradient.astype(BF),
            grad_w_out.astype(BF),
            grad_w_up.astype(BF),
            grad_w_down.astype(BF),
        ),
        "dp",
    )
    return (
        output.astype(BF),
        grad_tokens,
        grad_bn_gain,
        grad_bn_shift,
        weights[0].astype(F32),
        small[0],
        small[1],
        small[2],
        weights[1].astype(F32),
        small_sums[6],
        small_sums[2],
        small_sums[3],
        weights[2].astype(F32),
        small[3],
        weights[3].astype(F32),
        small_sums[7],
        small_sums[4],
        small_sums[5],
    )


def solution(mesh):
    rows = P(("dp", "head"), None)
    in_specs = (
        rows,
        P("dp", None),
        P(None, "dp"),
        P(),
        P(),
        P(None, None, "head"),
        P(None, "head"),
        P("head", None),
        P(None, "head", None),
        P("head", None),
        P(),
        P(),
        P(),
        P(None, "head"),
        P("head"),
        P("head", None),
        P(),
        P(),
        P(),
        rows,
    )
    out_specs = (
        rows,
        rows,
        P(),
        P(),
        P(None, None, "head"),
        P(None, "head"),
        P("head", None),
        P(None, "head", None),
        P("head", None),
        P(),
        P(),
        P(),
        P(None, "head"),
        P("head"),
        P("head", None),
        P(),
        P(),
        P(),
    )
    return jax.shard_map(
        functools.partial(body, mesh.shape["dp"]),
        mesh=mesh,
        in_specs=in_specs,
        out_specs=out_specs,
        check_vma=False,
    )
```

```python
import functools

import jax
import jax.numpy as jnp
from jax import lax
from jax.experimental import pallas as pl
from jax.experimental.pallas import tpu as pltpu
from jax.sharding import PartitionSpec as P

DH = 64
VISUAL = 49
POSB = 32
BOXB = 64
POS_STEP = 16
NORM_EPS = 1e-05
BATCH_EPS = 1e-05
BIG = float(2.0**100)
BLK = 256
LANES = 128
SEG0 = 96
LSE0 = 112
VMEM_CAP = 58 << 20

MESH = pl.DeviceIdType.MESH
BF = jnp.bfloat16
F32 = jnp.float32
I32 = jnp.int32
VM = pl.BlockSpec(memory_space=pltpu.VMEM)
SM = pl.BlockSpec(memory_space=pltpu.SMEM)


def iota(shape, dim):
    return lax.broadcasted_iota(I32, shape, dim)


def mm(a, b):
    return jnp.dot(a, b, preferred_element_type=F32)


def mm_nt(a, b):
    return lax.dot_general(a, b, (((1,), (1,)), ((), ())), preferred_element_type=F32)


def mm_tn(a, b):
    return lax.dot_general(a, b, (((0,), (0,)), ((), ())), preferred_element_type=F32)


def head_peers():
    hd = lax.axis_index("head")
    sib = hd + 1 - 2 * lax.rem(hd, 2)
    cross = lax.rem(hd + 2, 4)
    diag = lax.rem(sib + 2, 4)
    return hd, sib, cross, diag


def row_layout(rows, lens):
    seg = jnp.zeros_like(rows)
    first = jnp.zeros_like(rows)
    end = 0
    for size in lens:
        end = end + size + VISUAL
        past = rows >= end
        seg = seg + past.astype(I32)
        first = jnp.where(past, end, first)
    offset = rows - first
    visual = jnp.logical_and(seg < len(lens), offset < VISUAL)
    position = jnp.where(visual, offset, offset - VISUAL)
    bucket = jnp.minimum(lax.shift_right_logical(jnp.maximum(position, 0), 4), POSB - 1)
    return seg, visual, bucket


def block_window(block, lens, group_rows):
    first, last = block * BLK, block * BLK + BLK - 1
    low, high, end = 0, group_rows, 0
    ends = []
    for size in lens:
        end = end + size + VISUAL
        ends.append(end)
        low = jnp.where(first >= end, end, low)
    for end in reversed(ends):
        high = jnp.where(last < end, end, high)
    return low // BLK, (high + BLK - 1) // BLK


def entry_kernel(
    len_ref,
    tok_ref,
    box_ref,
    gain_ref,
    shift_ref,
    w_ref,
    b_ref,
    tp_ref,
    tb_ref,
    wo_ref,
    xin_ref,
    a_ref,
    q0_ref,
    q1_ref,
    k0_ref,
    k1_ref,
    vx_ref,
    st_ref,
    wof_ref,
    abuf,
    hbuf,
    dbuf,
    map0,
    map1,
    hsend,
    hrecv,
    dsend,
    drecv,
    asend,
    arecv,
    wsend,
    wrecv,
    osem,
):
    n_dp = dbuf.shape[0]
    own = tok_ref.shape[0]
    group = abuf.shape[0]
    docs = len_ref.shape[1]
    heads = w_ref.shape[2] // DH
    hd, sib, cross, diag = head_peers()
    dp = lax.axis_index("dp")
    lens = [len_ref[0, d] for d in range(docs)]

    barrier = pltpu.get_barrier_semaphore()
    for peer in (sib, cross, diag):
        pl.semaphore_signal(barrier, inc=1, device_id={"head": peer}, device_id_type=MESH)

    def greet(j, carry):
        pl.semaphore_signal(
            barrier, inc=1, device_id={"dp": lax.rem(dp + j, n_dp)}, device_id_type=MESH
        )
        return carry

    lax.fori_loop(1, n_dp, greet, 0)

    rows = iota((own, LANES), 0) + hd * own
    _, visual, _ = row_layout(rows, lens)
    vis_f = visual.astype(F32)
    for c in range(0, tok_ref.shape[1], LANES):
        v = tok_ref[:, c : c + LANES].astype(F32) * vis_f
        hbuf[hd, 0:1, c : c + LANES] = jnp.sum(v, axis=0, keepdims=True)
        hbuf[hd, 1:2, c : c + LANES] = jnp.sum(v * v, axis=0, keepdims=True)
    pl.semaphore_wait(barrier, n_dp + 2)

    def hcopy(i, peer):
        return pltpu.make_async_remote_copy(
            src_ref=hbuf.at[hd],
            dst_ref=hbuf.at[hd],
            send_sem=hsend.at[i],
            recv_sem=hrecv.at[i],
            device_id={"head": peer},
            device_id_type=MESH,
        )

    hcopies = [hcopy(i, peer) for i, peer in enumerate((sib, cross, diag))]
    for copy in hcopies:
        copy.start()

    part = wo_ref.shape[0]

    def wcopy(source, i, peer):
        at = pl.ds(pl.multiple_of(source * part, DH), part)
        return pltpu.make_async_remote_copy(
            src_ref=wof_ref.at[at],
            dst_ref=wof_ref.at[at],
            send_sem=wsend.at[i],
            recv_sem=wrecv.at[i],
            device_id={"head": peer},
            device_id_type=MESH,
        )

    wof_ref[pl.ds(pl.multiple_of(hd * part, DH), part)] = wo_ref[...]
    wcopy(hd, 0, cross).start()
    wcopy(hd, 1, sib).start()

    r_i, l_i = iota((LANES, LANES), 0), iota((LANES, LANES), 1)

    def toeplitz(table, count):
        t_i, j_i = iota((count, LANES), 0), iota((count, LANES), 1)
        low = 63 - count // 2
        pick = (t_i == jnp.clip(j_i - low, 0, count - 1)).astype(BF)
        ext = mm(table.astype(BF), pick)
        return [
            pltpu.roll(jnp.broadcast_to(ext[h : h + 1], (LANES, LANES)), 65, 1, stride=1, stride_axis=0)
            for h in range(heads)
        ]

    pos_t = toeplitz(tp_ref[...], POSB)
    x_t = toeplitz(tb_ref[0], BOXB)
    y_t = toeplitz(tb_ref[1], BOXB)

    def within(low, high):
        return (r_i >= low) & (r_i < high) & (l_i >= low) & (l_i < high)

    seg_part = jnp.where(within(SEG0, LSE0) & (r_i != l_i), -BIG, 0.0)
    for h in range(heads):
        map1[h] = jnp.where(
            within(0, 64), x_t[h], jnp.where(within(64, 96), pos_t[h], seg_part)
        ).astype(BF)
        map0[h] = jnp.where(within(64, 128), y_t[h], 0.0).astype(BF)

    for copy in hcopies:
        copy.wait()
    dbuf[dp] = ((hbuf[0] + hbuf[1]) + hbuf[2]) + hbuf[3]

    def dcopy(j):
        return pltpu.make_async_remote_copy(
            src_ref=dbuf.at[dp],
            dst_ref=dbuf.at[dp],
            send_sem=dsend.at[j],
            recv_sem=drecv.at[j],
            device_id={"dp": lax.rem(dp + j, n_dp)},
            device_id_type=MESH,
        )

    def dstart(j, carry):
        dcopy(j).start()
        return carry

    def dwait(j, carry):
        dcopy(j).wait()
        return carry

    lax.fori_loop(1, n_dp, dstart, 0)

    def features(c, carry):
        at = pl.ds(pl.multiple_of(c * LANES, LANES), LANES)
        seg, _, bucket = row_layout(r_i + c * LANES, lens)
        bx = jnp.broadcast_to(box_ref[0:1, at].astype(F32), (LANES, LANES)).T.astype(I32)
        by = jnp.broadcast_to(box_ref[1:2, at].astype(F32), (LANES, LANES)).T.astype(I32)
        hot = (
            (l_i == bx)
            | (l_i == bucket + 64)
            | (l_i == seg + SEG0)
        )
        key1 = hot.astype(F32)
        k1_ref[at] = jnp.where((l_i >= LSE0) & (l_i < LSE0 + 3), 1.0, key1).astype(BF)
        key1 = key1.astype(BF)
        key0 = (l_i == by + 64).astype(F32).astype(BF)
        for h in range(heads):
            q1_ref[h, at] = mm(key1, map1[h]).astype(BF)
            q0_ref[h, at] = mm(key0, map0[h]).astype(BF)
            k0_ref[h, at] = key0
        return carry

    lax.fori_loop(0, group // LANES, features, 0)
    lax.fori_loop(1, n_dp, dwait, 0)

    def dsum(j, total):
        return total + dbuf[j]

    total = lax.fori_loop(1, n_dp, dsum, dbuf[0])
    count = float(VISUAL * docs) * n_dp
    mean = total[0:1] / count
    inv_std = lax.rsqrt(total[1:2] / count - mean * mean + BATCH_EPS)
    st_ref[0:1] = mean
    st_ref[1:2] = inv_std
    pieces = asend.shape[1]
    piece = own // pieces

    def acopy(source, s, i, peer):
        at = pl.ds(pl.multiple_of(source * own + s * piece, piece), piece)
        return pltpu.make_async_remote_copy(
            src_ref=abuf.at[at],
            dst_ref=abuf.at[at],
            send_sem=asend.at[i, s],
            recv_sem=arecv.at[i, s],
            device_id={"head": peer},
            device_id_type=MESH,
        )

    for s in range(pieces):
        at = pl.ds(s * piece, piece)
        v = tok_ref[at].astype(F32)
        vis = vis_f[s * piece : (s + 1) * piece, 0:1] > 0.5
        x_in = jnp.where(vis, (v - mean) * inv_std * gain_ref[...] + shift_ref[...], v)
        xin_ref[at] = x_in
        abuf[pl.ds(pl.multiple_of(hd * own + s * piece, piece), piece)] = x_in.astype(BF)
        acopy(hd, s, 0, cross).start()
        acopy(hd, s, 1, sib).start()

    lane = iota((piece, LANES), 1)

    def project(source, s):
        at = pl.ds(pl.multiple_of(source * own + s * piece, piece), piece)
        a = abuf[at]
        q = ((mm(a, w_ref[0]) + b_ref[0:1]).astype(BF)).astype(F32) * 0.125
        k = mm(a, w_ref[1])
        v = mm(a, w_ref[2]) + b_ref[1:2]
        for h in range(heads):
            cols = slice(h * DH, (h + 1) * DH)
            zero = jnp.zeros((piece, DH), F32)
            q0_ref[h, at] = jnp.where(
                lane < DH, jnp.concatenate([q[:, cols], zero], axis=1), q0_ref[h, at].astype(F32)
            ).astype(BF)
            k0_ref[h, at] = jnp.where(
                lane < DH, jnp.concatenate([k[:, cols], zero], axis=1), k0_ref[h, at].astype(F32)
            ).astype(BF)
            vx_ref[h, at] = jnp.where(
                lane < DH, jnp.concatenate([v[:, cols], zero], axis=1), 1.0
            ).astype(BF)

    def loop_project(source):
        def step(s, carry):
            project(source, s)
            return carry

        lax.fori_loop(0, pieces, step, 0)

    loop_project(hd)
    wcopy(cross, 0, cross).wait_recv()
    wcopy(cross, 2, sib).start()
    for s in range(pieces):
        acopy(sib, s, 1, sib).wait_recv()
    loop_project(sib)
    for s in range(pieces):
        acopy(cross, s, 0, cross).wait_recv()
        acopy(cross, s, 2, sib).start()
        project(cross, s)
    for s in range(pieces):
        acopy(diag, s, 2, sib).wait_recv()
        project(diag, s)
    out = pltpu.make_async_copy(abuf, a_ref, osem)
    out.start()
    wcopy(sib, 1, sib).wait_recv()
    wcopy(diag, 2, sib).wait_recv()
    wcopy(hd, 0, cross).wait_send()
    wcopy(hd, 1, sib).wait_send()
    wcopy(cross, 2, sib).wait_send()
    for s in range(pieces):
        acopy(hd, s, 0, cross).wait_send()
        acopy(hd, s, 1, sib).wait_send()
        acopy(cross, s, 2, sib).wait_send()
    out.wait()


def entry(tokens, lengths, box_cells, bn_gain, bn_shift, w, b_qv, tab_pos, tab_box, w_out, n_dp):
    own, width = tokens.shape
    group = box_cells.shape[1]
    heads = w.shape[2] // DH
    pieces = 4
    tile = jax.ShapeDtypeStruct((heads, group, LANES), BF)
    dma = pltpu.SemaphoreType.DMA
    return pl.pallas_call(
        entry_kernel,
        out_shape=(
            jax.ShapeDtypeStruct((own, width), F32),
            jax.ShapeDtypeStruct((group, width), BF),
            tile,
            tile,
            tile,
            jax.ShapeDtypeStruct((group, LANES), BF),
            tile,
            jax.ShapeDtypeStruct((2, width), F32),
            jax.ShapeDtypeStruct((4 * w_out.shape[0], w_out.shape[1]), BF),
        ),
        in_specs=[SM] + [VM] * 9,
        out_specs=(VM, pl.BlockSpec(memory_space=pl.ANY), VM, VM, VM, VM, VM, VM, VM),
        scratch_shapes=[
            pltpu.VMEM((group, width), BF),
            pltpu.VMEM((4, 8, width), F32),
            pltpu.VMEM((n_dp, 8, width), F32),
            pltpu.VMEM((heads, LANES, LANES), BF),
            pltpu.VMEM((heads, LANES, LANES), BF),
            dma((3,)),
            dma((3,)),
            dma((n_dp,)),
            dma((n_dp,)),
            dma((3, pieces)),
            dma((3, pieces)),
            dma((3,)),
            dma((3,)),
            dma,
        ],
        compiler_params=pltpu.CompilerParams(
            collective_id=0, has_side_effects=True, vmem_limit_bytes=VMEM_CAP
        ),
        name="entry",
    )(
        lengths,
        tokens,
        box_cells,
        bn_gain.reshape(1, width),
        bn_shift.reshape(1, width),
        w,
        b_qv,
        tab_pos,
        tab_box,
        w_out,
    )


def attend_kernel(
    len_ref, q0_ref, q1_ref, k0_ref, k1_ref, vx_ref, o_ref, q1b_ref, s_scr, m_scr, acc
):
    heads, group = q0_ref.shape[0], q0_ref.shape[1]
    lens = [len_ref[0, d] for d in range(len_ref.shape[1])]
    lane = iota((BLK, LANES), 1)

    def block(qb, carry):
        low, high = block_window(qb, lens, group)
        at = pl.ds(pl.multiple_of(qb * BLK, BLK), BLK)
        m_scr[...] = jnp.full_like(m_scr, -2.0 * BIG)
        acc[...] = jnp.zeros_like(acc)

        def score(kb, c):
            ks = pl.ds(pl.multiple_of(kb * BLK, BLK), BLK)
            for h in range(heads):
                qa = jnp.concatenate([q0_ref[h, at], q1_ref[h, at]], axis=1)
                ka = jnp.concatenate([k0_ref[h, ks], k1_ref[ks]], axis=1)
                s = mm_nt(qa, ka)
                s_scr[h, kb] = s
                m_scr[h] = jnp.maximum(m_scr[h], jnp.maximum(s[:, :LANES], s[:, LANES:]))
            return c

        lax.fori_loop(low, high, score, 0)
        for h in range(heads):
            m_scr[h] = jnp.broadcast_to(
                jnp.max(m_scr[h], axis=1, keepdims=True), (BLK, LANES)
            )

        def weigh(kb, c):
            ks = pl.ds(pl.multiple_of(kb * BLK, BLK), BLK)
            for h in range(heads):
                m = m_scr[h]
                p = jnp.exp(s_scr[h, kb] - jnp.concatenate([m, m], axis=1)).astype(BF)
                acc[h] += mm(p, vx_ref[h, ks])
            return c

        lax.fori_loop(low, high, weigh, 0)
        for h in range(heads):
            a = acc[h]
            turned = pltpu.roll(a, DH, 1)
            o_ref[at, h * DH : (h + 1) * DH] = (a / turned)[:, :DH].astype(BF)
            total = jnp.where(lane < DH, turned, a)
            rest = -(m_scr[h] + jnp.log(total))
            tile = q1_ref[h, at].astype(F32)
            for i in range(3):
                part = rest.astype(BF).astype(F32)
                tile = jnp.where(lane == LSE0 + i, part, tile)
                rest = rest - part
            q1b_ref[h, at] = tile.astype(BF)
        return carry

    lax.fori_loop(0, group // BLK, block, 0)


def attend(lengths, q0, q1, k0, k1, vx):
    heads, group, _ = q0.shape
    return pl.pallas_call(
        attend_kernel,
        out_shape=(
            jax.ShapeDtypeStruct((group, heads * DH), BF),
            jax.ShapeDtypeStruct(q1.shape, BF),
        ),
        in_specs=[SM] + [VM] * 5,
        out_specs=(VM, VM),
        scratch_shapes=[
            pltpu.VMEM((heads, group // BLK, BLK, BLK), F32),
            pltpu.VMEM((heads, BLK, LANES), F32),
            pltpu.VMEM((heads, BLK, LANES), F32),
        ],
        compiler_params=pltpu.CompilerParams(vmem_limit_bytes=VMEM_CAP),
        name="attend",
    )(lengths, q0, q1, k0, k1, vx)


C_TAIL = 0.23
TAIL = (
    -2.7761570891016163e-05,
    0.09237844496965408,
    0.08576294034719467,
    0.1195140853524208,
    -0.032920535653829575,
    0.30147361755371094,
    -0.2781279683113098,
    0.2904147207736969,
    -0.07846760004758835,
)


def gelu_pair(v):
    a = jnp.abs(v)
    t = 1.0 / (1.0 + C_TAIL * a)
    g = jnp.full_like(v, TAIL[-1])
    for c in TAIL[-2::-1]:
        g = g * t + c
    e = jnp.exp(v * v * -0.5)
    tail = g * e
    phi = jnp.where(v > 0.0, 1.0 - tail, tail)
    return v * phi, phi + v * (e * 0.3989422804014327)


def row(ref):
    return ref[...].reshape(1, ref.shape[0])


def row_stats(h):
    scale = 1.0 / h.shape[1]
    centred = h - jnp.sum(h, axis=1, keepdims=True) * scale
    rstd = lax.rsqrt(jnp.sum(centred * centred, axis=1, keepdims=True) * scale + NORM_EPS)
    return centred * rstd, rstd


def norm_back(grad, normed, rstd):
    scale = 1.0 / grad.shape[1]
    mean = jnp.sum(grad, axis=1, keepdims=True) * scale
    along = jnp.sum(grad * normed, axis=1, keepdims=True) * scale
    return rstd * (grad - mean - normed * along)


def add_row(ref, i, v):
    ref[i : i + 1] += jnp.sum(v, axis=0, keepdims=True)


def outer_sum(out_ref, a_ref, b_ref, rows):
    def step(m, c):
        cols = pl.ds(pl.multiple_of(m * BLK, BLK), BLK)
        out_ref[cols] = mm_tn(a_ref[0:rows, cols], b_ref[0:rows])
        return c

    lax.fori_loop(0, out_ref.shape[0] // BLK, step, 0)


class Exchange:
    def __init__(self, own, piece):
        self.own, self.piece, self.pieces = own, piece, own // piece
        self.hd, self.sib, self.cross, self.diag = head_peers()

    def rows(self, source, s, base=0):
        return pl.ds(pl.multiple_of(source * self.own + s * self.piece, self.piece), self.piece)

    def send(self, src, dst, sems, i, s, peer):
        return pltpu.make_async_remote_copy(
            src_ref=src,
            dst_ref=dst,
            send_sem=sems.at[0, i, s],
            recv_sem=sems.at[1, i, s],
            device_id={"head": peer},
            device_id_type=MESH,
        )

    def gather(self, buf, sems, i, s):
        source = self.cross if i == 2 else self.hd
        at = self.rows(source, s)
        return self.send(buf.at[at], buf.at[at], sems, i, s, self.cross if i == 0 else self.sib)

    def gather_from(self, buf, sems, i, s):
        source = (self.cross, self.sib, self.diag)[i]
        at = self.rows(source, s)
        return self.send(buf.at[at], buf.at[at], sems, i, s, self.cross if i == 0 else self.sib)

    def partial(self, snd, rcv, sems, i, s):
        return self.send(
            snd.at[i, s], rcv.at[i, s], sems, i, s, self.cross if i == 2 else self.sib
        )


def barrier_head(peers):
    barrier = pltpu.get_barrier_semaphore()
    for peer in peers:
        pl.semaphore_signal(barrier, inc=1, device_id={"head": peer}, device_id_type=MESH)
    pl.semaphore_wait(barrier, len(peers))


def middle_kernel(
    attn_ref,
    xin_ref,
    cot_ref,
    wo_ref,
    wu_ref,
    wd_ref,
    bo_ref,
    g1_ref,
    s1_ref,
    bu_ref,
    bd_ref,
    g2_ref,
    s2_ref,
    out_ref,
    gone_ref,
    ga_ref,
    gwo_ref,
    gwu_ref,
    gwd_ref,
    sums_ref,
    gbu_ref,
    abuf,
    full,
    fin,
    gl,
    gd,
    fgr,
    gpre,
    xh1,
    rs1,
    two,
    ownp,
    crossp,
    snd1,
    rcv1,
    snd2,
    rcv2,
    asems,
    f1sems,
    r1sems,
    f2sems,
    r2sems,
    gsems,
):
    own, width = xin_ref.shape
    hcols = attn_ref.shape[1]
    piece = own // asems.shape[2]
    ex = Exchange(own, piece)
    hd, sib, cross, diag = ex.hd, ex.sib, ex.cross, ex.diag
    peers = (cross, diag, sib)
    barrier_head(peers)

    def own_at(s):
        return pl.ds(pl.multiple_of(s * piece, piece), piece)

    def acopy(s, i):
        at = ex.rows(peers[i], s)
        return ex.send(attn_ref.at[at], abuf.at[hd, own_at(s)], asems, i, s, peers[i])

    def afrom(s, i):
        return ex.send(
            attn_ref.at[own_at(s)], abuf.at[peers[i], own_at(s)], asems, i, s, peers[i]
        )

    def all_sends(s, c):
        for i in range(3):
            acopy(s, i).start()
        return c

    lax.fori_loop(0, ex.pieces, all_sends, 0)
    abuf[hd] = attn_ref[pl.ds(pl.multiple_of(hd * own, own), own)]
    sums_ref[...] = jnp.zeros_like(sums_ref)
    gbu_ref[...] = jnp.zeros_like(gbu_ref)

    def first_norm(s, c):
        at = own_at(s)
        for i in range(3):
            afrom(s, i).wait_recv()
        for source in range(4):
            full[at, source * hcols : (source + 1) * hcols] = abuf[source, at]
        h = xin_ref[at] + (mm(full[at], wo_ref[...]) + row(bo_ref))
        normed, rstd = row_stats(h)
        xh1[at] = normed
        rs1[at] = jnp.broadcast_to(rstd, (piece, LANES))
        fin[ex.rows(hd, s)] = (normed * row(g1_ref) + row(s1_ref)).astype(BF)
        ex.gather(fin, f1sems, 0, s).start()
        ex.gather(fin, f1sems, 1, s).start()
        return c

    lax.fori_loop(0, ex.pieces, first_norm, 0)

    def pipeline(buf, fsems, snd, rcv, rsems, compute):
        def near(s):
            ex.gather_from(buf, fsems, 1, s).wait_recv()
            part = compute(ex.rows(hd, s), ex.rows(sib, s))
            ownp[own_at(s)] = part[:piece]
            snd[0, s] = part[piece:].astype(BF)
            ex.partial(snd, rcv, rsems, 0, s).start()

        def far(s):
            ex.gather_from(buf, fsems, 2, s).wait_recv()
            part = compute(ex.rows(cross, s), ex.rows(diag, s))
            crossp[own_at(s)] = part[:piece]
            snd[1, s] = part[piece:].astype(BF)
            ex.partial(snd, rcv, rsems, 1, s).start()

        def combine(s):
            ex.partial(snd, rcv, rsems, 1, s).wait_recv()
            snd[2, s] = (crossp[own_at(s)] + rcv[1, s].astype(F32)).astype(BF)
            ex.partial(snd, rcv, rsems, 2, s).start()

        def step(s, c):
            @pl.when(s >= 2)
            def _():
                combine(s - 2)

            @pl.when(s < ex.pieces)
            def _():
                near(s)
                ex.gather_from(buf, fsems, 0, s).wait_recv()
                ex.gather(buf, fsems, 2, s).start()

            @pl.when((s >= 1) & (s <= ex.pieces))
            def _():
                far(s - 1)

            return c

        lax.fori_loop(0, ex.pieces + 2, step, 0)

    def collected(rcv, rsems, snd, s):
        ex.partial(snd, rcv, rsems, 0, s).wait_recv()
        ex.partial(snd, rcv, rsems, 2, s).wait_recv()
        return ownp[own_at(s)] + rcv[0, s].astype(F32) + rcv[2, s].astype(F32)

    def forward(at_a, at_b):
        x = jnp.concatenate([fin[at_a], fin[at_b]], axis=0)
        value, slope = gelu_pair(mm(x, wu_ref[...]) + row(bu_ref))
        low = value.astype(BF)
        gl[at_a] = low[:piece]
        gl[at_b] = low[piece:]
        gd[at_a] = slope[:piece]
        gd[at_b] = slope[piece:]
        return mm(low, wd_ref[...])

    pipeline(fin, f1sems, snd1, rcv1, r1sems, forward)

    def second_norm(s, c):
        at = own_at(s)
        mid = xh1[at] * row(g1_ref) + row(s1_ref)
        h = mid + (collected(rcv1, r1sems, snd1, s) + row(bd_ref))
        normed, rstd = row_stats(h)
        out_ref[at] = (normed * row(g2_ref) + row(s2_ref)).astype(BF)
        cot = cot_ref[at].astype(F32)
        add_row(sums_ref, 2, cot * normed)
        add_row(sums_ref, 3, cot)
        grad = norm_back(cot * row(g2_ref), normed, rstd)
        two[at] = grad
        add_row(sums_ref, 5, grad)
        fgr[ex.rows(hd, s)] = grad.astype(BF)
        ex.gather(fgr, f2sems, 0, s).start()
        ex.gather(fgr, f2sems, 1, s).start()
        return c

    lax.fori_loop(0, ex.pieces, second_norm, 0)

    def backward(at_a, at_b):
        x = jnp.concatenate([fgr[at_a], fgr[at_b]], axis=0)
        slope = jnp.concatenate([gd[at_a], gd[at_b]], axis=0)
        low = (mm_nt(x, wd_ref[...]) * slope).astype(BF)
        gpre[at_a] = low[:piece]
        gpre[at_b] = low[piece:]
        add_row(gbu_ref, 0, low.astype(F32))
        return mm_nt(low, wu_ref[...])

    pipeline(fgr, f2sems, snd2, rcv2, r2sems, backward)
    outer_sum(gwd_ref, gl, fgr, gl.shape[0])

    def gcopy(s, i, source):
        return ex.send(
            abuf.at[peers[i], own_at(s)], ga_ref.at[ex.rows(source, s)], gsems, i, s, peers[i]
        )

    for i in range(3):
        for s in range(ex.pieces):
            acopy(s, i).wait_send()

    def last_norm(s, c):
        at = own_at(s)
        grad = two[at] + collected(rcv2, r2sems, snd2, s)
        normed = xh1[at]
        add_row(sums_ref, 0, grad * normed)
        add_row(sums_ref, 1, grad)
        one = norm_back(grad * row(g1_ref), normed, rs1[at][:, 0:1])
        gone_ref[at] = one
        add_row(sums_ref, 4, one)
        low = one.astype(BF)
        fin[at] = low
        heads = mm_nt(low, wo_ref[...]).astype(BF)
        for source in range(4):
            abuf[source, at] = heads[:, source * hcols : (source + 1) * hcols]
        for i in range(3):
            gcopy(s, i, hd).start()
        return c

    outer_sum(gwu_ref, fin, gpre, fin.shape[0])
    for s in range(ex.pieces):
        for i in range(3):
            ex.gather(fin, f1sems, i, s).wait_send()
    lax.fori_loop(0, ex.pieces, last_norm, 0)
    ga_ref[pl.ds(pl.multiple_of(hd * own, own), own)] = abuf[hd]
    outer_sum(gwo_ref, full, fin, own)
    for s in range(ex.pieces):
        for i in range(3):
            gcopy(s, i, peers[i]).wait()
            ex.partial(snd1, rcv1, r1sems, i, s).wait_send()
            ex.gather(fgr, f2sems, i, s).wait_send()
            ex.partial(snd2, rcv2, r2sems, i, s).wait_send()


def middle(attn, x_in, cotangent, w_out, w_up, w_down, vectors):
    own, width = x_in.shape
    group, hcols = attn.shape
    hidden = w_up.shape[1]
    pieces = 4
    piece = own // pieces
    dma = pltpu.SemaphoreType.DMA
    exchange = pltpu.VMEM((3, pieces, piece, width), BF)
    return pl.pallas_call(
        middle_kernel,
        out_shape=(
            jax.ShapeDtypeStruct((own, width), BF),
            jax.ShapeDtypeStruct((own, width), F32),
            jax.ShapeDtypeStruct((group, hcols), BF),
            jax.ShapeDtypeStruct((4 * hcols, width), F32),
            jax.ShapeDtypeStruct((width, hidden), F32),
            jax.ShapeDtypeStruct((hidden, width), F32),
            jax.ShapeDtypeStruct((8, width), F32),
            jax.ShapeDtypeStruct((1, hidden), F32),
        ),
        in_specs=[VM] * 13,
        out_specs=(VM,) * 8,
        scratch_shapes=[
            pltpu.VMEM((4, own, hcols), BF),
            pltpu.VMEM((own, 4 * hcols), BF),
            pltpu.VMEM((group, width), BF),
            pltpu.VMEM((group, hidden), BF),
            pltpu.VMEM((group, hidden), F32),
            pltpu.VMEM((group, width), BF),
            pltpu.VMEM((group, hidden), BF),
            pltpu.VMEM((own, width), F32),
            pltpu.VMEM((own, LANES), F32),
            pltpu.VMEM((own, width), F32),
            pltpu.VMEM((own, width), F32),
            pltpu.VMEM((own, width), F32),
            exchange,
            exchange,
            exchange,
            exchange,
        ]
        + [dma((2, 3, pieces))] * 6,
        compiler_params=pltpu.CompilerParams(
            collective_id=1, has_side_effects=True, vmem_limit_bytes=VMEM_CAP
        ),
        name="middle",
    )(attn, x_in, cotangent, w_out, w_up, w_down, *vectors)


def attend_back_kernel(
    len_ref,
    q0_ref,
    q1_ref,
    k0_ref,
    k1_ref,
    vx_ref,
    o_ref,
    go_ref,
    dqkv_ref,
    gt_ref,
    dox,
    kacc,
    vacc,
    qacc,
    map0,
    map1,
):
    heads, group = q0_ref.shape[0], q0_ref.shape[1]
    width = heads * DH
    lens = [len_ref[0, d] for d in range(len_ref.shape[1])]
    lane = iota((BLK, LANES), 1)
    spread = (
        iota((width, heads * LANES), 0) // DH == iota((width, heads * LANES), 1) // LANES
    ).astype(F32).astype(BF)
    map0[...] = jnp.zeros_like(map0)
    map1[...] = jnp.zeros_like(map1)
    kacc[...] = jnp.zeros_like(kacc)
    vacc[...] = jnp.zeros_like(vacc)

    def prepare(qb, carry):
        at = pl.ds(pl.multiple_of(qb * BLK, BLK), BLK)
        g = go_ref[at].astype(F32)
        e = g * o_ref[at].astype(F32)
        e_high = e.astype(BF)
        e_low = (e - e_high.astype(F32)).astype(BF)
        dots = mm(e_high, spread) + mm(e_low, spread)
        for h in range(heads):
            rest = -dots[:, h * LANES : (h + 1) * LANES]
            tile = jnp.where(
                lane < DH,
                jnp.concatenate([g[:, h * DH : (h + 1) * DH], jnp.zeros((BLK, DH), F32)], axis=1),
                0.0,
            )
            for i in range(3):
                part = rest.astype(BF).astype(F32)
                tile = jnp.where(lane == DH + i, part, tile)
                rest = rest - part
            dox[h, at] = tile.astype(BF)
        return carry

    lax.fori_loop(0, group // BLK, prepare, 0)

    def block(qb, carry):
        low, high = block_window(qb, lens, group)
        at = pl.ds(pl.multiple_of(qb * BLK, BLK), BLK)
        qacc[...] = jnp.zeros_like(qacc)

        def pair(kb, c):
            ks = pl.ds(pl.multiple_of(kb * BLK, BLK), BLK)
            for h in range(heads):
                q0 = q0_ref[h, at]
                qa = jnp.concatenate([q0, q1_ref[h, at]], axis=1)
                ka = jnp.concatenate([k0_ref[h, ks], k1_ref[ks]], axis=1)
                g = dox[h, at]
                p = jnp.exp(mm_nt(ka, qa))
                ds = (p * mm_nt(vx_ref[h, ks], g)).astype(BF)
                vacc[h, ks] += mm(p.astype(BF), g)
                kacc[h, ks] += mm(ds, q0)
                qacc[h] += mm_tn(ds, ka)
            return c

        lax.fori_loop(low, high, pair, 0)
        for h in range(heads):
            a = qacc[h]
            dqkv_ref[at, h * DH : (h + 1) * DH] = (a[:, :DH] * 0.125).astype(BF)
            high_part = a.astype(BF)
            low_part = (a - high_part.astype(F32)).astype(BF)
            for m, hot, cols in (
                (map0, k0_ref[h, at], slice(0, LANES)),
                (map1, k1_ref[at], slice(LANES, 2 * LANES)),
            ):
                both = jnp.concatenate([high_part[:, cols], low_part[:, cols]], axis=1)
                m[h] += mm_tn(hot, both)
        return carry

    lax.fori_loop(0, group // BLK, block, 0)

    def finish(kb, carry):
        at = pl.ds(pl.multiple_of(kb * BLK, BLK), BLK)
        for h in range(heads):
            k_at, v_at = width + h * DH, 2 * width + h * DH
            dqkv_ref[at, k_at : k_at + DH] = kacc[h, at][:, :DH].astype(BF)
            dqkv_ref[at, v_at : v_at + DH] = vacc[h, at][:, :DH].astype(BF)
        return carry

    lax.fori_loop(0, group // BLK, finish, 0)

    gt_ref[...] = jnp.zeros_like(gt_ref)
    r_i, l_i = iota((LANES, LANES), 0), iota((LANES, LANES), 1)

    def exact(a, b):
        return jnp.dot(a, b, precision=lax.Precision.HIGHEST, preferred_element_type=F32)

    def diagonals(block, base, count):
        inside = (r_i >= base) & (r_i < base + count) & (l_i >= base) & (l_i < base + count)
        flip = ((l_i == base + count - 1 - r_i) & (r_i < count)).astype(F32)
        turned = exact(flip, jnp.where(inside, block, 0.0))
        moved = pltpu.roll(turned, (64 - base - count) % LANES, 1, stride=1, stride_axis=0)
        return jnp.sum(moved, axis=0, keepdims=True)

    def fold(block, base, count):
        sums = jnp.broadcast_to(diagonals(block, base, count), (8, LANES))
        j_i, t_i = iota((LANES, count), 0), iota((LANES, count), 1)
        low = 63 - count // 2
        pick = (t_i == jnp.clip(j_i - low, 0, count - 1)).astype(F32)
        return exact(sums, pick)[0:1]

    for h in range(heads):
        one = map1[h][:, :LANES] + map1[h][:, LANES:]
        zero = map0[h][:, :LANES] + map0[h][:, LANES:]
        gt_ref[h : h + 1, 0:POSB] = fold(one, 64, POSB)
        gt_ref[heads + h : heads + h + 1, 0:BOXB] = fold(one, 0, BOXB)
        gt_ref[2 * heads + h : 2 * heads + h + 1, 0:BOXB] = fold(zero, 64, BOXB)


def attend_back(lengths, q0, q1, k0, k1, vx, out, grad_out):
    heads, group, _ = q0.shape
    return pl.pallas_call(
        attend_back_kernel,
        out_shape=(
            jax.ShapeDtypeStruct((group, 3 * heads * DH), BF),
            jax.ShapeDtypeStruct((16, LANES), F32),
        ),
        in_specs=[SM] + [VM] * 7,
        out_specs=(VM,) * 2,
        scratch_shapes=[
            pltpu.VMEM((heads, group, LANES), BF),
            pltpu.VMEM((heads, group, LANES), F32),
            pltpu.VMEM((heads, group, LANES), F32),
            pltpu.VMEM((heads, BLK, 2 * LANES), F32),
            pltpu.VMEM((heads, LANES, 2 * LANES), F32),
            pltpu.VMEM((heads, LANES, 2 * LANES), F32),
        ],
        compiler_params=pltpu.CompilerParams(vmem_limit_bytes=VMEM_CAP),
        name="attend_back",
    )(lengths, q0, q1, k0, k1, vx, out, grad_out)


class Reduce:
    def __init__(self, value, snd, rcv, psnd, prcv, half, other, mine, sems, psems):
        self.value, self.snd, self.rcv, self.psnd, self.prcv = value, snd, rcv, psnd, prcv
        self.half, self.other, self.mine, self.sems, self.psems = half, other, mine, sems, psems
        self.members, self.part = half.shape[0], half.shape[1]
        dp = lax.axis_index("dp")
        self.bit = lax.rem(dp, 2)
        self.partner = dp + 1 - 2 * self.bit
        self.me = dp // 2

    def at(self, bit, j):
        step = self.part
        return pl.ds(pl.multiple_of((bit * self.members + j) * step, 8), step)

    def pair(self, i, src, dst):
        return pltpu.make_async_remote_copy(
            src_ref=src,
            dst_ref=dst,
            send_sem=self.sems.at[0, i],
            recv_sem=self.sems.at[1, i],
            device_id={"dp": self.partner},
            device_id_type=MESH,
        )

    def first(self):
        return self.pair(0, self.snd, self.rcv)

    def fourth(self):
        return self.pair(1, self.half, self.other)

    def member(self, i, k, src, slot_of_receiver):
        target = lax.rem(self.me + k, self.members)
        return pltpu.make_async_remote_copy(
            src_ref=src.at[target] if i == 0 else src.at[self.me],
            dst_ref=slot_of_receiver.at[self.me],
            send_sem=self.psems.at[i, 0, k],
            recv_sem=self.psems.at[i, 1, k],
            device_id={"dp": 2 * target + self.bit},
            device_id_type=MESH,
        )

    def second(self, k):
        return self.member(0, k, self.psnd, self.prcv)

    def third(self, k):
        return self.member(1, k, self.half, self.half)

    def arrived(self, i, k):
        source = lax.rem(self.me - k + self.members, self.members)
        buf = self.prcv if i == 0 else self.half
        return pltpu.make_async_remote_copy(
            src_ref=buf.at[source],
            dst_ref=buf.at[source],
            send_sem=self.psems.at[i, 0, k],
            recv_sem=self.psems.at[i, 1, k],
            device_id={"dp": 2 * source + self.bit},
            device_id_type=MESH,
        )

    def loop(self, low, fn):
        def step(j, c):
            fn(j)
            return c

        lax.fori_loop(low, self.members, step, 0)

    def start(self):
        def fill(j):
            self.snd[j] = self.value[self.at(1 - self.bit, j)].astype(BF)

        self.loop(0, fill)
        self.first().start()

    def spread(self):
        self.first().wait()

        def fill(k):
            j = lax.rem(self.me + k, self.members)
            self.psnd[j] = (
                self.value[self.at(self.bit, j)] + self.rcv[j].astype(F32)
            ).astype(BF)
            self.second(k).start()

        self.loop(1, fill)
        self.mine[...] = self.value[self.at(self.bit, self.me)] + self.rcv[self.me].astype(F32)

    def total(self):
        def take(k):
            self.arrived(0, k).wait_recv()
            source = lax.rem(self.me - k + self.members, self.members)
            self.mine[...] += self.prcv[source].astype(F32)

        self.loop(1, take)
        self.half[self.me] = self.mine[...].astype(BF)
        self.loop(1, lambda k: self.third(k).start())

    def share(self):
        self.loop(1, lambda k: self.arrived(1, k).wait_recv())
        self.fourth().start()

    def finish(self, store):
        self.loop(0, lambda j: store(self.at(self.bit, j), self.half[j].astype(F32)))
        self.fourth().wait()
        self.loop(0, lambda j: store(self.at(1 - self.bit, j), self.other[j].astype(F32)))

        def done(k):
            self.second(k).wait_send()
            self.third(k).wait_send()

        self.loop(1, done)


def final_kernel(
    len_ref,
    dqkv_ref,
    w_ref,
    a_ref,
    tok_ref,
    st_ref,
    gone_ref,
    gain_ref,
    gwu_ref,
    gwd_ref,
    gwo_ref,
    sums_ref,
    gbu_ref,
    gt_ref,
    gtok_ref,
    all_ref,
    gw_ref,
    gb_ref,
    gp_ref,
    gx_ref,
    gwoo_ref,
    gwuo_ref,
    gbuo_ref,
    gwdo_ref,
    wcat,
    mixed,
    ownp,
    crossp,
    snd,
    rcv,
    osnd,
    orcv,
    hbuf,
    dbuf,
    rsems,
    osems,
    hsems,
    dsems,
    *reduce_refs,
):
    own, width = gone_ref.shape
    hcols = w_ref.shape[2]
    heads = hcols // DH
    n_dp = dbuf.shape[0]
    docs = len_ref.shape[1]
    pieces = rsems.shape[2]
    piece = own // pieces
    ex = Exchange(own, piece)
    hd, sib, cross, diag = ex.hd, ex.sib, ex.cross, ex.diag
    dp = lax.axis_index("dp")
    barrier = pltpu.get_barrier_semaphore()
    for peer in (sib, cross, diag):
        pl.semaphore_signal(barrier, inc=1, device_id={"head": peer}, device_id_type=MESH)

    def greet(j, carry):
        pl.semaphore_signal(
            barrier, inc=1, device_id={"dp": lax.rem(dp + j, n_dp)}, device_id_type=MESH
        )
        return carry

    lax.fori_loop(1, n_dp, greet, 0)
    pl.semaphore_wait(barrier, n_dp + 2)

    per = len(reduce_refs) // 3
    down, up, rest = [
        Reduce(value, *reduce_refs[i * per : (i + 1) * per])
        for i, value in enumerate((gwd_ref, gwu_ref, mixed))
    ]
    down.start()
    up.start()

    def own_at(s):
        return pl.ds(pl.multiple_of(s * piece, piece), piece)

    for e in range(3):
        wcat[:, e * hcols : (e + 1) * hcols] = w_ref[e]

    def grad_rows(at):
        return mm_nt(dqkv_ref[at], wcat[...])

    def far(s, c):
        snd[1, s] = grad_rows(ex.rows(diag, s)).astype(BF)
        ex.partial(snd, rcv, rsems, 1, s).start()
        crossp[own_at(s)] = grad_rows(ex.rows(cross, s))
        return c

    def mix(s, c):
        ex.partial(snd, rcv, rsems, 1, s).wait_recv()
        snd[2, s] = (crossp[own_at(s)] + rcv[1, s].astype(F32)).astype(BF)
        ex.partial(snd, rcv, rsems, 2, s).start()
        return c

    def near(s, c):
        snd[0, s] = grad_rows(ex.rows(sib, s)).astype(BF)
        ex.partial(snd, rcv, rsems, 0, s).start()
        ownp[own_at(s)] = grad_rows(ex.rows(hd, s))
        return c

    lax.fori_loop(0, pieces, far, 0)
    lax.fori_loop(0, pieces, mix, 0)
    lax.fori_loop(0, pieces, near, 0)

    def block_of(source):
        return pl.ds(pl.multiple_of(source * hcols, DH), hcols)

    def osend(i):
        return ex.send(
            osnd.at[i], orcv.at[i], osems, i, 0, cross if i == 2 else sib
        )

    osnd[1] = gwo_ref[block_of(diag)].astype(BF)
    osend(1).start()
    osnd[0] = gwo_ref[block_of(sib)].astype(BF)
    osend(0).start()

    def weight_step(m, c):
        cols = pl.ds(pl.multiple_of(m * BLK, BLK), BLK)
        mixed[cols, 0 : 3 * hcols] = mm_tn(a_ref[:, cols], dqkv_ref[...])
        return c

    osend(1).wait_recv()
    osnd[2] = (gwo_ref[block_of(cross)] + orcv[1].astype(F32)).astype(BF)
    osend(2).start()
    lax.fori_loop(0, width // BLK, weight_step, 0)
    osend(0).wait_recv()
    osend(2).wait_recv()
    gwo = gwo_ref[block_of(hd)] + orcv[0].astype(F32) + orcv[2].astype(F32)
    for b in range(4):
        mixed[b * hcols : (b + 1) * hcols, 3 * hcols :] = gwo[:, b * hcols : (b + 1) * hcols]
    rest.start()
    down.spread()
    up.spread()

    lens = [len_ref[0, d] for d in range(docs)]
    mean, inv_std = st_ref[0:1], st_ref[1:2]
    hbuf[hd] = sums_ref[...]

    def grad_own(s, c):
        at = own_at(s)
        ex.partial(snd, rcv, rsems, 0, s).wait_recv()
        ex.partial(snd, rcv, rsems, 2, s).wait_recv()
        g = gone_ref[at] + (ownp[at] + rcv[0, s].astype(F32) + rcv[2, s].astype(F32))
        gtok_ref[at] = g
        _, visual, _ = row_layout(iota((piece, LANES), 0) + (hd * own + s * piece), lens)
        g = jnp.where(visual[:, 0:1], g, 0.0)
        x_hat = (tok_ref[at].astype(F32) - mean) * inv_std
        hbuf[hd, 6:7] += jnp.sum(g, axis=0, keepdims=True)
        hbuf[hd, 7:8] += jnp.sum(g * x_hat, axis=0, keepdims=True)
        return c

    lax.fori_loop(0, pieces, grad_own, 0)

    def hcopy(i, peer):
        return ex.send(hbuf.at[hd], hbuf.at[hd], hsems, i, 0, peer)

    hcopies = [hcopy(i, peer) for i, peer in enumerate((sib, cross, diag))]
    for copy in hcopies:
        copy.start()
    dbuf[dp, 8:] = jnp.zeros((dbuf.shape[1] - 8, width), F32)
    dbuf[dp, 8:9] = gbu_ref[...]
    dbuf[dp, 9:10, 0 : 3 * hcols] = jnp.zeros((1, 3 * hcols), F32)

    def col_sums(s, c):
        at = pl.ds(pl.multiple_of(s * BLK, BLK), BLK)
        dbuf[dp, 9:10, 0 : 3 * hcols] += jnp.sum(
            dqkv_ref[at].astype(F32), axis=0, keepdims=True
        )
        return c

    lax.fori_loop(0, dqkv_ref.shape[0] // BLK, col_sums, 0)
    dbuf[dp, 16:32, 0:LANES] = gt_ref[...]
    for copy in hcopies:
        copy.wait()
    dbuf[dp, 0:8] = ((hbuf[0] + hbuf[1]) + hbuf[2]) + hbuf[3]

    def dcopy(j):
        return pltpu.make_async_remote_copy(
            src_ref=dbuf.at[dp],
            dst_ref=dbuf.at[dp],
            send_sem=dsems.at[0, j],
            recv_sem=dsems.at[1, j],
            device_id={"dp": lax.rem(dp + j, n_dp)},
            device_id_type=MESH,
        )

    def dstart(j, carry):
        dcopy(j).start()
        return carry

    def dwait(j, carry):
        dcopy(j).wait()
        return carry

    lax.fori_loop(1, n_dp, dstart, 0)
    down.total()
    rest.spread()
    up.total()
    lax.fori_loop(1, n_dp, dwait, 0)

    def dsum(j, total):
        return total + dbuf[j]

    total = lax.fori_loop(1, n_dp, dsum, dbuf[0])
    all_ref[...] = total[0:8]
    gbuo_ref[...] = total[8:9]
    gb_ref[0:1] = total[9:10, 0:hcols]
    gb_ref[1:2] = total[9:10, 2 * hcols : 3 * hcols]
    gp_ref[...] = total[16 : 16 + heads, 0:POSB]
    gx_ref[0] = total[16 + heads : 16 + 2 * heads, 0:BOXB]
    gx_ref[1] = total[16 + 2 * heads : 16 + 3 * heads, 0:BOXB]
    gain = gain_ref[...].reshape(1, width)
    count = float(VISUAL * docs) * n_dp
    shift_part = total[6:7] / count
    gain_part = total[7:8] / count
    down.share()

    def tokens_out(s, c):
        at = own_at(s)
        g = gtok_ref[at]
        _, visual, _ = row_layout(iota((piece, LANES), 0) + (hd * own + s * piece), lens)
        x_hat = (tok_ref[at].astype(F32) - mean) * inv_std
        normed = inv_std * gain * (g - (shift_part + x_hat * gain_part))
        gtok_ref[at] = jnp.where(visual[:, 0:1], normed, g)
        return c

    lax.fori_loop(0, pieces, tokens_out, 0)
    rest.total()
    up.share()

    def store_in(ref):
        def store(at, v):
            ref[at] = v

        return store

    down.finish(store_in(gwdo_ref))
    rest.share()
    up.finish(store_in(gwuo_ref))

    def store_rest(at, v):
        mixed[at] = v

    rest.finish(store_rest)
    for e in range(3):
        gw_ref[e] = mixed[:, e * hcols : (e + 1) * hcols]
    for b in range(4):
        gwoo_ref[:, b * hcols : (b + 1) * hcols] = mixed[
            b * hcols : (b + 1) * hcols, 3 * hcols :
        ]
    for i in range(3):
        osend(i).wait_send()
        for s in range(pieces):
            ex.partial(snd, rcv, rsems, i, s).wait_send()


def final(lengths, dqkv, w, attn_in, tokens, stats, gone, bn_gain, gwu, gwd, gwo, sums, gbu, gt, n_dp):
    own, width = gone.shape
    hcols = w.shape[2]
    heads = hcols // DH
    hidden = gwu.shape[1]
    pieces = 4
    piece = own // pieces
    members = n_dp // 2
    part = width // n_dp
    dma = pltpu.SemaphoreType.DMA
    exchange = pltpu.VMEM((3, pieces, piece, width), BF)
    small = pltpu.VMEM((3, hcols, width), BF)
    parts = pltpu.VMEM((members, part, width), BF)
    reduce_refs = [parts] * 6 + [
        pltpu.VMEM((part, width), F32),
        dma((2, 2)),
        dma((2, 2, members)),
    ]
    return pl.pallas_call(
        final_kernel,
        out_shape=(
            jax.ShapeDtypeStruct((own, width), F32),
            jax.ShapeDtypeStruct((8, width), F32),
            jax.ShapeDtypeStruct((3, width, hcols), F32),
            jax.ShapeDtypeStruct((2, hcols), F32),
            jax.ShapeDtypeStruct((heads, POSB), F32),
            jax.ShapeDtypeStruct((2, heads, BOXB), F32),
            jax.ShapeDtypeStruct((hcols, width), F32),
            jax.ShapeDtypeStruct((width, hidden), F32),
            jax.ShapeDtypeStruct((1, hidden), F32),
            jax.ShapeDtypeStruct((hidden, width), F32),
        ),
        in_specs=[SM] + [VM] * 13,
        out_specs=(VM,) * 10,
        scratch_shapes=[
            pltpu.VMEM((width, 3 * hcols), BF),
            pltpu.VMEM((width, width), F32),
            pltpu.VMEM((own, width), F32),
            pltpu.VMEM((own, width), F32),
            exchange,
            exchange,
            small,
            small,
            pltpu.VMEM((4, 8, width), F32),
            pltpu.VMEM((n_dp, 32, width), F32),
            dma((2, 3, pieces)),
            dma((2, 3, 1)),
            dma((2, 3, 1)),
            dma((2, n_dp)),
        ]
        + reduce_refs * 3,
        compiler_params=pltpu.CompilerParams(
            collective_id=2, has_side_effects=True, vmem_limit_bytes=VMEM_CAP
        ),
        name="final",
    )(lengths, dqkv, w, attn_in, tokens, stats, gone, bn_gain, gwu, gwd, gwo, sums, gbu, gt)


def body(
    n_dp,
    tokens,
    lengths,
    box_cells,
    bn_gain,
    bn_shift,
    query_key_value_weight,
    b_qv,
    tab_pos,
    tab_box,
    w_out,
    b_out,
    ln1_gain,
    ln1_shift,
    w_up,
    b_up,
    w_down,
    b_down,
    ln2_gain,
    ln2_shift,
    cotangent,
):
    x_in, attn_in, q0, q1, k0, k1, vx, stats, w_out_all = entry(
        tokens,
        lengths,
        box_cells,
        bn_gain,
        bn_shift,
        query_key_value_weight,
        b_qv,
        tab_pos,
        tab_box,
        w_out,
        n_dp,
    )
    attn, q1b = attend(lengths, q0, q1, k0, k1, vx)
    vectors = (b_out, ln1_gain, ln1_shift, b_up, b_down, ln2_gain, ln2_shift)
    output, grad_one, grad_attn, gwo, gwu, gwd, sums, gbu = middle(
        attn, x_in, cotangent, w_out_all, w_up, w_down, vectors
    )
    dqkv, grad_tables = attend_back(lengths, q0, q1b, k0, k1, vx, attn, grad_attn)
    grad_tokens, total, gw, gb, gp, gx, gwo, gwu, gbu, gwd = final(
        lengths,
        dqkv,
        query_key_value_weight,
        attn_in,
        tokens,
        stats,
        grad_one,
        bn_gain,
        gwu,
        gwd,
        gwo,
        sums,
        gbu,
        grad_tables,
        n_dp,
    )
    return (
        output,
        grad_tokens,
        total[7],
        total[6],
        gw,
        gb,
        gp,
        gx,
        gwo,
        total[4],
        total[0],
        total[1],
        gwu,
        gbu[0],
        gwd,
        total[5],
        total[2],
        total[3],
    )


def solution(mesh):
    rows = P(("dp", "head"), None)
    in_specs = (
        rows,
        P("dp", None),
        P(None, "dp"),
        P(),
        P(),
        P(None, None, "head"),
        P(None, "head"),
        P("head", None),
        P(None, "head", None),
        P("head", None),
        P(),
        P(),
        P(),
        P(None, "head"),
        P("head"),
        P("head", None),
        P(),
        P(),
        P(),
        rows,
    )
    out_specs = (
        rows,
        rows,
        P(),
        P(),
        P(None, None, "head"),
        P(None, "head"),
        P("head", None),
        P(None, "head", None),
        P("head", None),
        P(),
        P(),
        P(),
        P(None, "head"),
        P("head"),
        P("head", None),
        P(),
        P(),
        P(),
    )
    return jax.shard_map(
        functools.partial(body, mesh.shape["dp"]),
        mesh=mesh,
        in_specs=in_specs,
        out_specs=out_specs,
        check_vma=False,
    )
```

```python
import functools

import jax
import jax.numpy as jnp
from jax import lax
from jax.experimental import pallas as pl
from jax.experimental.pallas import tpu as pltpu
from jax.sharding import PartitionSpec as P

DH = 64
VISUAL = 49
POSB = 32
BOXB = 64
POS_STEP = 16
NORM_EPS = 1e-05
BATCH_EPS = 1e-05
BIG = float(2.0**100)
BLK = 256
LANES = 128
SEG0 = 96
LSE0 = 112
VMEM_CAP = 58 << 20

MESH = pl.DeviceIdType.MESH
BF = jnp.bfloat16
F32 = jnp.float32
I32 = jnp.int32
VM = pl.BlockSpec(memory_space=pltpu.VMEM)
SM = pl.BlockSpec(memory_space=pltpu.SMEM)


def iota(shape, dim):
    return lax.broadcasted_iota(I32, shape, dim)


def mm(a, b):
    return jnp.dot(a, b, preferred_element_type=F32)


def mm_nt(a, b):
    return lax.dot_general(a, b, (((1,), (1,)), ((), ())), preferred_element_type=F32)


def mm_tn(a, b):
    return lax.dot_general(a, b, (((0,), (0,)), ((), ())), preferred_element_type=F32)


def head_peers():
    hd = lax.axis_index("head")
    sib = hd + 1 - 2 * lax.rem(hd, 2)
    cross = lax.rem(hd + 2, 4)
    diag = lax.rem(sib + 2, 4)
    return hd, sib, cross, diag


def row_layout(rows, lens):
    seg = jnp.zeros_like(rows)
    first = jnp.zeros_like(rows)
    end = 0
    for size in lens:
        end = end + size + VISUAL
        past = rows >= end
        seg = seg + past.astype(I32)
        first = jnp.where(past, end, first)
    offset = rows - first
    visual = jnp.logical_and(seg < len(lens), offset < VISUAL)
    position = jnp.where(visual, offset, offset - VISUAL)
    bucket = jnp.minimum(lax.shift_right_logical(jnp.maximum(position, 0), 4), POSB - 1)
    return seg, visual, bucket


def block_window(block, lens, group_rows):
    first, last = block * BLK, block * BLK + BLK - 1
    low, high, end = 0, group_rows, 0
    ends = []
    for size in lens:
        end = end + size + VISUAL
        ends.append(end)
        low = jnp.where(first >= end, end, low)
    for end in reversed(ends):
        high = jnp.where(last < end, end, high)
    return low // BLK, (high + BLK - 1) // BLK


def row(ref):
    return ref[...].reshape(1, ref.shape[0])


def head_and_dp_barrier(n_dp):
    barrier = pltpu.get_barrier_semaphore()
    dp = lax.axis_index("dp")
    for peer in head_peers()[1:]:
        pl.semaphore_signal(barrier, inc=1, device_id={"head": peer}, device_id_type=MESH)

    def greet(j, carry):
        pl.semaphore_signal(
            barrier, inc=1, device_id={"dp": lax.rem(dp + j, n_dp)}, device_id_type=MESH
        )
        return carry

    lax.fori_loop(1, n_dp, greet, 0)
    return lambda: pl.semaphore_wait(barrier, n_dp + 2)


class Reduce:
    def __init__(self, members, part, refs, value=None, base=0):
        self.members, self.part, self.value, self.base = members, part, value, base
        for name, ref in refs.items():
            setattr(self, name, ref)
        dp = lax.axis_index("dp")
        self.bit = lax.rem(dp, 2)
        self.partner = dp + 1 - 2 * self.bit
        self.me = dp // 2

    def at(self, bit, j, base=None):
        base = self.base if base is None else base
        step = self.part
        return pl.ds(pl.multiple_of(base + (bit * self.members + j) * step, 8), step)

    def pair(self, i, src, dst):
        return pltpu.make_async_remote_copy(
            src_ref=src,
            dst_ref=dst,
            send_sem=self.sems.at[0, i],
            recv_sem=self.sems.at[1, i],
            device_id={"dp": self.partner},
            device_id_type=MESH,
        )

    def first(self):
        return self.pair(0, self.snd, self.rcv)

    def fourth(self):
        return self.pair(1, self.half, self.other)

    def member(self, i, k, src, slot):
        target = lax.rem(self.me + k, self.members)
        return pltpu.make_async_remote_copy(
            src_ref=src.at[target] if i == 0 else src.at[self.me],
            dst_ref=slot.at[self.me],
            send_sem=self.psems.at[i, 0, k],
            recv_sem=self.psems.at[i, 1, k],
            device_id={"dp": 2 * target + self.bit},
            device_id_type=MESH,
        )

    def second(self, k):
        return self.member(0, k, self.psnd, self.prcv)

    def third(self, k):
        return self.member(1, k, self.half, self.half)

    def arrived(self, i, k):
        source = lax.rem(self.me - k + self.members, self.members)
        buf = self.prcv if i == 0 else self.half
        return pltpu.make_async_remote_copy(
            src_ref=buf.at[source],
            dst_ref=buf.at[source],
            send_sem=self.psems.at[i, 0, k],
            recv_sem=self.psems.at[i, 1, k],
            device_id={"dp": 2 * source + self.bit},
            device_id_type=MESH,
        )

    def loop(self, low, fn):
        def step(j, c):
            fn(j)
            return c

        lax.fori_loop(low, self.members, step, 0)

    def start(self):
        def fill(j):
            self.snd[j] = self.value[self.at(1 - self.bit, j)].astype(BF)

        self.loop(0, fill)
        self.first().start()

    def halves(self, j):
        return self.value[self.at(self.bit, j)] + self.rcv[j].astype(F32)

    def collect(self, out):
        self.first().wait()

        def keep(j):
            out[j] = self.halves(j)

        self.loop(0, keep)

    def spread(self, sums=None):
        if sums is None:
            self.first().wait()
        take = self.halves if sums is None else (lambda j: sums[j])

        def fill(k):
            j = lax.rem(self.me + k, self.members)
            self.psnd[j] = take(j).astype(BF)
            self.second(k).start()

        self.loop(1, fill)
        self.mine[...] = take(self.me)

    def gather(self):
        def take(k):
            self.arrived(0, k).wait_recv()
            source = lax.rem(self.me - k + self.members, self.members)
            self.mine[...] += self.prcv[source].astype(F32)

        self.loop(1, take)

    def publish(self, total=None):
        self.half[self.me] = self.mine[...].astype(BF) if total is None else total
        self.loop(1, lambda k: self.third(k).start())

    def share(self):
        self.loop(1, lambda k: self.arrived(1, k).wait_recv())
        self.fourth().start()

    def finish(self, out, base=0):
        def near(j):
            out[self.at(self.bit, j, base)] = self.half[j]

        def far(j):
            out[self.at(1 - self.bit, j, base)] = self.other[j]

        self.loop(0, near)
        self.fourth().wait()
        self.loop(0, far)
        self.loop(1, lambda k: self.third(k).wait_send())

    def sent(self):
        self.loop(1, lambda k: self.second(k).wait_send())


def entry_kernel(
    len_ref,
    tok_ref,
    box_ref,
    gain_ref,
    shift_ref,
    w_ref,
    b_ref,
    tp_ref,
    tb_ref,
    wo_ref,
    xin_ref,
    a_ref,
    q0_ref,
    q1_ref,
    k0_ref,
    k1_ref,
    vx_ref,
    st_ref,
    wof_ref,
    abuf,
    hbuf,
    dbuf,
    map0,
    map1,
    hsend,
    hrecv,
    dsend,
    drecv,
    asend,
    arecv,
    wsend,
    wrecv,
    osem,
):
    n_dp = dbuf.shape[0]
    own = tok_ref.shape[0]
    group = abuf.shape[0]
    docs = len_ref.shape[1]
    heads = w_ref.shape[1] // DH
    hd, sib, cross, diag = head_peers()
    dp = lax.axis_index("dp")
    lens = [len_ref[0, d] for d in range(docs)]

    barrier = pltpu.get_barrier_semaphore()
    for peer in (sib, cross, diag):
        pl.semaphore_signal(barrier, inc=1, device_id={"head": peer}, device_id_type=MESH)

    def greet(j, carry):
        pl.semaphore_signal(
            barrier, inc=1, device_id={"dp": lax.rem(dp + j, n_dp)}, device_id_type=MESH
        )
        return carry

    lax.fori_loop(1, n_dp, greet, 0)

    rows = iota((own, LANES), 0) + hd * own
    _, visual, _ = row_layout(rows, lens)
    vis_f = visual.astype(F32)
    for c in range(0, tok_ref.shape[1], LANES):
        v = tok_ref[:, c : c + LANES].astype(F32) * vis_f
        hbuf[hd, 0:1, c : c + LANES] = jnp.sum(v, axis=0, keepdims=True)
        hbuf[hd, 1:2, c : c + LANES] = jnp.sum(v * v, axis=0, keepdims=True)
    pl.semaphore_wait(barrier, n_dp + 2)

    def hcopy(i, peer):
        return pltpu.make_async_remote_copy(
            src_ref=hbuf.at[hd],
            dst_ref=hbuf.at[hd],
            send_sem=hsend.at[i],
            recv_sem=hrecv.at[i],
            device_id={"head": peer},
            device_id_type=MESH,
        )

    hcopies = [hcopy(i, peer) for i, peer in enumerate((sib, cross, diag))]
    for copy in hcopies:
        copy.start()

    part = wo_ref.shape[0]

    def wcopy(source, i, peer):
        at = pl.ds(pl.multiple_of(source * part, DH), part)
        return pltpu.make_async_remote_copy(
            src_ref=wof_ref.at[at],
            dst_ref=wof_ref.at[at],
            send_sem=wsend.at[i],
            recv_sem=wrecv.at[i],
            device_id={"head": peer},
            device_id_type=MESH,
        )

    wof_ref[pl.ds(pl.multiple_of(hd * part, DH), part)] = wo_ref[...]
    wcopy(hd, 0, cross).start()
    wcopy(hd, 1, sib).start()

    r_i, l_i = iota((LANES, LANES), 0), iota((LANES, LANES), 1)

    def toeplitz(table, count):
        t_i, j_i = iota((count, LANES), 0), iota((count, LANES), 1)
        low = 63 - count // 2
        pick = (t_i == jnp.clip(j_i - low, 0, count - 1)).astype(BF)
        ext = mm(table.astype(BF), pick)
        return [
            pltpu.roll(jnp.broadcast_to(ext[h : h + 1], (LANES, LANES)), 65, 1, stride=1, stride_axis=0)
            for h in range(heads)
        ]

    pos_t = toeplitz(tp_ref[...], POSB)
    x_t = toeplitz(tb_ref[:, 0, :], BOXB)
    y_t = toeplitz(tb_ref[:, 1, :], BOXB)

    def within(low, high):
        return (r_i >= low) & (r_i < high) & (l_i >= low) & (l_i < high)

    seg_part = jnp.where(within(SEG0, LSE0) & (r_i != l_i), -BIG, 0.0)
    for h in range(heads):
        map1[h] = jnp.where(
            within(0, 64), x_t[h], jnp.where(within(64, 96), pos_t[h], seg_part)
        ).astype(BF)
        map0[h] = jnp.where(within(64, 128), y_t[h], 0.0).astype(BF)

    for copy in hcopies:
        copy.wait()
    dbuf[dp] = ((hbuf[0] + hbuf[1]) + hbuf[2]) + hbuf[3]

    def dcopy(j):
        return pltpu.make_async_remote_copy(
            src_ref=dbuf.at[dp],
            dst_ref=dbuf.at[dp],
            send_sem=dsend.at[j],
            recv_sem=drecv.at[j],
            device_id={"dp": lax.rem(dp + j, n_dp)},
            device_id_type=MESH,
        )

    def dstart(j, carry):
        dcopy(j).start()
        return carry

    def dwait(j, carry):
        dcopy(j).wait()
        return carry

    lax.fori_loop(1, n_dp, dstart, 0)

    def features(c, carry):
        at = pl.ds(pl.multiple_of(c * LANES, LANES), LANES)
        seg, _, bucket = row_layout(r_i + c * LANES, lens)
        bx = jnp.broadcast_to(box_ref[0:1, at].astype(F32), (LANES, LANES)).T.astype(I32)
        by = jnp.broadcast_to(box_ref[1:2, at].astype(F32), (LANES, LANES)).T.astype(I32)
        hot = (
            (l_i == bx)
            | (l_i == bucket + 64)
            | (l_i == seg + SEG0)
        )
        key1 = hot.astype(F32)
        k1_ref[at] = jnp.where((l_i >= LSE0) & (l_i < LSE0 + 3), 1.0, key1).astype(BF)
        key1 = key1.astype(BF)
        key0 = (l_i == by + 64).astype(F32).astype(BF)
        for h in range(heads):
            q1_ref[h, at] = mm(key1, map1[h]).astype(BF)
            q0_ref[h, at] = mm(key0, map0[h]).astype(BF)
            k0_ref[h, at] = key0
        return carry

    lax.fori_loop(0, group // LANES, features, 0)
    lax.fori_loop(1, n_dp, dwait, 0)

    def dsum(j, total):
        return total + dbuf[j]

    total = lax.fori_loop(1, n_dp, dsum, dbuf[0])
    count = float(VISUAL * docs) * n_dp
    mean = total[0:1] / count
    inv_std = lax.rsqrt(total[1:2] / count - mean * mean + BATCH_EPS)
    st_ref[0:1] = mean
    st_ref[1:2] = inv_std
    pieces = asend.shape[1]
    piece = own // pieces

    def acopy(source, s, i, peer):
        at = pl.ds(pl.multiple_of(source * own + s * piece, piece), piece)
        return pltpu.make_async_remote_copy(
            src_ref=abuf.at[at],
            dst_ref=abuf.at[at],
            send_sem=asend.at[i, s],
            recv_sem=arecv.at[i, s],
            device_id={"head": peer},
            device_id_type=MESH,
        )

    for s in range(pieces):
        at = pl.ds(s * piece, piece)
        v = tok_ref[at].astype(F32)
        vis = vis_f[s * piece : (s + 1) * piece, 0:1] > 0.5
        x_in = jnp.where(vis, (v - mean) * inv_std * row(gain_ref) + row(shift_ref), v)
        xin_ref[at] = x_in
        abuf[pl.ds(pl.multiple_of(hd * own + s * piece, piece), piece)] = x_in.astype(BF)
        acopy(hd, s, 0, cross).start()
        acopy(hd, s, 1, sib).start()

    lane = iota((piece, LANES), 1)

    def project(source, s):
        at = pl.ds(pl.multiple_of(source * own + s * piece, piece), piece)
        a = abuf[at]
        q = ((mm_nt(a, w_ref[0]) + b_ref[0:1]).astype(BF)).astype(F32) * 0.125
        k = mm_nt(a, w_ref[1])
        v = mm_nt(a, w_ref[2]) + b_ref[1:2]
        for h in range(heads):
            cols = slice(h * DH, (h + 1) * DH)
            zero = jnp.zeros((piece, DH), F32)
            q0_ref[h, at] = jnp.where(
                lane < DH, jnp.concatenate([q[:, cols], zero], axis=1), q0_ref[h, at].astype(F32)
            ).astype(BF)
            k0_ref[h, at] = jnp.where(
                lane < DH, jnp.concatenate([k[:, cols], zero], axis=1), k0_ref[h, at].astype(F32)
            ).astype(BF)
            vx_ref[h, at] = jnp.where(
                lane < DH, jnp.concatenate([v[:, cols], zero], axis=1), 1.0
            ).astype(BF)

    def loop_project(source):
        def step(s, carry):
            project(source, s)
            return carry

        lax.fori_loop(0, pieces, step, 0)

    loop_project(hd)
    wcopy(cross, 0, cross).wait_recv()
    wcopy(cross, 2, sib).start()
    for s in range(pieces):
        acopy(sib, s, 1, sib).wait_recv()
    loop_project(sib)
    for s in range(pieces):
        acopy(cross, s, 0, cross).wait_recv()
        acopy(cross, s, 2, sib).start()
        project(cross, s)
    for s in range(pieces):
        acopy(diag, s, 2, sib).wait_recv()
        project(diag, s)
    out = pltpu.make_async_copy(abuf, a_ref, osem)
    out.start()
    wcopy(sib, 1, sib).wait_recv()
    wcopy(diag, 2, sib).wait_recv()
    wcopy(hd, 0, cross).wait_send()
    wcopy(hd, 1, sib).wait_send()
    wcopy(cross, 2, sib).wait_send()
    for s in range(pieces):
        acopy(hd, s, 0, cross).wait_send()
        acopy(hd, s, 1, sib).wait_send()
        acopy(cross, s, 2, sib).wait_send()
    out.wait()


def entry(tokens, lengths, box_cells, bn_gain, bn_shift, w, b_qv, tab_pos, tab_box, w_out, n_dp):
    own, width = tokens.shape
    group = box_cells.shape[1]
    heads = w.shape[1] // DH
    pieces = 4
    tile = jax.ShapeDtypeStruct((heads, group, LANES), BF)
    dma = pltpu.SemaphoreType.DMA
    return pl.pallas_call(
        entry_kernel,
        out_shape=(
            jax.ShapeDtypeStruct((own, width), F32),
            jax.ShapeDtypeStruct((group, width), BF),
            tile,
            tile,
            tile,
            jax.ShapeDtypeStruct((group, LANES), BF),
            tile,
            jax.ShapeDtypeStruct((2, width), F32),
            jax.ShapeDtypeStruct((4 * w_out.shape[0], w_out.shape[1]), BF),
        ),
        in_specs=[SM] + [VM] * 9,
        out_specs=(VM, pl.BlockSpec(memory_space=pl.ANY), VM, VM, VM, VM, VM, VM, VM),
        scratch_shapes=[
            pltpu.VMEM((group, width), BF),
            pltpu.VMEM((4, 8, width), F32),
            pltpu.VMEM((n_dp, 8, width), F32),
            pltpu.VMEM((heads, LANES, LANES), BF),
            pltpu.VMEM((heads, LANES, LANES), BF),
            dma((3,)),
            dma((3,)),
            dma((n_dp,)),
            dma((n_dp,)),
            dma((3, pieces)),
            dma((3, pieces)),
            dma((3,)),
            dma((3,)),
            dma,
        ],
        compiler_params=pltpu.CompilerParams(
            collective_id=0, has_side_effects=True, vmem_limit_bytes=VMEM_CAP
        ),
        name="entry",
    )(
        lengths,
        tokens,
        box_cells,
        bn_gain,
        bn_shift,
        w,
        b_qv,
        tab_pos,
        tab_box,
        w_out,
    )


def attend_kernel(
    len_ref, q0_ref, q1_ref, k0_ref, k1_ref, vx_ref, o_ref, q1b_ref, s_scr, m_scr, acc
):
    heads, group = q0_ref.shape[0], q0_ref.shape[1]
    lens = [len_ref[0, d] for d in range(len_ref.shape[1])]
    lane = iota((BLK, LANES), 1)

    def block(qb, carry):
        low, high = block_window(qb, lens, group)
        at = pl.ds(pl.multiple_of(qb * BLK, BLK), BLK)
        m_scr[...] = jnp.full_like(m_scr, -2.0 * BIG)
        acc[...] = jnp.zeros_like(acc)

        def score(kb, c):
            ks = pl.ds(pl.multiple_of(kb * BLK, BLK), BLK)
            for h in range(heads):
                qa = jnp.concatenate([q0_ref[h, at], q1_ref[h, at]], axis=1)
                ka = jnp.concatenate([k0_ref[h, ks], k1_ref[ks]], axis=1)
                s = mm_nt(qa, ka)
                s_scr[h, kb] = s
                m_scr[h] = jnp.maximum(m_scr[h], jnp.maximum(s[:, :LANES], s[:, LANES:]))
            return c

        lax.fori_loop(low, high, score, 0)
        for h in range(heads):
            m_scr[h] = jnp.broadcast_to(
                jnp.max(m_scr[h], axis=1, keepdims=True), (BLK, LANES)
            )

        def weigh(kb, c):
            ks = pl.ds(pl.multiple_of(kb * BLK, BLK), BLK)
            for h in range(heads):
                m = m_scr[h]
                p = jnp.exp(s_scr[h, kb] - jnp.concatenate([m, m], axis=1)).astype(BF)
                acc[h] += mm(p, vx_ref[h, ks])
            return c

        lax.fori_loop(low, high, weigh, 0)
        for h in range(heads):
            a = acc[h]
            turned = pltpu.roll(a, DH, 1)
            o_ref[at, h * DH : (h + 1) * DH] = (a / turned)[:, :DH].astype(BF)
            total = jnp.where(lane < DH, turned, a)
            rest = -(m_scr[h] + jnp.log(total))
            tile = q1_ref[h, at].astype(F32)
            for i in range(3):
                part = rest.astype(BF).astype(F32)
                tile = jnp.where(lane == LSE0 + i, part, tile)
                rest = rest - part
            q1b_ref[h, at] = tile.astype(BF)
        return carry

    lax.fori_loop(0, group // BLK, block, 0)


def attend(lengths, q0, q1, k0, k1, vx):
    heads, group, _ = q0.shape
    return pl.pallas_call(
        attend_kernel,
        out_shape=(
            jax.ShapeDtypeStruct((group, heads * DH), BF),
            jax.ShapeDtypeStruct(q1.shape, BF),
        ),
        in_specs=[SM] + [VM] * 5,
        out_specs=(VM, VM),
        scratch_shapes=[
            pltpu.VMEM((heads, group // BLK, BLK, BLK), F32),
            pltpu.VMEM((heads, BLK, LANES), F32),
            pltpu.VMEM((heads, BLK, LANES), F32),
        ],
        compiler_params=pltpu.CompilerParams(vmem_limit_bytes=VMEM_CAP),
        name="attend",
    )(lengths, q0, q1, k0, k1, vx)


C_TAIL = 0.23
TAIL = (
    -2.7761570891016163e-05,
    0.09237844496965408,
    0.08576294034719467,
    0.1195140853524208,
    -0.032920535653829575,
    0.30147361755371094,
    -0.2781279683113098,
    0.2904147207736969,
    -0.07846760004758835,
)


def gelu_pair(v):
    a = jnp.abs(v)
    t = 1.0 / (1.0 + C_TAIL * a)
    g = jnp.full_like(v, TAIL[-1])
    for c in TAIL[-2::-1]:
        g = g * t + c
    e = jnp.exp(v * v * -0.5)
    tail = g * e
    phi = jnp.where(v > 0.0, 1.0 - tail, tail)
    return v * phi, phi + v * (e * 0.3989422804014327)


def row_stats(h):
    scale = 1.0 / h.shape[1]
    centred = h - jnp.sum(h, axis=1, keepdims=True) * scale
    rstd = lax.rsqrt(jnp.sum(centred * centred, axis=1, keepdims=True) * scale + NORM_EPS)
    return centred * rstd, rstd


def norm_back(grad, normed, rstd):
    scale = 1.0 / grad.shape[1]
    mean = jnp.sum(grad, axis=1, keepdims=True) * scale
    along = jnp.sum(grad * normed, axis=1, keepdims=True) * scale
    return rstd * (grad - mean - normed * along)


def add_row(ref, i, v):
    ref[i : i + 1] += jnp.sum(v, axis=0, keepdims=True)


def outer_sum(out_ref, a_ref, b_ref, rows):
    def step(m, c):
        cols = pl.ds(pl.multiple_of(m * BLK, BLK), BLK)
        out_ref[cols] = mm_tn(a_ref[0:rows, cols], b_ref[0:rows])
        return c

    lax.fori_loop(0, out_ref.shape[0] // BLK, step, 0)


class Exchange:
    def __init__(self, own, piece):
        self.own, self.piece, self.pieces = own, piece, own // piece
        self.hd, self.sib, self.cross, self.diag = head_peers()

    def rows(self, source, s, base=0):
        return pl.ds(pl.multiple_of(source * self.own + s * self.piece, self.piece), self.piece)

    def send(self, src, dst, sems, i, s, peer):
        return pltpu.make_async_remote_copy(
            src_ref=src,
            dst_ref=dst,
            send_sem=sems.at[0, i, s],
            recv_sem=sems.at[1, i, s],
            device_id={"head": peer},
            device_id_type=MESH,
        )

    def gather(self, buf, sems, i, s):
        source = self.cross if i == 2 else self.hd
        at = self.rows(source, s)
        return self.send(buf.at[at], buf.at[at], sems, i, s, self.cross if i == 0 else self.sib)

    def gather_from(self, buf, sems, i, s):
        source = (self.cross, self.sib, self.diag)[i]
        at = self.rows(source, s)
        return self.send(buf.at[at], buf.at[at], sems, i, s, self.cross if i == 0 else self.sib)

    def partial(self, snd, rcv, sems, i, s):
        return self.send(
            snd.at[i, s], rcv.at[i, s], sems, i, s, self.cross if i == 2 else self.sib
        )


def middle_kernel(
    attn_ref,
    xin_ref,
    cot_ref,
    wo_ref,
    wu_ref,
    wd_ref,
    bo_ref,
    g1_ref,
    s1_ref,
    bu_ref,
    bd_ref,
    g2_ref,
    s2_ref,
    out_ref,
    gone_ref,
    ga_ref,
    gwo_ref,
    dtot_ref,
    usum_ref,
    sums_ref,
    gbu_ref,
    abuf,
    full,
    fin,
    gl,
    gd,
    fgr,
    gpre,
    xh1,
    rs1,
    two,
    ownp,
    crossp,
    snd1,
    rcv1,
    snd2,
    rcv2,
    asems,
    f1sems,
    r1sems,
    f2sems,
    r2sems,
    gsems,
    dsnd,
    drcv,
    dpsnd,
    dprcv,
    dmine,
    dsems,
    dpsems,
    usnd,
    urcv,
    usems,
):
    own, width = xin_ref.shape
    hcols = attn_ref.shape[1]
    piece = own // asems.shape[2]
    ex = Exchange(own, piece)
    hd, sib, cross, diag = ex.hd, ex.sib, ex.cross, ex.diag
    peers = (cross, diag, sib)
    members, part = usum_ref.shape[0], usum_ref.shape[1]
    head_and_dp_barrier(2 * members)()

    def own_at(s):
        return pl.ds(pl.multiple_of(s * piece, piece), piece)

    def acopy(s, i):
        at = ex.rows(peers[i], s)
        return ex.send(attn_ref.at[at], abuf.at[hd, own_at(s)], asems, i, s, peers[i])

    def afrom(s, i):
        return ex.send(
            attn_ref.at[own_at(s)], abuf.at[peers[i], own_at(s)], asems, i, s, peers[i]
        )

    def all_sends(s, c):
        for i in range(3):
            acopy(s, i).start()
        return c

    lax.fori_loop(0, ex.pieces, all_sends, 0)
    abuf[hd] = attn_ref[pl.ds(pl.multiple_of(hd * own, own), own)]
    sums_ref[...] = jnp.zeros_like(sums_ref)
    gbu_ref[...] = jnp.zeros_like(gbu_ref)

    def first_norm(s, c):
        at = own_at(s)
        for i in range(3):
            afrom(s, i).wait_recv()
        for source in range(4):
            full[at, source * hcols : (source + 1) * hcols] = abuf[source, at]
        h = xin_ref[at] + (mm(full[at], wo_ref[...]) + row(bo_ref))
        normed, rstd = row_stats(h)
        xh1[at] = normed
        rs1[at] = jnp.broadcast_to(rstd, (piece, LANES))
        fin[ex.rows(hd, s)] = (normed * row(g1_ref) + row(s1_ref)).astype(BF)
        ex.gather(fin, f1sems, 0, s).start()
        ex.gather(fin, f1sems, 1, s).start()
        return c

    lax.fori_loop(0, ex.pieces, first_norm, 0)

    def pipeline(buf, fsems, snd, rcv, rsems, compute):
        def near(s):
            ex.gather_from(buf, fsems, 1, s).wait_recv()
            part = compute(ex.rows(hd, s), ex.rows(sib, s))
            ownp[own_at(s)] = part[:piece]
            snd[0, s] = part[piece:].astype(BF)
            ex.partial(snd, rcv, rsems, 0, s).start()

        def far(s):
            ex.gather_from(buf, fsems, 2, s).wait_recv()
            part = compute(ex.rows(cross, s), ex.rows(diag, s))
            crossp[own_at(s)] = part[:piece]
            snd[1, s] = part[piece:].astype(BF)
            ex.partial(snd, rcv, rsems, 1, s).start()

        def combine(s):
            ex.partial(snd, rcv, rsems, 1, s).wait_recv()
            snd[2, s] = (crossp[own_at(s)] + rcv[1, s].astype(F32)).astype(BF)
            ex.partial(snd, rcv, rsems, 2, s).start()

        def step(s, c):
            @pl.when(s >= 2)
            def _():
                combine(s - 2)

            @pl.when(s < ex.pieces)
            def _():
                near(s)
                ex.gather_from(buf, fsems, 0, s).wait_recv()
                ex.gather(buf, fsems, 2, s).start()

            @pl.when((s >= 1) & (s <= ex.pieces))
            def _():
                far(s - 1)

            return c

        lax.fori_loop(0, ex.pieces + 2, step, 0)

    def collected(rcv, rsems, snd, s):
        ex.partial(snd, rcv, rsems, 0, s).wait_recv()
        ex.partial(snd, rcv, rsems, 2, s).wait_recv()
        return ownp[own_at(s)] + rcv[0, s].astype(F32) + rcv[2, s].astype(F32)

    def forward(at_a, at_b):
        x = jnp.concatenate([fin[at_a], fin[at_b]], axis=0)
        value, slope = gelu_pair(mm(x, wu_ref[...]) + row(bu_ref))
        low = value.astype(BF)
        gl[at_a] = low[:piece]
        gl[at_b] = low[piece:]
        gd[at_a] = slope[:piece]
        gd[at_b] = slope[piece:]
        return mm(low, wd_ref[...])

    pipeline(fin, f1sems, snd1, rcv1, r1sems, forward)

    def second_norm(s, c):
        at = own_at(s)
        mid = xh1[at] * row(g1_ref) + row(s1_ref)
        h = mid + (collected(rcv1, r1sems, snd1, s) + row(bd_ref))
        normed, rstd = row_stats(h)
        out_ref[at] = (normed * row(g2_ref) + row(s2_ref)).astype(BF)
        cot = cot_ref[at].astype(F32)
        add_row(sums_ref, 2, cot * normed)
        add_row(sums_ref, 3, cot)
        grad = norm_back(cot * row(g2_ref), normed, rstd)
        two[at] = grad
        add_row(sums_ref, 5, grad)
        fgr[ex.rows(hd, s)] = grad.astype(BF)
        ex.gather(fgr, f2sems, 0, s).start()
        ex.gather(fgr, f2sems, 1, s).start()
        return c

    lax.fori_loop(0, ex.pieces, second_norm, 0)

    def backward(at_a, at_b):
        x = jnp.concatenate([fgr[at_a], fgr[at_b]], axis=0)
        slope = jnp.concatenate([gd[at_a], gd[at_b]], axis=0)
        low = (mm_nt(x, wd_ref[...]) * slope).astype(BF)
        gpre[at_a] = low[:piece]
        gpre[at_b] = low[piece:]
        add_row(gbu_ref, 0, low.astype(F32))
        return mm_nt(low, wu_ref[...])

    pipeline(fgr, f2sems, snd2, rcv2, r2sems, backward)
    gwd, gwu = gd.at[0:width], gd.at[width : 2 * width]
    outer_sum(gwd, gl, fgr, gl.shape[0])
    down = Reduce(
        members,
        part,
        dict(snd=dsnd, rcv=drcv, psnd=dpsnd, prcv=dprcv, mine=dmine, sems=dsems, psems=dpsems),
        gwd,
    )
    up = Reduce(members, part, dict(snd=usnd, rcv=urcv, sems=usems), gwu)
    down.start()

    def gcopy(s, i, source):
        return ex.send(
            abuf.at[peers[i], own_at(s)], ga_ref.at[ex.rows(source, s)], gsems, i, s, peers[i]
        )

    for i in range(3):
        for s in range(ex.pieces):
            acopy(s, i).wait_send()

    def last_norm(s, c):
        at = own_at(s)
        grad = two[at] + collected(rcv2, r2sems, snd2, s)
        normed = xh1[at]
        add_row(sums_ref, 0, grad * normed)
        add_row(sums_ref, 1, grad)
        one = norm_back(grad * row(g1_ref), normed, rs1[at][:, 0:1])
        gone_ref[at] = one
        add_row(sums_ref, 4, one)
        low = one.astype(BF)
        fin[at] = low
        heads = mm_nt(low, wo_ref[...]).astype(BF)
        for source in range(4):
            abuf[source, at] = heads[:, source * hcols : (source + 1) * hcols]
        for i in range(3):
            gcopy(s, i, hd).start()
        return c

    for s in range(ex.pieces):
        for i in range(3):
            ex.gather(fin, f1sems, i, s).wait_send()
    outer_sum(gwu, fin, gpre, fin.shape[0])
    up.start()
    lax.fori_loop(0, ex.pieces, last_norm, 0)
    ga_ref[pl.ds(pl.multiple_of(hd * own, own), own)] = abuf[hd]
    down.spread()
    outer_sum(gwo_ref, full, fin, own)
    up.collect(usum_ref)
    down.gather()
    dtot_ref[...] = dmine[...].astype(BF)
    down.sent()
    for s in range(ex.pieces):
        for i in range(3):
            gcopy(s, i, peers[i]).wait()
            ex.partial(snd1, rcv1, r1sems, i, s).wait_send()
            ex.gather(fgr, f2sems, i, s).wait_send()
            ex.partial(snd2, rcv2, r2sems, i, s).wait_send()


def middle(attn, x_in, cotangent, w_out, w_up, w_down, vectors, n_dp):
    own, width = x_in.shape
    group, hcols = attn.shape
    hidden = w_up.shape[1]
    pieces = 4
    piece = own // pieces
    dma = pltpu.SemaphoreType.DMA
    exchange = pltpu.VMEM((3, pieces, piece, width), BF)
    members, part = n_dp // 2, width // n_dp
    parts = pltpu.VMEM((members, part, width), BF)
    return pl.pallas_call(
        middle_kernel,
        out_shape=(
            jax.ShapeDtypeStruct((own, width), BF),
            jax.ShapeDtypeStruct((own, width), F32),
            jax.ShapeDtypeStruct((group, hcols), BF),
            jax.ShapeDtypeStruct((4 * hcols, width), F32),
            jax.ShapeDtypeStruct((part, width), BF),
            jax.ShapeDtypeStruct((members, part, width), F32),
            jax.ShapeDtypeStruct((8, width), F32),
            jax.ShapeDtypeStruct((1, hidden), F32),
        ),
        in_specs=[VM] * 13,
        out_specs=(VM,) * 8,
        scratch_shapes=[
            pltpu.VMEM((4, own, hcols), BF),
            pltpu.VMEM((own, 4 * hcols), BF),
            pltpu.VMEM((group, width), BF),
            pltpu.VMEM((group, hidden), BF),
            pltpu.VMEM((group, hidden), F32),
            pltpu.VMEM((group, width), BF),
            pltpu.VMEM((group, hidden), BF),
            pltpu.VMEM((own, width), F32),
            pltpu.VMEM((own, LANES), F32),
            pltpu.VMEM((own, width), F32),
            pltpu.VMEM((own, width), F32),
            pltpu.VMEM((own, width), F32),
            exchange,
            exchange,
            exchange,
            exchange,
        ]
        + [dma((2, 3, pieces))] * 6
        + [parts] * 4
        + [pltpu.VMEM((part, width), F32), dma((2, 2)), dma((2, 2, members))]
        + [parts] * 2
        + [dma((2, 2))],
        compiler_params=pltpu.CompilerParams(
            collective_id=1, has_side_effects=True, vmem_limit_bytes=VMEM_CAP
        ),
        name="middle",
    )(attn, x_in, cotangent, w_out, w_up, w_down, *vectors)


def attend_back_kernel(
    len_ref,
    q0_ref,
    q1_ref,
    k0_ref,
    k1_ref,
    vx_ref,
    o_ref,
    go_ref,
    dqkv_ref,
    gt_ref,
    dox,
    kacc,
    vacc,
    qacc,
    k0t,
    k1t,
    map0,
    map1,
    pbuf,
    dbuf,
    pairs,
):
    heads, group = q0_ref.shape[0], q0_ref.shape[1]
    width = heads * DH
    lens = [len_ref[0, d] for d in range(len_ref.shape[1])]
    lane = iota((BLK, LANES), 1)
    spread = (
        iota((width, heads * LANES), 0) // DH == iota((width, heads * LANES), 1) // LANES
    ).astype(F32).astype(BF)
    map0[...] = jnp.zeros_like(map0)
    map1[...] = jnp.zeros_like(map1)
    kacc[...] = jnp.zeros_like(kacc)
    vacc[...] = jnp.zeros_like(vacc)
    qacc[...] = jnp.zeros_like(qacc)

    def prepare(qb, carry):
        at = pl.ds(pl.multiple_of(qb * BLK, BLK), BLK)
        g = go_ref[at].astype(F32)
        e = g * o_ref[at].astype(F32)
        e_high = e.astype(BF)
        e_low = (e - e_high.astype(F32)).astype(BF)
        dots = mm(e_high, spread) + mm(e_low, spread)
        for h in range(heads):
            rest = -dots[:, h * LANES : (h + 1) * LANES]
            tile = jnp.where(
                lane < DH,
                jnp.concatenate([g[:, h * DH : (h + 1) * DH], jnp.zeros((BLK, DH), F32)], axis=1),
                0.0,
            )
            for i in range(3):
                part = rest.astype(BF).astype(F32)
                tile = jnp.where(lane == DH + i, part, tile)
                rest = rest - part
            dox[h, at] = tile.astype(BF)
        return carry

    lax.fori_loop(0, group // BLK, prepare, 0)

    def turn(kb, carry):
        at = pl.ds(pl.multiple_of(kb * BLK, BLK), BLK)
        k1t[:, at] = k1_ref[at].T
        for h in range(heads):
            k0t[h, :, at] = k0_ref[h, at].T
        return carry

    lax.fori_loop(0, group // BLK, turn, 0)

    def list_block(qb, n):
        low, high = block_window(qb, lens, group)

        def add(kb, m):
            pairs[0, m] = qb
            pairs[1, m] = kb
            return m + 1

        return lax.fori_loop(low, high, add, n)

    count = lax.fori_loop(0, group // BLK, list_block, 0)
    hs = range(heads)

    def spots(i):
        return (
            pl.ds(pl.multiple_of(pairs[0, i] * BLK, BLK), BLK),
            pl.ds(pl.multiple_of(pairs[1, i] * BLK, BLK), BLK),
        )

    def weigh(i, slot):
        at, ks = spots(i)
        kf = k1_ref[ks]
        st = [
            mm_nt(
                jnp.concatenate([k0_ref[h, ks], kf], axis=1),
                jnp.concatenate([q0_ref[h, at], q1_ref[h, at]], axis=1),
            )
            for h in hs
        ]
        dp = [mm_nt(vx_ref[h, ks], dox[h, at]) for h in hs]
        p = [jnp.exp(st[h]) for h in hs]
        for h in hs:
            pbuf[slot, h] = p[h].astype(BF)
            dbuf[slot, h] = (p[h] * dp[h]).astype(BF)

    def gather(i, slot):
        at, ks = spots(i)
        qb = pairs[0, i]
        for h in hs:
            vacc[h, ks] += mm(pbuf[slot, h], dox[h, at])
        for h in hs:
            kacc[h, ks] += mm(dbuf[slot, h], q0_ref[h, at])
        kt = k1t[:, ks]
        for h in hs:
            qacc[qb, h] += mm(jnp.concatenate([k0t[h, :, ks], kt], axis=0), dbuf[slot, h])

    weigh(0, 0)

    def pair(i, carry):
        gather(i - 1, lax.rem(i - 1, 2))
        weigh(jnp.minimum(i, count - 1), lax.rem(i, 2))
        return carry

    lax.fori_loop(1, count + 1, pair, 0)

    def block(qb, carry):
        at = pl.ds(pl.multiple_of(qb * BLK, BLK), BLK)
        for h in range(heads):
            a = qacc[qb, h]
            dqkv_ref[at, h * DH : (h + 1) * DH] = (a[:LANES].T[:, :DH] * 0.125).astype(BF)
            high_part = a.astype(BF)
            low_part = (a - high_part.astype(F32)).astype(BF)
            for m, hot, rows in (
                (map0, k0_ref[h, at], slice(0, LANES)),
                (map1, k1_ref[at], slice(LANES, 2 * LANES)),
            ):
                m[h] += mm(jnp.concatenate([high_part[rows], low_part[rows]], axis=0), hot)
        return carry

    lax.fori_loop(0, group // BLK, block, 0)

    def finish(kb, carry):
        at = pl.ds(pl.multiple_of(kb * BLK, BLK), BLK)
        for h in range(heads):
            k_at, v_at = width + h * DH, 2 * width + h * DH
            dqkv_ref[at, k_at : k_at + DH] = kacc[h, at][:, :DH].astype(BF)
            dqkv_ref[at, v_at : v_at + DH] = vacc[h, at][:, :DH].astype(BF)
        return carry

    lax.fori_loop(0, group // BLK, finish, 0)

    gt_ref[...] = jnp.zeros_like(gt_ref)
    r_i, l_i = iota((LANES, LANES), 0), iota((LANES, LANES), 1)

    def exact(a, b):
        return jnp.dot(a, b, precision=lax.Precision.HIGHEST, preferred_element_type=F32)

    def diagonals(block, base, count):
        inside = (r_i >= base) & (r_i < base + count) & (l_i >= base) & (l_i < base + count)
        flip = ((l_i == base + count - 1 - r_i) & (l_i < count)).astype(F32)
        turned = exact(jnp.where(inside, block, 0.0), flip)
        moved = pltpu.roll(turned, (64 - base - count) % LANES, 1, stride=1, stride_axis=0)
        return jnp.sum(moved, axis=0, keepdims=True)

    def fold(block, base, count):
        sums = jnp.broadcast_to(diagonals(block, base, count), (8, LANES))
        j_i, t_i = iota((LANES, count), 0), iota((LANES, count), 1)
        low = 63 - count // 2
        pick = (t_i == jnp.clip(j_i - low, 0, count - 1)).astype(F32)
        return exact(sums, pick)[0:1]

    for h in range(heads):
        one = map1[h][:LANES] + map1[h][LANES:]
        zero = map0[h][:LANES] + map0[h][LANES:]
        gt_ref[h : h + 1, 0:POSB] = fold(one, 64, POSB)
        gt_ref[heads + h : heads + h + 1, 0:BOXB] = fold(one, 0, BOXB)
        gt_ref[2 * heads + h : 2 * heads + h + 1, 0:BOXB] = fold(zero, 64, BOXB)


def attend_back(lengths, q0, q1, k0, k1, vx, out, grad_out):
    heads, group, _ = q0.shape
    return pl.pallas_call(
        attend_back_kernel,
        out_shape=(
            jax.ShapeDtypeStruct((group, 3 * heads * DH), BF),
            jax.ShapeDtypeStruct((16, LANES), F32),
        ),
        in_specs=[SM] + [VM] * 7,
        out_specs=(VM,) * 2,
        scratch_shapes=[
            pltpu.VMEM((heads, group, LANES), BF),
            pltpu.VMEM((heads, group, LANES), F32),
            pltpu.VMEM((heads, group, LANES), F32),
            pltpu.VMEM((group // BLK, heads, 2 * LANES, BLK), F32),
            pltpu.VMEM((heads, LANES, group), BF),
            pltpu.VMEM((LANES, group), BF),
            pltpu.VMEM((heads, 2 * LANES, LANES), F32),
            pltpu.VMEM((heads, 2 * LANES, LANES), F32),
            pltpu.VMEM((2, heads, BLK, BLK), BF),
            pltpu.VMEM((2, heads, BLK, BLK), BF),
            pltpu.SMEM((2, (group // BLK) ** 2), I32),
        ],
        compiler_params=pltpu.CompilerParams(vmem_limit_bytes=VMEM_CAP),
        name="attend_back",
    )(lengths, q0, q1, k0, k1, vx, out, grad_out)


def final_kernel(
    len_ref,
    dqkv_ref,
    w_ref,
    a_ref,
    tok_ref,
    st_ref,
    gone_ref,
    dtot_ref,
    usum_ref,
    gwo_ref,
    sums_ref,
    gbu_ref,
    gt_ref,
    gin_ref,
    tot_ref,
    wd_ref,
    wu_ref,
    wq_ref,
    mixed,
    ownp,
    crossp,
    snd,
    rcv,
    osnd,
    orcv,
    hbuf,
    dbuf,
    rsems,
    osems,
    hsems,
    dsems,
    dhalf,
    dother,
    dpair,
    dpart,
    upsnd,
    uprcv,
    uhalf,
    uother,
    umine,
    upair,
    upart,
    *qrefs,
):
    own, width = gone_ref.shape
    qcols = dqkv_ref.shape[1]
    hcols = qcols // 3
    n_dp = dbuf.shape[0]
    members = n_dp // 2
    pieces = rsems.shape[2]
    piece = own // pieces
    ex = Exchange(own, piece)
    hd, sib, cross, diag = ex.hd, ex.sib, ex.cross, ex.diag
    dp = lax.axis_index("dp")
    head_and_dp_barrier(n_dp)()

    down = Reduce(
        members, width // n_dp, dict(half=dhalf, other=dother, sems=dpair, psems=dpart)
    )
    up = Reduce(
        members,
        width // n_dp,
        dict(psnd=upsnd, prcv=uprcv, half=uhalf, other=uother, mine=umine, sems=upair, psems=upart),
    )
    names = ("snd", "rcv", "psnd", "prcv", "half", "other", "mine", "sems", "psems")
    chunks = [
        Reduce(
            members,
            BLK // n_dp,
            dict(zip(names, qrefs[m * len(names) : (m + 1) * len(names)])),
            mixed,
            m * BLK,
        )
        for m in range(3)
    ]
    down.publish(dtot_ref[...])
    up.spread(usum_ref)

    def own_at(s):
        return pl.ds(pl.multiple_of(s * piece, piece), piece)

    def block_of(source):
        return pl.ds(pl.multiple_of(source * hcols, DH), hcols)

    def osend(i):
        return ex.send(osnd.at[i], orcv.at[i], osems, i, 0, cross if i == 2 else sib)

    osnd[1] = gwo_ref[block_of(diag)].astype(BF)
    osend(1).start()
    osnd[0] = gwo_ref[block_of(sib)].astype(BF)
    osend(0).start()

    for m in range(3):
        cols = slice(m * BLK, min((m + 1) * BLK, qcols))
        mixed[cols] = mm_tn(dqkv_ref[:, cols], a_ref[...])
        if m < 2:
            chunks[m].start()
    osend(1).wait_recv()
    osnd[2] = (gwo_ref[block_of(cross)] + orcv[1].astype(F32)).astype(BF)
    osend(2).start()

    def grad_rows(at):
        return mm(dqkv_ref[at], w_ref[...])

    def far(s, c):
        snd[1, s] = grad_rows(ex.rows(diag, s)).astype(BF)
        ex.partial(snd, rcv, rsems, 1, s).start()
        crossp[own_at(s)] = grad_rows(ex.rows(cross, s))

        @pl.when(s >= 1)
        def _():
            mix(s - 1)

        return c

    def mix(s):
        ex.partial(snd, rcv, rsems, 1, s).wait_recv()
        snd[2, s] = (crossp[own_at(s)] + rcv[1, s].astype(F32)).astype(BF)
        ex.partial(snd, rcv, rsems, 2, s).start()

    def near(s, c):
        snd[0, s] = grad_rows(ex.rows(sib, s)).astype(BF)
        ex.partial(snd, rcv, rsems, 0, s).start()
        ownp[own_at(s)] = grad_rows(ex.rows(hd, s))
        return c

    lax.fori_loop(0, pieces, far, 0)
    mix(pieces - 1)
    osend(0).wait_recv()
    osend(2).wait_recv()
    mixed[qcols:] = gwo_ref[block_of(hd)] + orcv[0].astype(F32) + orcv[2].astype(F32)
    chunks[2].start()
    lax.fori_loop(0, pieces, near, 0)
    chunks[0].spread()
    chunks[1].spread()

    dbuf[dp, 8:] = jnp.zeros((8, width), F32)
    dbuf[dp, 8:9] = gbu_ref[...]
    for b in range(9):
        dbuf[dp, 10 + b // 6 : 11 + b // 6, (b % 6) * LANES : (b % 6 + 1) * LANES] = gt_ref[
            b : b + 1
        ]

    def col_sums(s, c):
        at = pl.ds(pl.multiple_of(s * BLK, BLK), BLK)
        dbuf[dp, 9:10, 0:qcols] += jnp.sum(dqkv_ref[at].astype(F32), axis=0, keepdims=True)
        return c

    lax.fori_loop(0, dqkv_ref.shape[0] // BLK, col_sums, 0)
    chunks[2].spread()

    lens = [len_ref[0, d] for d in range(len_ref.shape[1])]
    mean, inv_std = st_ref[0:1], st_ref[1:2]
    hbuf[hd] = sums_ref[...]

    def grad_own(s, c):
        at = own_at(s)
        ex.partial(snd, rcv, rsems, 0, s).wait_recv()
        ex.partial(snd, rcv, rsems, 2, s).wait_recv()
        g = gone_ref[at] + (ownp[at] + rcv[0, s].astype(F32) + rcv[2, s].astype(F32))
        gin_ref[at] = g
        _, visual, _ = row_layout(iota((piece, LANES), 0) + (hd * own + s * piece), lens)
        g = jnp.where(visual[:, 0:1], g, 0.0)
        x_hat = (tok_ref[at].astype(F32) - mean) * inv_std
        hbuf[hd, 6:7] += jnp.sum(g, axis=0, keepdims=True)
        hbuf[hd, 7:8] += jnp.sum(g * x_hat, axis=0, keepdims=True)
        return c

    lax.fori_loop(0, pieces, grad_own, 0)
    hcopies = [
        ex.send(hbuf.at[hd], hbuf.at[hd], hsems, i, 0, peer)
        for i, peer in enumerate((sib, cross, diag))
    ]
    for copy in hcopies:
        copy.start()
    down.share()
    for copy in hcopies:
        copy.wait()
    dbuf[dp, 0:8] = ((hbuf[0] + hbuf[1]) + hbuf[2]) + hbuf[3]

    def dcopy(j):
        return pltpu.make_async_remote_copy(
            src_ref=dbuf.at[dp],
            dst_ref=dbuf.at[dp],
            send_sem=dsems.at[0, j],
            recv_sem=dsems.at[1, j],
            device_id={"dp": lax.rem(dp + j, n_dp)},
            device_id_type=MESH,
        )

    def dstart(j, carry):
        dcopy(j).start()
        return carry

    def dwait(j, carry):
        dcopy(j).wait()
        return carry

    lax.fori_loop(1, n_dp, dstart, 0)
    for chunk in chunks:
        chunk.gather()
        chunk.publish()
    up.gather()
    up.publish()
    lax.fori_loop(1, n_dp, dwait, 0)

    def dsum(j, total):
        return total + dbuf[j]

    tot_ref[...] = lax.fori_loop(1, n_dp, dsum, dbuf[0])
    for chunk in chunks:
        chunk.share()
    up.share()
    down.finish(wd_ref)
    for m, chunk in enumerate(chunks):
        chunk.finish(wq_ref, m * BLK)
        chunk.sent()
    up.finish(wu_ref)
    up.sent()
    for i in range(3):
        osend(i).wait_send()
        for s in range(pieces):
            ex.partial(snd, rcv, rsems, i, s).wait_send()


def final(lengths, dqkv, w, attn_in, tokens, stats, gone, dtot, usum, gwo, sums, gbu, gt, n_dp):
    own, width = gone.shape
    hcols = dqkv.shape[1] // 3
    pieces = 4
    members, part = n_dp // 2, width // n_dp
    dma = pltpu.SemaphoreType.DMA
    exchange = pltpu.VMEM((3, pieces, own // pieces, width), BF)
    small = pltpu.VMEM((3, hcols, width), BF)
    parts = pltpu.VMEM((members, part, width), BF)
    bits = pltpu.VMEM((members, BLK // n_dp, width), BF)
    sems = [dma((2, 2)), dma((2, 2, members))]
    square = jax.ShapeDtypeStruct((width, width), BF)
    return pl.pallas_call(
        final_kernel,
        out_shape=(
            jax.ShapeDtypeStruct((own, width), F32),
            jax.ShapeDtypeStruct((16, width), F32),
            square,
            square,
            square,
        ),
        in_specs=[SM] + [VM] * 12,
        out_specs=(VM,) * 5,
        scratch_shapes=[
            pltpu.VMEM((width, width), F32),
            pltpu.VMEM((own, width), F32),
            pltpu.VMEM((own, width), F32),
            exchange,
            exchange,
            small,
            small,
            pltpu.VMEM((4, 8, width), F32),
            pltpu.VMEM((n_dp, 16, width), F32),
            dma((2, 3, pieces)),
            dma((2, 3, 1)),
            dma((2, 3, 1)),
            dma((2, n_dp)),
        ]
        + [parts, parts]
        + sems
        + [parts] * 4
        + [pltpu.VMEM((part, width), F32)]
        + sems
        + ([bits] * 6 + [pltpu.VMEM((BLK // n_dp, width), F32)] + sems) * 3,
        compiler_params=pltpu.CompilerParams(
            collective_id=2, has_side_effects=True, vmem_limit_bytes=VMEM_CAP
        ),
        name="final",
    )(lengths, dqkv, w, attn_in, tokens, stats, gone, dtot, usum, gwo, sums, gbu, gt)


def finish_kernel(
    count,
    len_ref,
    gin_ref,
    tok_ref,
    st_ref,
    tot_ref,
    gain_ref,
    low_ref,
    wd_ref,
    wu_ref,
    wq_ref,
    out_ref,
    gtok_ref,
    bng_ref,
    bns_ref,
    gw_ref,
    gb_ref,
    gp_ref,
    gx_ref,
    gwo_ref,
    bo_ref,
    g1_ref,
    s1_ref,
    gwu_ref,
    gbu_ref,
    gwd_ref,
    bd_ref,
    g2_ref,
    s2_ref,
):
    own, width = gin_ref.shape
    qcols = 3 * gw_ref.shape[1]
    heads = gp_ref.shape[0]
    piece = LANES
    hd = lax.axis_index("head")
    lens = [len_ref[0, d] for d in range(len_ref.shape[1])]
    mean, inv_std = st_ref[0:1], st_ref[1:2]
    gain = row(gain_ref)
    shift_part = tot_ref[6:7] / count
    gain_part = tot_ref[7:8] / count

    def tokens_out(s, c):
        at = pl.ds(pl.multiple_of(s * piece, piece), piece)
        g = gin_ref[at]
        _, visual, _ = row_layout(iota((piece, LANES), 0) + (hd * own + s * piece), lens)
        x_hat = (tok_ref[at].astype(F32) - mean) * inv_std
        normed = inv_std * gain * (g - (shift_part + x_hat * gain_part))
        gtok_ref[at] = jnp.where(visual[:, 0:1], normed, g)
        return c

    lax.fori_loop(0, own // piece, tokens_out, 0)
    out_ref[...] = low_ref[...]
    gwd_ref[...] = wd_ref[...].astype(F32)
    gwu_ref[...] = wu_ref[...].astype(F32)
    for e in range(3):
        at = slice(e * gw_ref.shape[1], (e + 1) * gw_ref.shape[1])
        gw_ref[e] = wq_ref[at].astype(F32)
    gwo_ref[...] = wq_ref[qcols:].astype(F32)
    for ref, i in (
        (g1_ref, 0),
        (s1_ref, 1),
        (g2_ref, 2),
        (s2_ref, 3),
        (bo_ref, 4),
        (bd_ref, 5),
        (bns_ref, 6),
        (bng_ref, 7),
        (gbu_ref, 8),
    ):
        ref[...] = tot_ref[i : i + 1].reshape(width)
    hcols = qcols // 3
    gb_ref[0:1] = tot_ref[9:10, 0:hcols]
    gb_ref[1:2] = tot_ref[9:10, 2 * hcols : qcols]

    def table(b):
        at = (b % 6) * LANES
        return tot_ref[10 + b // 6 : 11 + b // 6, at : at + LANES]

    for h in range(heads):
        gp_ref[h : h + 1] = table(h)[:, :POSB]
        for e in range(2):
            gx_ref[h, e : e + 1] = table((1 + e) * heads + h)[:, :BOXB]


def finish(lengths, gin, tokens, stats, tot, bn_gain, low, wd, wu, wq, heads, n_dp):
    own, width = gin.shape
    hcols = heads * DH
    count = float(VISUAL * lengths.shape[1] * n_dp)
    vector = jax.ShapeDtypeStruct((width,), F32)
    square = jax.ShapeDtypeStruct((width, width), F32)
    return pl.pallas_call(
        functools.partial(finish_kernel, count),
        out_shape=(
            jax.ShapeDtypeStruct((own, width), BF),
            jax.ShapeDtypeStruct((own, width), F32),
            vector,
            vector,
            jax.ShapeDtypeStruct((3, hcols, width), F32),
            jax.ShapeDtypeStruct((2, hcols), F32),
            jax.ShapeDtypeStruct((heads, POSB), F32),
            jax.ShapeDtypeStruct((heads, 2, BOXB), F32),
            jax.ShapeDtypeStruct((hcols, width), F32),
            vector,
            vector,
            vector,
            square,
            vector,
            square,
            vector,
            vector,
            vector,
        ),
        in_specs=[SM] + [VM] * 9,
        out_specs=(VM,) * 18,
        compiler_params=pltpu.CompilerParams(vmem_limit_bytes=VMEM_CAP),
        name="finish",
    )(lengths, gin, tokens, stats, tot, bn_gain, low, wd, wu, wq)


def body(
    n_dp,
    tokens,
    lengths,
    box_cells,
    bn_gain,
    bn_shift,
    query_key_value_weight,
    b_qv,
    tab_pos,
    tab_box,
    w_out,
    b_out,
    ln1_gain,
    ln1_shift,
    w_up,
    b_up,
    w_down,
    b_down,
    ln2_gain,
    ln2_shift,
    cotangent,
):
    width = tokens.shape[1]
    heads = tab_pos.shape[0]
    w_turned = jnp.swapaxes(query_key_value_weight, 1, 2)
    x_in, attn_in, q0, q1, k0, k1, vx, stats, w_out_all = entry(
        tokens,
        lengths,
        box_cells,
        bn_gain,
        bn_shift,
        w_turned,
        b_qv,
        tab_pos,
        jnp.swapaxes(tab_box, 0, 1),
        w_out,
        n_dp,
    )
    attn, q1b = attend(lengths, q0, q1, k0, k1, vx)
    vectors = (b_out, ln1_gain, ln1_shift, b_up, b_down, ln2_gain, ln2_shift)
    low, grad_one, grad_attn, gwo, dtot, usum, sums, gbu = middle(
        attn, x_in, cotangent, w_out_all, w_up, w_down, vectors, n_dp
    )
    dqkv, grad_tables = attend_back(lengths, q0, q1b, k0, k1, vx, attn, grad_attn)
    grad_in, total, wd, wu, wq = final(
        lengths,
        dqkv,
        w_turned.reshape(-1, width),
        attn_in,
        tokens,
        stats,
        grad_one,
        dtot,
        usum,
        gwo,
        sums,
        gbu,
        grad_tables,
        n_dp,
    )
    outs = list(
        finish(lengths, grad_in, tokens, stats, total, bn_gain, low, wd, wu, wq, heads, n_dp)
    )
    outs[4] = jnp.swapaxes(outs[4], 1, 2)
    outs[7] = jnp.swapaxes(outs[7], 0, 1)
    return tuple(outs)


def solution(mesh):
    rows = P(("dp", "head"), None)
    in_specs = (
        rows,
        P("dp", None),
        P(None, "dp"),
        P(),
        P(),
        P(None, None, "head"),
        P(None, "head"),
        P("head", None),
        P(None, "head", None),
        P("head", None),
        P(),
        P(),
        P(),
        P(None, "head"),
        P("head"),
        P("head", None),
        P(),
        P(),
        P(),
        rows,
    )
    out_specs = (
        rows,
        rows,
        P(),
        P(),
        P(None, None, "head"),
        P(None, "head"),
        P("head", None),
        P(None, "head", None),
        P("head", None),
        P(),
        P(),
        P(),
        P(None, "head"),
        P("head"),
        P("head", None),
        P(),
        P(),
        P(),
    )
    return jax.shard_map(
        functools.partial(body, mesh.shape["dp"]),
        mesh=mesh,
        in_specs=in_specs,
        out_specs=out_specs,
        check_vma=False,
    )
```

```python
import functools

import jax
import jax.numpy as jnp
from jax import lax
from jax.experimental import pallas as pl
from jax.experimental.pallas import tpu as pltpu
from jax.sharding import PartitionSpec as P

DH = 64
VISUAL = 49
POSB = 32
BOXB = 64
POS_STEP = 16
NORM_EPS = 1e-05
BATCH_EPS = 1e-05
BIG = float(2.0**100)
BLK = 256
LANES = 128
SEG0 = 96
LSE0 = 112
VMEM_CAP = 58 << 20

MESH = pl.DeviceIdType.MESH
BF = jnp.bfloat16
F32 = jnp.float32
I32 = jnp.int32
VM = pl.BlockSpec(memory_space=pltpu.VMEM)
SM = pl.BlockSpec(memory_space=pltpu.SMEM)
HB = pl.BlockSpec(memory_space=pl.ANY)


def iota(shape, dim):
    return lax.broadcasted_iota(I32, shape, dim)


def mm(a, b):
    return jnp.dot(a, b, preferred_element_type=F32)


def mm_nt(a, b):
    return lax.dot_general(a, b, (((1,), (1,)), ((), ())), preferred_element_type=F32)


def mm_tn(a, b):
    return lax.dot_general(a, b, (((0,), (0,)), ((), ())), preferred_element_type=F32)


def head_peers():
    hd = lax.axis_index("head")
    sib = hd + 1 - 2 * lax.rem(hd, 2)
    cross = lax.rem(hd + 2, 4)
    diag = lax.rem(sib + 2, 4)
    return hd, sib, cross, diag


def row_layout(rows, lens):
    seg = jnp.zeros_like(rows)
    first = jnp.zeros_like(rows)
    end = 0
    for size in lens:
        end = end + size + VISUAL
        past = rows >= end
        seg = seg + past.astype(I32)
        first = jnp.where(past, end, first)
    offset = rows - first
    visual = jnp.logical_and(seg < len(lens), offset < VISUAL)
    position = jnp.where(visual, offset, offset - VISUAL)
    bucket = jnp.minimum(lax.shift_right_logical(jnp.maximum(position, 0), 4), POSB - 1)
    return seg, visual, bucket


def block_window(block, lens, group_rows):
    first, last = block * BLK, block * BLK + BLK - 1
    low, high, end = 0, group_rows, 0
    ends = []
    for size in lens:
        end = end + size + VISUAL
        ends.append(end)
        low = jnp.where(first >= end, end, low)
    for end in reversed(ends):
        high = jnp.where(last < end, end, high)
    return low // BLK, (high + BLK - 1) // BLK


def row(ref):
    return ref[...].reshape(1, ref.shape[0])


def head_and_dp_barrier(n_dp):
    barrier = pltpu.get_barrier_semaphore()
    dp = lax.axis_index("dp")
    for peer in head_peers()[1:]:
        pl.semaphore_signal(barrier, inc=1, device_id={"head": peer}, device_id_type=MESH)

    def greet(j, carry):
        pl.semaphore_signal(
            barrier, inc=1, device_id={"dp": lax.rem(dp + j, n_dp)}, device_id_type=MESH
        )
        return carry

    lax.fori_loop(1, n_dp, greet, 0)
    return lambda: pl.semaphore_wait(barrier, n_dp + 2)


class Reduce:
    def __init__(self, members, part, refs, value=None, base=0):
        self.members, self.part, self.value, self.base = members, part, value, base
        for name, ref in refs.items():
            setattr(self, name, ref)
        dp = lax.axis_index("dp")
        self.bit = lax.rem(dp, 2)
        self.partner = dp + 1 - 2 * self.bit
        self.me = dp // 2

    def at(self, bit, j, base=None):
        base = self.base if base is None else base
        step = self.part
        return pl.ds(pl.multiple_of(base + (bit * self.members + j) * step, 8), step)

    def pair(self, i, src, dst):
        return pltpu.make_async_remote_copy(
            src_ref=src,
            dst_ref=dst,
            send_sem=self.sems.at[0, i],
            recv_sem=self.sems.at[1, i],
            device_id={"dp": self.partner},
            device_id_type=MESH,
        )

    def first(self):
        return self.pair(0, self.snd, self.rcv)

    def fourth(self):
        return self.pair(1, self.half, self.other)

    def member(self, i, k, src, slot):
        target = lax.rem(self.me + k, self.members)
        return pltpu.make_async_remote_copy(
            src_ref=src.at[target] if i == 0 else src.at[self.me],
            dst_ref=slot.at[self.me],
            send_sem=self.psems.at[i, 0, k],
            recv_sem=self.psems.at[i, 1, k],
            device_id={"dp": 2 * target + self.bit},
            device_id_type=MESH,
        )

    def second(self, k):
        return self.member(0, k, self.psnd, self.prcv)

    def third(self, k):
        return self.member(1, k, self.half, self.half)

    def arrived(self, i, k):
        source = lax.rem(self.me - k + self.members, self.members)
        buf = self.prcv if i == 0 else self.half
        return pltpu.make_async_remote_copy(
            src_ref=buf.at[source],
            dst_ref=buf.at[source],
            send_sem=self.psems.at[i, 0, k],
            recv_sem=self.psems.at[i, 1, k],
            device_id={"dp": 2 * source + self.bit},
            device_id_type=MESH,
        )

    def loop(self, low, fn):
        def step(j, c):
            fn(j)
            return c

        lax.fori_loop(low, self.members, step, 0)

    def start(self):
        def fill(j):
            self.snd[j] = self.value[self.at(1 - self.bit, j)].astype(BF)

        self.loop(0, fill)
        self.first().start()

    def halves(self, j):
        return self.value[self.at(self.bit, j)] + self.rcv[j].astype(F32)

    def collect(self, out):
        self.first().wait()

        def keep(j):
            out[j] = self.halves(j)

        self.loop(0, keep)

    def spread(self, sums=None):
        if sums is None:
            self.first().wait()
        take = self.halves if sums is None else (lambda j: sums[j])

        def fill(k):
            j = lax.rem(self.me + k, self.members)
            self.psnd[j] = take(j).astype(BF)
            self.second(k).start()

        self.loop(1, fill)
        self.mine[...] = take(self.me)

    def gather(self):
        def take(k):
            self.arrived(0, k).wait_recv()
            source = lax.rem(self.me - k + self.members, self.members)
            self.mine[...] += self.prcv[source].astype(F32)

        self.loop(1, take)

    def publish(self, total=None):
        self.half[self.me] = self.mine[...].astype(BF) if total is None else total
        self.loop(1, lambda k: self.third(k).start())

    def share(self):
        self.loop(1, lambda k: self.arrived(1, k).wait_recv())
        self.fourth().start()

    def finish(self, out, base=0, moved=False):
        def near(j):
            out[self.at(self.bit, j, base)] = self.half[j]

        def far(j):
            out[self.at(1 - self.bit, j, base)] = self.other[j]

        self.loop(0, near)
        self.fourth().wait()
        self.loop(0, far)
        if not moved:
            self.loop(1, lambda k: self.third(k).wait_send())

    def sent(self):
        self.loop(1, lambda k: self.second(k).wait_send())


def entry_kernel(
    len_ref,
    tok_ref,
    box_ref,
    gain_ref,
    shift_ref,
    w_hbm,
    b_ref,
    tp_ref,
    tb_ref,
    wo_hbm,
    xin_hbm,
    a_hbm,
    q0_hbm,
    q1_hbm,
    k0_hbm,
    k1_hbm,
    vx_hbm,
    st_ref,
    wof_hbm,
    w_ref,
    xin_ref,
    q0_ref,
    q1_ref,
    k0_ref,
    k1_ref,
    vx_ref,
    wof_ref,
    abuf,
    hbuf,
    dbuf,
    map0,
    map1,
    hsend,
    hrecv,
    dsend,
    drecv,
    asend,
    arecv,
    wsend,
    wrecv,
    lsems,
    osems,
    bsems,
):
    n_dp = dbuf.shape[0]
    own = tok_ref.shape[0]
    group = abuf.shape[0]
    docs = len_ref.shape[1]
    heads = w_ref.shape[1] // DH
    hd, sib, cross, diag = head_peers()
    dp = lax.axis_index("dp")
    lens = [len_ref[0, d] for d in range(docs)]
    part = w_ref.shape[1]
    own_part = pl.ds(pl.multiple_of(hd * part, DH), part)
    loads = [
        pltpu.make_async_copy(w_hbm, w_ref, lsems.at[0]),
        pltpu.make_async_copy(wo_hbm, wof_ref.at[own_part], lsems.at[1]),
    ]
    for load in loads:
        load.start()

    barrier = pltpu.get_barrier_semaphore()
    for peer in (sib, cross, diag):
        pl.semaphore_signal(barrier, inc=1, device_id={"head": peer}, device_id_type=MESH)

    def greet(j, carry):
        pl.semaphore_signal(
            barrier, inc=1, device_id={"dp": lax.rem(dp + j, n_dp)}, device_id_type=MESH
        )
        return carry

    lax.fori_loop(1, n_dp, greet, 0)

    rows = iota((own, LANES), 0) + hd * own
    _, visual, _ = row_layout(rows, lens)
    vis_f = visual.astype(F32)
    for c in range(0, tok_ref.shape[1], LANES):
        v = tok_ref[:, c : c + LANES].astype(F32) * vis_f
        hbuf[hd, 0:1, c : c + LANES] = jnp.sum(v, axis=0, keepdims=True)
        hbuf[hd, 1:2, c : c + LANES] = jnp.sum(v * v, axis=0, keepdims=True)
    pl.semaphore_wait(barrier, n_dp + 2)

    def hcopy(i, peer):
        return pltpu.make_async_remote_copy(
            src_ref=hbuf.at[hd],
            dst_ref=hbuf.at[hd],
            send_sem=hsend.at[i],
            recv_sem=hrecv.at[i],
            device_id={"head": peer},
            device_id_type=MESH,
        )

    hcopies = [hcopy(i, peer) for i, peer in enumerate((sib, cross, diag))]
    for copy in hcopies:
        copy.start()


    def wcopy(source, i, peer):
        at = pl.ds(pl.multiple_of(source * part, DH), part)
        return pltpu.make_async_remote_copy(
            src_ref=wof_ref.at[at],
            dst_ref=wof_ref.at[at],
            send_sem=wsend.at[i],
            recv_sem=wrecv.at[i],
            device_id={"head": peer},
            device_id_type=MESH,
        )

    loads[1].wait()
    wcopy(hd, 0, cross).start()
    wcopy(hd, 1, sib).start()

    r_i, l_i = iota((LANES, LANES), 0), iota((LANES, LANES), 1)

    def toeplitz(table, count):
        t_i, j_i = iota((count, LANES), 0), iota((count, LANES), 1)
        low = 63 - count // 2
        pick = (t_i == jnp.clip(j_i - low, 0, count - 1)).astype(BF)
        ext = mm(table.astype(BF), pick)
        return [
            pltpu.roll(jnp.broadcast_to(ext[h : h + 1], (LANES, LANES)), 65, 1, stride=1, stride_axis=0)
            for h in range(heads)
        ]

    pos_t = toeplitz(tp_ref[...], POSB)
    x_t = toeplitz(tb_ref[:, 0, :], BOXB)
    y_t = toeplitz(tb_ref[:, 1, :], BOXB)

    def within(low, high):
        return (r_i >= low) & (r_i < high) & (l_i >= low) & (l_i < high)

    seg_part = jnp.where(within(SEG0, LSE0) & (r_i != l_i), -BIG, 0.0)
    for h in range(heads):
        map1[h] = jnp.where(
            within(0, 64), x_t[h], jnp.where(within(64, 96), pos_t[h], seg_part)
        ).astype(BF)
        map0[h] = jnp.where(within(64, 128), y_t[h], 0.0).astype(BF)

    for copy in hcopies:
        copy.wait()
    dbuf[dp] = ((hbuf[0] + hbuf[1]) + hbuf[2]) + hbuf[3]

    def dcopy(j):
        return pltpu.make_async_remote_copy(
            src_ref=dbuf.at[dp],
            dst_ref=dbuf.at[dp],
            send_sem=dsend.at[j],
            recv_sem=drecv.at[j],
            device_id={"dp": lax.rem(dp + j, n_dp)},
            device_id_type=MESH,
        )

    def dstart(j, carry):
        dcopy(j).start()
        return carry

    def dwait(j, carry):
        dcopy(j).wait()
        return carry

    lax.fori_loop(1, n_dp, dstart, 0)

    def features(c, carry):
        at = pl.ds(pl.multiple_of(c * LANES, LANES), LANES)
        seg, _, bucket = row_layout(r_i + c * LANES, lens)
        bx = jnp.broadcast_to(box_ref[0:1, at].astype(F32), (LANES, LANES)).T.astype(I32)
        by = jnp.broadcast_to(box_ref[1:2, at].astype(F32), (LANES, LANES)).T.astype(I32)
        hot = (
            (l_i == bx)
            | (l_i == bucket + 64)
            | (l_i == seg + SEG0)
        )
        key1 = hot.astype(F32)
        k1_ref[at] = jnp.where((l_i >= LSE0) & (l_i < LSE0 + 3), 1.0, key1).astype(BF)
        key1 = key1.astype(BF)
        key0 = (l_i == by + 64).astype(F32).astype(BF)
        for h in range(heads):
            q1_ref[h, at] = mm(key1, map1[h]).astype(BF)
            q0_ref[h, at] = mm(key0, map0[h]).astype(BF)
            k0_ref[h, at] = key0
        return carry

    per = own // LANES

    def block_features(source):
        lax.fori_loop(source * per, (source + 1) * per, features, 0)

    block_features(hd)
    lax.fori_loop(1, n_dp, dwait, 0)

    def dsum(j, total):
        return total + dbuf[j]

    total = lax.fori_loop(1, n_dp, dsum, dbuf[0])
    count = float(VISUAL * docs) * n_dp
    mean = total[0:1] / count
    inv_std = lax.rsqrt(total[1:2] / count - mean * mean + BATCH_EPS)
    st_ref[0:1] = mean
    st_ref[1:2] = inv_std
    pieces = asend.shape[1]
    piece = own // pieces

    def acopy(source, s, i, peer):
        at = pl.ds(pl.multiple_of(source * own + s * piece, piece), piece)
        return pltpu.make_async_remote_copy(
            src_ref=abuf.at[at],
            dst_ref=abuf.at[at],
            send_sem=asend.at[i, s],
            recv_sem=arecv.at[i, s],
            device_id={"head": peer},
            device_id_type=MESH,
        )

    for s in range(pieces):
        at = pl.ds(s * piece, piece)
        v = tok_ref[at].astype(F32)
        vis = vis_f[s * piece : (s + 1) * piece, 0:1] > 0.5
        x_in = jnp.where(vis, (v - mean) * inv_std * row(gain_ref) + row(shift_ref), v)
        xin_ref[at] = x_in
        abuf[pl.ds(pl.multiple_of(hd * own + s * piece, piece), piece)] = x_in.astype(BF)
        acopy(hd, s, 0, cross).start()
        acopy(hd, s, 1, sib).start()

    lane = iota((piece, LANES), 1)

    def project(source, s):
        at = pl.ds(pl.multiple_of(source * own + s * piece, piece), piece)
        a = abuf[at]
        q = ((mm_nt(a, w_ref[0]) + b_ref[0:1]).astype(BF)).astype(F32) * 0.125
        k = mm_nt(a, w_ref[1])
        v = mm_nt(a, w_ref[2]) + b_ref[1:2]
        for h in range(heads):
            cols = slice(h * DH, (h + 1) * DH)
            zero = jnp.zeros((piece, DH), F32)
            q0_ref[h, at] = jnp.where(
                lane < DH, jnp.concatenate([q[:, cols], zero], axis=1), q0_ref[h, at].astype(F32)
            ).astype(BF)
            k0_ref[h, at] = jnp.where(
                lane < DH, jnp.concatenate([k[:, cols], zero], axis=1), k0_ref[h, at].astype(F32)
            ).astype(BF)
            vx_ref[h, at] = jnp.where(
                lane < DH, jnp.concatenate([v[:, cols], zero], axis=1), 1.0
            ).astype(BF)

    def loop_project(source):
        def step(s, carry):
            project(source, s)
            return carry

        lax.fori_loop(0, pieces, step, 0)

    def outputs(source, i):
        at = pl.ds(pl.multiple_of(source * own, own), own)
        pairs = [(abuf.at[at], a_hbm.at[at]), (k1_ref.at[at], k1_hbm.at[at])]
        for src, dst in (
            (q0_ref, q0_hbm),
            (q1_ref, q1_hbm),
            (k0_ref, k0_hbm),
            (vx_ref, vx_hbm),
        ):
            pairs.append((src.at[:, at], dst.at[:, at]))
        return [
            pltpu.make_async_copy(src, dst, bsems.at[i, j]) for j, (src, dst) in enumerate(pairs)
        ]

    writes = [
        pltpu.make_async_copy(xin_ref, xin_hbm, osems.at[0]),
        pltpu.make_async_copy(wof_ref, wof_hbm, osems.at[1]),
    ]

    def write_block(source, i):
        block = outputs(source, i)
        for copy in block:
            copy.start()
        writes.extend(block)

    writes[0].start()
    loads[0].wait()
    loop_project(hd)
    write_block(hd, 0)
    wcopy(cross, 0, cross).wait_recv()
    wcopy(cross, 2, sib).start()
    block_features(sib)
    for s in range(pieces):
        acopy(sib, s, 1, sib).wait_recv()
    loop_project(sib)
    write_block(sib, 1)
    block_features(cross)
    block_features(diag)

    def late(s, c):
        acopy(cross, s, 0, cross).wait_recv()
        acopy(cross, s, 2, sib).start()
        project(cross, s)

        @pl.when(s >= 1)
        def _():
            acopy(diag, s - 1, 2, sib).wait_recv()
            project(diag, s - 1)

        return c

    lax.fori_loop(0, pieces, late, 0)
    write_block(cross, 2)
    wcopy(sib, 1, sib).wait_recv()
    wcopy(diag, 2, sib).wait_recv()
    writes[1].start()
    acopy(diag, pieces - 1, 2, sib).wait_recv()
    project(diag, pieces - 1)
    write_block(diag, 3)
    wcopy(hd, 0, cross).wait_send()
    wcopy(hd, 1, sib).wait_send()
    wcopy(cross, 2, sib).wait_send()
    for s in range(pieces):
        acopy(hd, s, 0, cross).wait_send()
        acopy(hd, s, 1, sib).wait_send()
        acopy(cross, s, 2, sib).wait_send()
    for copy in writes:
        copy.wait()


def entry(tokens, lengths, box_cells, bn_gain, bn_shift, w, b_qv, tab_pos, tab_box, w_out, n_dp):
    own, width = tokens.shape
    group = box_cells.shape[1]
    heads = w.shape[1] // DH
    pieces = 4
    tile = jax.ShapeDtypeStruct((heads, group, LANES), BF)
    dma = pltpu.SemaphoreType.DMA
    return pl.pallas_call(
        entry_kernel,
        out_shape=(
            jax.ShapeDtypeStruct((own, width), F32),
            jax.ShapeDtypeStruct((group, width), BF),
            tile,
            tile,
            tile,
            jax.ShapeDtypeStruct((group, LANES), BF),
            tile,
            jax.ShapeDtypeStruct((2, width), F32),
            jax.ShapeDtypeStruct((4 * w_out.shape[0], w_out.shape[1]), BF),
        ),
        in_specs=[SM] + [VM] * 4 + [HB] + [VM] * 3 + [HB],
        out_specs=(HB,) * 7 + (VM, HB),
        scratch_shapes=[
            pltpu.VMEM(w.shape, BF),
            pltpu.VMEM((own, width), F32),
            pltpu.VMEM((heads, group, LANES), BF),
            pltpu.VMEM((heads, group, LANES), BF),
            pltpu.VMEM((heads, group, LANES), BF),
            pltpu.VMEM((group, LANES), BF),
            pltpu.VMEM((heads, group, LANES), BF),
            pltpu.VMEM((4 * w_out.shape[0], width), BF),
            pltpu.VMEM((group, width), BF),
            pltpu.VMEM((4, 8, width), F32),
            pltpu.VMEM((n_dp, 8, width), F32),
            pltpu.VMEM((heads, LANES, LANES), BF),
            pltpu.VMEM((heads, LANES, LANES), BF),
            dma((3,)),
            dma((3,)),
            dma((n_dp,)),
            dma((n_dp,)),
            dma((3, pieces)),
            dma((3, pieces)),
            dma((3,)),
            dma((3,)),
            dma((2,)),
            dma((2,)),
            dma((4, 6)),
        ],
        compiler_params=pltpu.CompilerParams(
            collective_id=0, has_side_effects=True, vmem_limit_bytes=VMEM_CAP
        ),
        name="entry",
    )(
        lengths,
        tokens,
        box_cells,
        bn_gain,
        bn_shift,
        w,
        b_qv,
        tab_pos,
        tab_box,
        w_out,
    )


def list_pairs(pairs, lens, group):
    blocks = group // BLK

    def list_block(qb, n):
        low, high = block_window(qb, lens, group)

        def add(kb, m):
            pairs[0, m] = qb
            pairs[1, m] = kb
            return m + 1

        return lax.fori_loop(low, high, add, n)

    count = lax.fori_loop(0, blocks, list_block, 0)
    pairs[0, count] = 0
    pairs[1, count] = blocks - 1
    return (count + 1) // 2


def spots(pairs, i):
    return (
        pl.ds(pl.multiple_of(pairs[0, i] * BLK, BLK), BLK),
        pl.ds(pl.multiple_of(pairs[1, i] * BLK, BLK), BLK),
    )


def split_columns(tile, lane, first, rest):
    for i in range(3):
        part = rest.astype(BF).astype(F32)
        tile = jnp.where(lane == first + i, part, tile)
        rest = rest - part
    return tile


def attend_kernel(
    len_ref, q0_ref, q1_ref, k0_ref, k1_ref, vx_ref, o_ref, q1b_ref, m_scr, acc, pbuf, pairs
):
    heads, group = q0_ref.shape[0], q0_ref.shape[1]
    lens = [len_ref[0, d] for d in range(len_ref.shape[1])]
    lane = iota((BLK, LANES), 1)
    hs = range(heads)
    steps = list_pairs(pairs, lens, group)
    m_scr[...] = jnp.full_like(m_scr, -2.0 * BIG)
    acc[...] = jnp.zeros_like(acc)

    def scores(at, ks, tail):
        kf = k1_ref[ks]
        return [
            mm_nt(
                jnp.concatenate([q0_ref[h, at], tail[h, at]], axis=1),
                jnp.concatenate([k0_ref[h, ks], kf], axis=1),
            )
            for h in hs
        ]

    def highest(i, c):
        for u in range(2):
            at, ks = spots(pairs, 2 * i + u)
            qb = pairs[0, 2 * i + u]
            st = scores(at, ks, q1_ref)
            for h in hs:
                m_scr[qb, h] = jnp.maximum(
                    m_scr[qb, h], jnp.maximum(st[h][:, :LANES], st[h][:, LANES:])
                )
        return c

    lax.fori_loop(0, steps, highest, 0)

    def shift(qb, c):
        at = pl.ds(pl.multiple_of(qb * BLK, BLK), BLK)
        for h in hs:
            m = jnp.max(m_scr[qb, h], axis=1, keepdims=True)
            m_scr[qb, h] = jnp.broadcast_to(m, (BLK, LANES))
            q1b_ref[h, at] = split_columns(q1_ref[h, at].astype(F32), lane, LSE0, -m).astype(BF)
        return c

    lax.fori_loop(0, group // BLK, shift, 0)

    def weigh(i, slot):
        for u in range(2):
            at, ks = spots(pairs, 2 * i + u)
            st = scores(at, ks, q1b_ref)
            for h in hs:
                pbuf[slot, u, h] = jnp.exp(st[h]).astype(BF)

    def gather(i, slot):
        for u in range(2):
            _, ks = spots(pairs, 2 * i + u)
            qb = pairs[0, 2 * i + u]
            for h in hs:
                acc[qb, h] += mm(pbuf[slot, u, h], vx_ref[h, ks])

    weigh(0, 0)

    def step(i, c):
        gather(i - 1, lax.rem(i - 1, 2))
        weigh(jnp.minimum(i, steps - 1), lax.rem(i, 2))
        return c

    lax.fori_loop(1, steps + 1, step, 0)

    def close(qb, c):
        at = pl.ds(pl.multiple_of(qb * BLK, BLK), BLK)
        for h in hs:
            a = acc[qb, h]
            turned = pltpu.roll(a, DH, 1)
            o_ref[at, h * DH : (h + 1) * DH] = (a / turned)[:, :DH].astype(BF)
            total = jnp.where(lane < DH, turned, a)
            q1b_ref[h, at] = split_columns(
                q1_ref[h, at].astype(F32), lane, LSE0, -(m_scr[qb, h] + jnp.log(total))
            ).astype(BF)
        return c

    lax.fori_loop(0, group // BLK, close, 0)


def attend(lengths, q0, q1, k0, k1, vx):
    heads, group, _ = q0.shape
    blocks = group // BLK
    return pl.pallas_call(
        attend_kernel,
        out_shape=(
            jax.ShapeDtypeStruct((group, heads * DH), BF),
            jax.ShapeDtypeStruct(q1.shape, BF),
        ),
        in_specs=[SM] + [VM] * 5,
        out_specs=(VM, VM),
        scratch_shapes=[
            pltpu.VMEM((blocks, heads, BLK, LANES), F32),
            pltpu.VMEM((blocks, heads, BLK, LANES), F32),
            pltpu.VMEM((2, 2, heads, BLK, BLK), BF),
            pltpu.SMEM((2, blocks * blocks + 1), I32),
        ],
        compiler_params=pltpu.CompilerParams(vmem_limit_bytes=VMEM_CAP),
        name="attend",
    )(lengths, q0, q1, k0, k1, vx)


C_TAIL = 0.23
TAIL = (
    -2.7761570891016163e-05,
    0.09237844496965408,
    0.08576294034719467,
    0.1195140853524208,
    -0.032920535653829575,
    0.30147361755371094,
    -0.2781279683113098,
    0.2904147207736969,
    -0.07846760004758835,
)


def gelu_pair(v):
    a = jnp.abs(v)
    t = 1.0 / (1.0 + C_TAIL * a)
    g = jnp.full_like(v, TAIL[-1])
    for c in TAIL[-2::-1]:
        g = g * t + c
    e = jnp.exp(v * v * -0.5)
    tail = g * e
    phi = jnp.where(v > 0.0, 1.0 - tail, tail)
    return v * phi, phi + v * (e * 0.3989422804014327)


def row_stats(h):
    scale = 1.0 / h.shape[1]
    centred = h - jnp.sum(h, axis=1, keepdims=True) * scale
    rstd = lax.rsqrt(jnp.sum(centred * centred, axis=1, keepdims=True) * scale + NORM_EPS)
    return centred * rstd, rstd


def norm_back(grad, normed, rstd):
    scale = 1.0 / grad.shape[1]
    mean = jnp.sum(grad, axis=1, keepdims=True) * scale
    along = jnp.sum(grad * normed, axis=1, keepdims=True) * scale
    return rstd * (grad - mean - normed * along)


def add_row(ref, i, v):
    ref[i : i + 1] += jnp.sum(v, axis=0, keepdims=True)


def outer_sum(out_ref, a_ref, b_ref, rows):
    def step(m, c):
        cols = pl.ds(pl.multiple_of(m * BLK, BLK), BLK)
        out_ref[cols] = mm_tn(a_ref[0:rows, cols], b_ref[0:rows])
        return c

    lax.fori_loop(0, out_ref.shape[0] // BLK, step, 0)


class Exchange:
    def __init__(self, own, piece):
        self.own, self.piece, self.pieces = own, piece, own // piece
        self.hd, self.sib, self.cross, self.diag = head_peers()

    def rows(self, source, s, base=0):
        return pl.ds(pl.multiple_of(source * self.own + s * self.piece, self.piece), self.piece)

    def send(self, src, dst, sems, i, s, peer):
        return pltpu.make_async_remote_copy(
            src_ref=src,
            dst_ref=dst,
            send_sem=sems.at[0, i, s],
            recv_sem=sems.at[1, i, s],
            device_id={"head": peer},
            device_id_type=MESH,
        )

    def gather(self, buf, sems, i, s):
        source = self.cross if i == 2 else self.hd
        at = self.rows(source, s)
        return self.send(buf.at[at], buf.at[at], sems, i, s, self.cross if i == 0 else self.sib)

    def gather_from(self, buf, sems, i, s):
        source = (self.cross, self.sib, self.diag)[i]
        at = self.rows(source, s)
        return self.send(buf.at[at], buf.at[at], sems, i, s, self.cross if i == 0 else self.sib)

    def partial(self, snd, rcv, sems, i, s):
        return self.send(
            snd.at[i, s], rcv.at[i, s], sems, i, s, self.cross if i == 2 else self.sib
        )


def middle_kernel(
    attn_ref,
    xin_ref,
    cot_ref,
    wo_ref,
    wu_ref,
    wd_ref,
    bo_ref,
    g1_ref,
    s1_ref,
    bu_ref,
    bd_ref,
    g2_ref,
    s2_ref,
    out_ref,
    gone_ref,
    ga_ref,
    gwo_ref,
    dtot_ref,
    usum_ref,
    sums_ref,
    gbu_ref,
    *rest,
):
    ships, rest = rest[:-32], rest[-32:]
    (
        abuf,
        full,
        fin,
        gl,
        gd,
        fgr,
        gpre,
        xh1,
        rs1,
        two,
        ownp,
        crossp,
        snd1,
        rcv1,
        snd2,
        rcv2,
        asems,
        f1sems,
        r1sems,
        f2sems,
        r2sems,
        gsems,
        dsnd,
        drcv,
        dpsnd,
        dprcv,
        dmine,
        dsems,
        dpsems,
        usnd,
        urcv,
        usems,
    ) = rest
    own, width = xin_ref.shape
    hcols = attn_ref.shape[1]
    piece = own // asems.shape[2]
    ex = Exchange(own, piece)
    hd, sib, cross, diag = ex.hd, ex.sib, ex.cross, ex.diag
    peers = (cross, diag, sib)
    members, part = len(ships) + 1, dtot_ref.shape[0]
    head_and_dp_barrier(2 * members)()

    def own_at(s):
        return pl.ds(pl.multiple_of(s * piece, piece), piece)

    def acopy(s, i):
        at = ex.rows(peers[i], s)
        return ex.send(attn_ref.at[at], abuf.at[hd, own_at(s)], asems, i, s, peers[i])

    def afrom(s, i):
        return ex.send(
            attn_ref.at[own_at(s)], abuf.at[peers[i], own_at(s)], asems, i, s, peers[i]
        )

    def all_sends(s, c):
        for i in range(3):
            acopy(s, i).start()
        return c

    lax.fori_loop(0, ex.pieces, all_sends, 0)
    abuf[hd] = attn_ref[pl.ds(pl.multiple_of(hd * own, own), own)]
    sums_ref[...] = jnp.zeros_like(sums_ref)
    gbu_ref[...] = jnp.zeros_like(gbu_ref)

    def first_norm(s, c):
        at = own_at(s)
        for i in range(3):
            afrom(s, i).wait_recv()
        for source in range(4):
            full[at, source * hcols : (source + 1) * hcols] = abuf[source, at]
        h = xin_ref[at] + (mm(full[at], wo_ref[...]) + row(bo_ref))
        normed, rstd = row_stats(h)
        xh1[at] = normed
        rs1[at] = jnp.broadcast_to(rstd, (piece, LANES))
        fin[ex.rows(hd, s)] = (normed * row(g1_ref) + row(s1_ref)).astype(BF)
        ex.gather(fin, f1sems, 0, s).start()
        ex.gather(fin, f1sems, 1, s).start()
        return c

    lax.fori_loop(0, ex.pieces, first_norm, 0)

    def pipeline(buf, fsems, snd, rcv, rsems, compute):
        def near(s):
            ex.gather_from(buf, fsems, 1, s).wait_recv()
            part = compute(ex.rows(hd, s), ex.rows(sib, s))
            ownp[own_at(s)] = part[:piece]
            snd[0, s] = part[piece:].astype(BF)
            ex.partial(snd, rcv, rsems, 0, s).start()

        def far(s):
            ex.gather_from(buf, fsems, 2, s).wait_recv()
            part = compute(ex.rows(cross, s), ex.rows(diag, s))
            crossp[own_at(s)] = part[:piece]
            snd[1, s] = part[piece:].astype(BF)
            ex.partial(snd, rcv, rsems, 1, s).start()

        def combine(s):
            ex.partial(snd, rcv, rsems, 1, s).wait_recv()
            snd[2, s] = (crossp[own_at(s)] + rcv[1, s].astype(F32)).astype(BF)
            ex.partial(snd, rcv, rsems, 2, s).start()

        def step(s, c):
            @pl.when(s >= 2)
            def _():
                combine(s - 2)

            @pl.when(s < ex.pieces)
            def _():
                near(s)
                ex.gather_from(buf, fsems, 0, s).wait_recv()
                ex.gather(buf, fsems, 2, s).start()

            @pl.when((s >= 1) & (s <= ex.pieces))
            def _():
                far(s - 1)

            return c

        lax.fori_loop(0, ex.pieces + 2, step, 0)

    def collected(rcv, rsems, snd, s):
        ex.partial(snd, rcv, rsems, 0, s).wait_recv()
        ex.partial(snd, rcv, rsems, 2, s).wait_recv()
        return ownp[own_at(s)] + rcv[0, s].astype(F32) + rcv[2, s].astype(F32)

    def forward(at_a, at_b):
        x = jnp.concatenate([fin[at_a], fin[at_b]], axis=0)
        value, slope = gelu_pair(mm(x, wu_ref[...]) + row(bu_ref))
        low = value.astype(BF)
        gl[at_a] = low[:piece]
        gl[at_b] = low[piece:]
        gd[at_a] = slope[:piece]
        gd[at_b] = slope[piece:]
        return mm(low, wd_ref[...])

    pipeline(fin, f1sems, snd1, rcv1, r1sems, forward)

    def second_norm(s, c):
        at = own_at(s)
        mid = xh1[at] * row(g1_ref) + row(s1_ref)
        h = mid + (collected(rcv1, r1sems, snd1, s) + row(bd_ref))
        normed, rstd = row_stats(h)
        out_ref[at] = (normed * row(g2_ref) + row(s2_ref)).astype(BF)
        cot = cot_ref[at].astype(F32)
        add_row(sums_ref, 2, cot * normed)
        add_row(sums_ref, 3, cot)
        grad = norm_back(cot * row(g2_ref), normed, rstd)
        two[at] = grad
        add_row(sums_ref, 5, grad)
        fgr[ex.rows(hd, s)] = grad.astype(BF)
        ex.gather(fgr, f2sems, 0, s).start()
        ex.gather(fgr, f2sems, 1, s).start()
        return c

    lax.fori_loop(0, ex.pieces, second_norm, 0)

    def backward(at_a, at_b):
        x = jnp.concatenate([fgr[at_a], fgr[at_b]], axis=0)
        slope = jnp.concatenate([gd[at_a], gd[at_b]], axis=0)
        low = (mm_nt(x, wd_ref[...]) * slope).astype(BF)
        gpre[at_a] = low[:piece]
        gpre[at_b] = low[piece:]
        add_row(gbu_ref, 0, low.astype(F32))
        return mm_nt(low, wu_ref[...])

    pipeline(fgr, f2sems, snd2, rcv2, r2sems, backward)
    gwd, gwu = gd.at[0:width], gd.at[width : 2 * width]
    outer_sum(gwd, gl, fgr, gl.shape[0])
    down = Reduce(
        members,
        part,
        dict(snd=dsnd, rcv=drcv, psnd=dpsnd, prcv=dprcv, mine=dmine, sems=dsems, psems=dpsems),
        gwd,
    )
    up = Reduce(members, part, dict(snd=usnd, rcv=urcv, sems=usems), gwu)
    down.start()

    def gcopy(s, i, source):
        return ex.send(
            abuf.at[peers[i], own_at(s)], ga_ref.at[ex.rows(source, s)], gsems, i, s, peers[i]
        )

    for i in range(3):
        for s in range(ex.pieces):
            acopy(s, i).wait_send()

    def last_norm(s, c):
        at = own_at(s)
        grad = two[at] + collected(rcv2, r2sems, snd2, s)
        normed = xh1[at]
        add_row(sums_ref, 0, grad * normed)
        add_row(sums_ref, 1, grad)
        one = norm_back(grad * row(g1_ref), normed, rs1[at][:, 0:1])
        gone_ref[at] = one
        add_row(sums_ref, 4, one)
        low = one.astype(BF)
        fin[at] = low
        heads = mm_nt(low, wo_ref[...]).astype(BF)
        for source in range(4):
            abuf[source, at] = heads[:, source * hcols : (source + 1) * hcols]
        for i in range(3):
            gcopy(s, i, hd).start()
        return c

    for s in range(ex.pieces):
        for i in range(3):
            ex.gather(fin, f1sems, i, s).wait_send()
    outer_sum(gwu, fin, gpre, fin.shape[0])
    up.start()
    lax.fori_loop(0, ex.pieces, last_norm, 0)
    ga_ref[pl.ds(pl.multiple_of(hd * own, own), own)] = abuf[hd]
    down.spread()
    outer_sum(gwo_ref, full, fin, own)
    up.first().wait()
    usum_ref[...] = up.halves(up.me)
    for k, ship in enumerate(ships):
        ship[:part] = up.halves(lax.rem(up.me + k + 1, members)).astype(BF)
    down.gather()
    low = dmine[...].astype(BF)
    dtot_ref[...] = low
    for ship in ships:
        ship[part:] = low
    down.sent()
    for s in range(ex.pieces):
        for i in range(3):
            gcopy(s, i, peers[i]).wait()
            ex.partial(snd1, rcv1, r1sems, i, s).wait_send()
            ex.gather(fgr, f2sems, i, s).wait_send()
            ex.partial(snd2, rcv2, r2sems, i, s).wait_send()


def middle(attn, x_in, cotangent, w_out, w_up, w_down, vectors, n_dp):
    own, width = x_in.shape
    group, hcols = attn.shape
    hidden = w_up.shape[1]
    pieces = 4
    piece = own // pieces
    dma = pltpu.SemaphoreType.DMA
    exchange = pltpu.VMEM((3, pieces, piece, width), BF)
    members, part = n_dp // 2, width // n_dp
    parts = pltpu.VMEM((members, part, width), BF)
    return pl.pallas_call(
        middle_kernel,
        out_shape=(
            jax.ShapeDtypeStruct((own, width), BF),
            jax.ShapeDtypeStruct((own, width), F32),
            jax.ShapeDtypeStruct((group, hcols), BF),
            jax.ShapeDtypeStruct((4 * hcols, width), F32),
            jax.ShapeDtypeStruct((part, width), BF),
            jax.ShapeDtypeStruct((part, width), F32),
            jax.ShapeDtypeStruct((8, width), F32),
            jax.ShapeDtypeStruct((1, hidden), F32),
        )
        + (jax.ShapeDtypeStruct((2 * part, width), BF),) * (members - 1),
        in_specs=[VM] * 13,
        out_specs=(VM,) * (7 + members),
        scratch_shapes=[
            pltpu.VMEM((4, own, hcols), BF),
            pltpu.VMEM((own, 4 * hcols), BF),
            pltpu.VMEM((group, width), BF),
            pltpu.VMEM((group, hidden), BF),
            pltpu.VMEM((group, hidden), F32),
            pltpu.VMEM((group, width), BF),
            pltpu.VMEM((group, hidden), BF),
            pltpu.VMEM((own, width), F32),
            pltpu.VMEM((own, LANES), F32),
            pltpu.VMEM((own, width), F32),
            pltpu.VMEM((own, width), F32),
            pltpu.VMEM((own, width), F32),
            exchange,
            exchange,
            exchange,
            exchange,
        ]
        + [dma((2, 3, pieces))] * 6
        + [parts] * 4
        + [pltpu.VMEM((part, width), F32), dma((2, 2)), dma((2, 2, members))]
        + [parts] * 2
        + [dma((2, 2))],
        compiler_params=pltpu.CompilerParams(
            collective_id=1, has_side_effects=True, vmem_limit_bytes=VMEM_CAP
        ),
        name="middle",
    )(attn, x_in, cotangent, w_out, w_up, w_down, *vectors)


def attend_back_kernel(
    len_ref,
    q0_ref,
    q1_ref,
    k0_ref,
    k1_ref,
    vx_ref,
    o_ref,
    go_ref,
    dqkv_ref,
    gt_ref,
    dox,
    kacc,
    vacc,
    qacc,
    k0t,
    k1t,
    map0,
    map1,
    pbuf,
    dbuf,
    pairs,
):
    heads, group = q0_ref.shape[0], q0_ref.shape[1]
    width = heads * DH
    lens = [len_ref[0, d] for d in range(len_ref.shape[1])]
    lane = iota((BLK, LANES), 1)
    spread = (
        iota((width, heads * LANES), 0) // DH == iota((width, heads * LANES), 1) // LANES
    ).astype(F32).astype(BF)
    map0[...] = jnp.zeros_like(map0)
    map1[...] = jnp.zeros_like(map1)
    kacc[...] = jnp.zeros_like(kacc)
    vacc[...] = jnp.zeros_like(vacc)
    qacc[...] = jnp.zeros_like(qacc)

    def prepare(qb, carry):
        at = pl.ds(pl.multiple_of(qb * BLK, BLK), BLK)
        g = go_ref[at].astype(F32)
        e = g * o_ref[at].astype(F32)
        e_high = e.astype(BF)
        e_low = (e - e_high.astype(F32)).astype(BF)
        dots = mm(e_high, spread) + mm(e_low, spread)
        for h in range(heads):
            rest = -dots[:, h * LANES : (h + 1) * LANES]
            tile = jnp.where(
                lane < DH,
                jnp.concatenate([g[:, h * DH : (h + 1) * DH], jnp.zeros((BLK, DH), F32)], axis=1),
                0.0,
            )
            for i in range(3):
                part = rest.astype(BF).astype(F32)
                tile = jnp.where(lane == DH + i, part, tile)
                rest = rest - part
            dox[h, at] = tile.astype(BF)
        return carry

    lax.fori_loop(0, group // BLK, prepare, 0)

    def turn(kb, carry):
        at = pl.ds(pl.multiple_of(kb * BLK, BLK), BLK)
        k1t[:, at] = k1_ref[at].T
        for h in range(heads):
            k0t[h, :, at] = k0_ref[h, at].T
        return carry

    lax.fori_loop(0, group // BLK, turn, 0)

    steps = list_pairs(pairs, lens, group)
    hs = range(heads)

    def weigh(i, slot):
        for u in range(2):
            at, ks = spots(pairs, 2 * i + u)
            kf = k1_ref[ks]
            st = [
                mm_nt(
                    jnp.concatenate([k0_ref[h, ks], kf], axis=1),
                    jnp.concatenate([q0_ref[h, at], q1_ref[h, at]], axis=1),
                )
                for h in hs
            ]
            dp = [mm_nt(vx_ref[h, ks], dox[h, at]) for h in hs]
            p = [jnp.exp(st[h]) for h in hs]
            for h in hs:
                pbuf[slot, u, h] = p[h].astype(BF)
                dbuf[slot, u, h] = (p[h] * dp[h]).astype(BF)

    def gather(i, slot):
        for u in range(2):
            at, ks = spots(pairs, 2 * i + u)
            qb = pairs[0, 2 * i + u]
            for h in hs:
                vacc[h, ks] += mm(pbuf[slot, u, h], dox[h, at])
            for h in hs:
                kacc[h, ks] += mm(dbuf[slot, u, h], q0_ref[h, at])
            kt = k1t[:, ks]
            for h in hs:
                qacc[qb, h] += mm(jnp.concatenate([k0t[h, :, ks], kt], axis=0), dbuf[slot, u, h])

    weigh(0, 0)

    def pair(i, carry):
        gather(i - 1, lax.rem(i - 1, 2))
        weigh(jnp.minimum(i, steps - 1), lax.rem(i, 2))
        return carry

    lax.fori_loop(1, steps + 1, pair, 0)

    def block(qb, carry):
        at = pl.ds(pl.multiple_of(qb * BLK, BLK), BLK)
        for h in range(heads):
            a = qacc[qb, h]
            dqkv_ref[at, h * DH : (h + 1) * DH] = (a[:LANES].T[:, :DH] * 0.125).astype(BF)
            high_part = a.astype(BF)
            low_part = (a - high_part.astype(F32)).astype(BF)
            for m, hot, rows in (
                (map0, k0_ref[h, at], slice(0, LANES)),
                (map1, k1_ref[at], slice(LANES, 2 * LANES)),
            ):
                m[h] += mm(jnp.concatenate([high_part[rows], low_part[rows]], axis=0), hot)
        return carry

    lax.fori_loop(0, group // BLK, block, 0)

    def finish(kb, carry):
        at = pl.ds(pl.multiple_of(kb * BLK, BLK), BLK)
        for h in range(heads):
            k_at, v_at = width + h * DH, 2 * width + h * DH
            dqkv_ref[at, k_at : k_at + DH] = kacc[h, at][:, :DH].astype(BF)
            dqkv_ref[at, v_at : v_at + DH] = vacc[h, at][:, :DH].astype(BF)
        return carry

    lax.fori_loop(0, group // BLK, finish, 0)

    gt_ref[...] = jnp.zeros_like(gt_ref)
    r_i, l_i = iota((LANES, LANES), 0), iota((LANES, LANES), 1)

    def exact(a, b):
        return jnp.dot(a, b, precision=lax.Precision.HIGHEST, preferred_element_type=F32)

    def diagonals(block, base, count):
        inside = (r_i >= base) & (r_i < base + count) & (l_i >= base) & (l_i < base + count)
        flip = ((l_i == base + count - 1 - r_i) & (l_i < count)).astype(F32)
        turned = exact(jnp.where(inside, block, 0.0), flip)
        moved = pltpu.roll(turned, (64 - base - count) % LANES, 1, stride=1, stride_axis=0)
        return jnp.sum(moved, axis=0, keepdims=True)

    def fold(block, base, count):
        sums = jnp.broadcast_to(diagonals(block, base, count), (8, LANES))
        j_i, t_i = iota((LANES, count), 0), iota((LANES, count), 1)
        low = 63 - count // 2
        pick = (t_i == jnp.clip(j_i - low, 0, count - 1)).astype(F32)
        return exact(sums, pick)[0:1]

    for h in range(heads):
        one = map1[h][:LANES] + map1[h][LANES:]
        zero = map0[h][:LANES] + map0[h][LANES:]
        gt_ref[h : h + 1, 0:POSB] = fold(one, 64, POSB)
        gt_ref[heads + h : heads + h + 1, 0:BOXB] = fold(one, 0, BOXB)
        gt_ref[2 * heads + h : 2 * heads + h + 1, 0:BOXB] = fold(zero, 64, BOXB)


def attend_back(lengths, q0, q1, k0, k1, vx, out, grad_out):
    heads, group, _ = q0.shape
    return pl.pallas_call(
        attend_back_kernel,
        out_shape=(
            jax.ShapeDtypeStruct((group, 3 * heads * DH), BF),
            jax.ShapeDtypeStruct((16, LANES), F32),
        ),
        in_specs=[SM] + [VM] * 7,
        out_specs=(VM,) * 2,
        scratch_shapes=[
            pltpu.VMEM((heads, group, LANES), BF),
            pltpu.VMEM((heads, group, LANES), F32),
            pltpu.VMEM((heads, group, LANES), F32),
            pltpu.VMEM((group // BLK, heads, 2 * LANES, BLK), F32),
            pltpu.VMEM((heads, LANES, group), BF),
            pltpu.VMEM((LANES, group), BF),
            pltpu.VMEM((heads, 2 * LANES, LANES), F32),
            pltpu.VMEM((heads, 2 * LANES, LANES), F32),
            pltpu.VMEM((2, 2, heads, BLK, BLK), BF),
            pltpu.VMEM((2, 2, heads, BLK, BLK), BF),
            pltpu.SMEM((2, (group // BLK) ** 2 + 1), I32),
        ],
        compiler_params=pltpu.CompilerParams(vmem_limit_bytes=VMEM_CAP),
        cost_estimate=pl.CostEstimate(
            flops=2 * 5 * heads * group * group * LANES, bytes_accessed=16 << 20, transcendentals=0
        ),
        name="attend_back",
    )(lengths, q0, q1, k0, k1, vx, out, grad_out)


def final_kernel(
    members,
    len_ref,
    dqkv_hbm,
    w_hbm,
    a_hbm,
    tok_hbm,
    st_ref,
    gone_hbm,
    dtot_ref,
    usum_ref,
    gwo_hbm,
    sums_ref,
    gbu_ref,
    gt_ref,
    *rest,
):
    ships = rest[: members - 1]
    (
        gin_ref,
        tot_ref,
        wd_ref,
        wu_ref,
        wq_ref,
        mixed,
        ownp,
        crossp,
        snd,
        rcv,
        osnd,
        orcv,
        hbuf,
        dbuf,
        rsems,
        osems,
        hsems,
        dsems,
        dhalf,
        dother,
        dpair,
        dpart,
        uhalf,
        uother,
        upair,
        upart,
        dqkv_ref,
        a_ref,
        gwo_ref,
        w_ref,
        gone_ref,
        tok_ref,
        lsems,
        *qrefs,
    ) = rest[members - 1 :]
    loads = [
        pltpu.make_async_copy(src, dst, lsems.at[i])
        for i, (src, dst) in enumerate(
            (
                (dqkv_hbm, dqkv_ref),
                (a_hbm, a_ref),
                (gwo_hbm, gwo_ref),
                (w_hbm, w_ref),
                (gone_hbm, gone_ref),
                (tok_hbm, tok_ref),
            )
        )
    ]
    for load in loads:
        load.start()
    own, width = gone_ref.shape
    qcols = dqkv_ref.shape[1]
    hcols = qcols // 3
    n_dp = dbuf.shape[0]
    pieces = rsems.shape[2]
    piece = own // pieces
    ex = Exchange(own, piece)
    hd, sib, cross, diag = ex.hd, ex.sib, ex.cross, ex.diag
    dp = lax.axis_index("dp")
    head_and_dp_barrier(n_dp)()

    down = Reduce(
        members, width // n_dp, dict(half=dhalf, other=dother, sems=dpair, psems=dpart)
    )
    up = Reduce(
        members,
        width // n_dp,
        dict(half=uhalf, other=uother, sems=upair, psems=upart),
    )
    names = ("snd", "rcv", "psnd", "prcv", "half", "other", "mine", "sems", "psems")
    chunks = [
        Reduce(
            members,
            BLK // n_dp,
            dict(zip(names, qrefs[m * len(names) : (m + 1) * len(names)])),
            mixed,
            m * BLK,
        )
        for m in range(3)
    ]
    part = dtot_ref.shape[0]
    total = usum_ref[...]
    dhalf[down.me] = dtot_ref[...]
    for k, ship in enumerate(ships):
        source = lax.rem(down.me - (k + 1) + members, members)
        dhalf[source] = ship[part:]
        total = total + ship[:part].astype(F32)
    up.publish(total.astype(BF))

    def own_at(s):
        return pl.ds(pl.multiple_of(s * piece, piece), piece)

    def block_of(source):
        return pl.ds(pl.multiple_of(source * hcols, DH), hcols)

    def osend(i):
        return ex.send(osnd.at[i], orcv.at[i], osems, i, 0, cross if i == 2 else sib)

    loads[0].wait()
    loads[1].wait()
    for m in range(3):
        cols = slice(m * BLK, min((m + 1) * BLK, qcols))
        mixed[cols] = mm_tn(dqkv_ref[:, cols], a_ref[...])
        if m < 2:
            chunks[m].start()
        if m == 0:
            loads[2].wait()
            osnd[1] = gwo_ref[block_of(diag)].astype(BF)
            osend(1).start()
            osnd[0] = gwo_ref[block_of(sib)].astype(BF)
            osend(0).start()
    osend(1).wait_recv()
    osnd[2] = (gwo_ref[block_of(cross)] + orcv[1].astype(F32)).astype(BF)
    osend(2).start()
    loads[3].wait()

    def grad_rows(at):
        return mm(dqkv_ref[at], w_ref[...])

    def far(s, c):
        snd[1, s] = grad_rows(ex.rows(diag, s)).astype(BF)
        ex.partial(snd, rcv, rsems, 1, s).start()
        crossp[own_at(s)] = grad_rows(ex.rows(cross, s))

        @pl.when(s >= 1)
        def _():
            mix(s - 1)

        return c

    def mix(s):
        ex.partial(snd, rcv, rsems, 1, s).wait_recv()
        snd[2, s] = (crossp[own_at(s)] + rcv[1, s].astype(F32)).astype(BF)
        ex.partial(snd, rcv, rsems, 2, s).start()

    def near(s, c):
        snd[0, s] = grad_rows(ex.rows(sib, s)).astype(BF)
        ex.partial(snd, rcv, rsems, 0, s).start()
        ownp[own_at(s)] = grad_rows(ex.rows(hd, s))
        return c

    lax.fori_loop(0, pieces, far, 0)
    mix(pieces - 1)
    chunks[0].spread()
    osend(0).wait_recv()
    osend(2).wait_recv()
    mixed[qcols:] = gwo_ref[block_of(hd)] + orcv[0].astype(F32) + orcv[2].astype(F32)
    chunks[2].start()
    chunks[1].spread()
    down.fourth().start()
    lax.fori_loop(0, pieces, near, 0)
    chunks[0].gather()
    chunks[0].publish()

    dbuf[dp, 8:] = jnp.zeros((8, width), F32)
    dbuf[dp, 8:9] = gbu_ref[...]
    for b in range(9):
        dbuf[dp, 10 + b // 6 : 11 + b // 6, (b % 6) * LANES : (b % 6 + 1) * LANES] = gt_ref[
            b : b + 1
        ]

    def col_sums(s, c):
        at = pl.ds(pl.multiple_of(s * BLK, BLK), BLK)
        dbuf[dp, 9:10, 0:qcols] += jnp.sum(dqkv_ref[at].astype(F32), axis=0, keepdims=True)
        return c

    lax.fori_loop(0, dqkv_ref.shape[0] // BLK, col_sums, 0)
    chunks[2].spread()
    chunks[1].gather()
    chunks[1].publish()
    up.share()

    lens = [len_ref[0, d] for d in range(len_ref.shape[1])]
    mean, inv_std = st_ref[0:1], st_ref[1:2]
    hbuf[hd] = sums_ref[...]
    loads[4].wait()
    loads[5].wait()

    def grad_own(s, c):
        at = own_at(s)
        ex.partial(snd, rcv, rsems, 0, s).wait_recv()
        ex.partial(snd, rcv, rsems, 2, s).wait_recv()
        g = gone_ref[at] + (ownp[at] + rcv[0, s].astype(F32) + rcv[2, s].astype(F32))
        gin_ref[at] = g
        _, visual, _ = row_layout(iota((piece, LANES), 0) + (hd * own + s * piece), lens)
        g = jnp.where(visual[:, 0:1], g, 0.0)
        x_hat = (tok_ref[at].astype(F32) - mean) * inv_std
        hbuf[hd, 6:7] += jnp.sum(g, axis=0, keepdims=True)
        hbuf[hd, 7:8] += jnp.sum(g * x_hat, axis=0, keepdims=True)
        return c

    lax.fori_loop(0, pieces, grad_own, 0)
    hcopies = [
        ex.send(hbuf.at[hd], hbuf.at[hd], hsems, i, 0, peer)
        for i, peer in enumerate((sib, cross, diag))
    ]
    for copy in hcopies:
        copy.start()
    chunks[2].gather()
    chunks[2].publish()
    chunks[0].share()
    for copy in hcopies:
        copy.wait()
    dbuf[dp, 0:8] = ((hbuf[0] + hbuf[1]) + hbuf[2]) + hbuf[3]

    def dcopy(j):
        return pltpu.make_async_remote_copy(
            src_ref=dbuf.at[dp],
            dst_ref=dbuf.at[dp],
            send_sem=dsems.at[0, j],
            recv_sem=dsems.at[1, j],
            device_id={"dp": lax.rem(dp + j, n_dp)},
            device_id_type=MESH,
        )

    def dstart(j, carry):
        dcopy(j).start()
        return carry

    def dwait(j, carry):
        dcopy(j).wait()
        return carry

    lax.fori_loop(1, n_dp, dstart, 0)
    chunks[1].share()
    down.finish(wd_ref, moved=True)
    chunks[2].share()
    lax.fori_loop(1, n_dp, dwait, 0)

    def dsum(j, total):
        return total + dbuf[j]

    tot_ref[...] = lax.fori_loop(1, n_dp, dsum, dbuf[0])
    up.finish(wu_ref)
    for m, chunk in enumerate(chunks):
        chunk.finish(wq_ref, m * BLK)
        chunk.sent()
    for i in range(3):
        osend(i).wait_send()
        for s in range(pieces):
            ex.partial(snd, rcv, rsems, i, s).wait_send()


def final(lengths, dqkv, w, attn_in, tokens, stats, gone, dtot, usum, gwo, sums, gbu, gt, ships, n_dp):
    own, width = gone.shape
    hcols = dqkv.shape[1] // 3
    pieces = 4
    members, part = n_dp // 2, width // n_dp
    dma = pltpu.SemaphoreType.DMA
    exchange = pltpu.VMEM((3, pieces, own // pieces, width), BF)
    small = pltpu.VMEM((3, hcols, width), BF)
    parts = pltpu.VMEM((members, part, width), BF)
    bits = pltpu.VMEM((members, BLK // n_dp, width), BF)
    sems = [dma((2, 2)), dma((2, 2, members))]
    square = jax.ShapeDtypeStruct((width, width), BF)
    return pl.pallas_call(
        functools.partial(final_kernel, members),
        out_shape=(
            jax.ShapeDtypeStruct((own, width), F32),
            jax.ShapeDtypeStruct((16, width), F32),
            square,
            square,
            square,
        ),
        in_specs=[SM] + [HB] * 4 + [VM, HB, VM, VM, HB] + [VM] * (2 + members),
        out_specs=(VM,) * 5,
        scratch_shapes=[
            pltpu.VMEM((width, width), F32),
            pltpu.VMEM((own, width), F32),
            pltpu.VMEM((own, width), F32),
            exchange,
            exchange,
            small,
            small,
            pltpu.VMEM((4, 8, width), F32),
            pltpu.VMEM((n_dp, 16, width), F32),
            dma((2, 3, pieces)),
            dma((2, 3, 1)),
            dma((2, 3, 1)),
            dma((2, n_dp)),
        ]
        + [parts, parts]
        + sems
        + [parts] * 2
        + sems
        + [
            pltpu.VMEM(v.shape, v.dtype)
            for v in (dqkv, attn_in, gwo, w, gone, tokens)
        ]
        + [dma((6,))]
        + ([bits] * 6 + [pltpu.VMEM((BLK // n_dp, width), F32)] + sems) * 3,
        compiler_params=pltpu.CompilerParams(
            collective_id=2, has_side_effects=True, vmem_limit_bytes=VMEM_CAP
        ),
        name="final",
    )(lengths, dqkv, w, attn_in, tokens, stats, gone, dtot, usum, gwo, sums, gbu, gt, *ships)


def finish_kernel(
    count,
    len_ref,
    gin_ref,
    tok_ref,
    st_ref,
    tot_ref,
    gain_ref,
    low_ref,
    wd_ref,
    wu_ref,
    wq_ref,
    out_ref,
    gtok_ref,
    bng_ref,
    bns_ref,
    gw_ref,
    gb_ref,
    gp_ref,
    gx_ref,
    gwo_ref,
    bo_ref,
    g1_ref,
    s1_ref,
    gwu_ref,
    gbu_ref,
    gwd_ref,
    bd_ref,
    g2_ref,
    s2_ref,
):
    own, width = gin_ref.shape
    qcols = 3 * gw_ref.shape[1]
    heads = gp_ref.shape[0]
    piece = LANES
    hd = lax.axis_index("head")
    lens = [len_ref[0, d] for d in range(len_ref.shape[1])]
    mean, inv_std = st_ref[0:1], st_ref[1:2]
    gain = row(gain_ref)
    shift_part = tot_ref[6:7] / count
    gain_part = tot_ref[7:8] / count

    def tokens_out(s, c):
        at = pl.ds(pl.multiple_of(s * piece, piece), piece)
        g = gin_ref[at]
        _, visual, _ = row_layout(iota((piece, LANES), 0) + (hd * own + s * piece), lens)
        x_hat = (tok_ref[at].astype(F32) - mean) * inv_std
        normed = inv_std * gain * (g - (shift_part + x_hat * gain_part))
        gtok_ref[at] = jnp.where(visual[:, 0:1], normed, g)
        return c

    lax.fori_loop(0, own // piece, tokens_out, 0)
    out_ref[...] = low_ref[...]
    gwd_ref[...] = wd_ref[...].astype(F32)
    gwu_ref[...] = wu_ref[...].astype(F32)
    for e in range(3):
        at = slice(e * gw_ref.shape[1], (e + 1) * gw_ref.shape[1])
        gw_ref[e] = wq_ref[at].astype(F32)
    gwo_ref[...] = wq_ref[qcols:].astype(F32)
    for ref, i in (
        (g1_ref, 0),
        (s1_ref, 1),
        (g2_ref, 2),
        (s2_ref, 3),
        (bo_ref, 4),
        (bd_ref, 5),
        (bns_ref, 6),
        (bng_ref, 7),
        (gbu_ref, 8),
    ):
        ref[...] = tot_ref[i : i + 1].reshape(width)
    hcols = qcols // 3
    gb_ref[0:1] = tot_ref[9:10, 0:hcols]
    gb_ref[1:2] = tot_ref[9:10, 2 * hcols : qcols]

    def table(b):
        at = (b % 6) * LANES
        return tot_ref[10 + b // 6 : 11 + b // 6, at : at + LANES]

    for h in range(heads):
        gp_ref[h : h + 1] = table(h)[:, :POSB]
        for e in range(2):
            gx_ref[h, e : e + 1] = table((1 + e) * heads + h)[:, :BOXB]


def finish(lengths, gin, tokens, stats, tot, bn_gain, low, wd, wu, wq, heads, n_dp):
    own, width = gin.shape
    hcols = heads * DH
    count = float(VISUAL * lengths.shape[1] * n_dp)
    vector = jax.ShapeDtypeStruct((width,), F32)
    square = jax.ShapeDtypeStruct((width, width), F32)
    return pl.pallas_call(
        functools.partial(finish_kernel, count),
        out_shape=(
            jax.ShapeDtypeStruct((own, width), BF),
            jax.ShapeDtypeStruct((own, width), F32),
            vector,
            vector,
            jax.ShapeDtypeStruct((3, hcols, width), F32),
            jax.ShapeDtypeStruct((2, hcols), F32),
            jax.ShapeDtypeStruct((heads, POSB), F32),
            jax.ShapeDtypeStruct((heads, 2, BOXB), F32),
            jax.ShapeDtypeStruct((hcols, width), F32),
            vector,
            vector,
            vector,
            square,
            vector,
            square,
            vector,
            vector,
            vector,
        ),
        in_specs=[SM] + [VM] * 9,
        out_specs=(VM,) * 18,
        compiler_params=pltpu.CompilerParams(vmem_limit_bytes=VMEM_CAP),
        name="finish",
    )(lengths, gin, tokens, stats, tot, bn_gain, low, wd, wu, wq)


def body(
    n_dp,
    tokens,
    lengths,
    box_cells,
    bn_gain,
    bn_shift,
    query_key_value_weight,
    b_qv,
    tab_pos,
    tab_box,
    w_out,
    b_out,
    ln1_gain,
    ln1_shift,
    w_up,
    b_up,
    w_down,
    b_down,
    ln2_gain,
    ln2_shift,
    cotangent,
):
    width = tokens.shape[1]
    heads = tab_pos.shape[0]
    w_turned = jnp.swapaxes(query_key_value_weight, 1, 2)
    x_in, attn_in, q0, q1, k0, k1, vx, stats, w_out_all = entry(
        tokens,
        lengths,
        box_cells,
        bn_gain,
        bn_shift,
        w_turned,
        b_qv,
        tab_pos,
        jnp.swapaxes(tab_box, 0, 1),
        w_out,
        n_dp,
    )
    attn, q1b = attend(lengths, q0, q1, k0, k1, vx)
    vectors = (b_out, ln1_gain, ln1_shift, b_up, b_down, ln2_gain, ln2_shift)
    low, grad_one, grad_attn, gwo, dtot, usum, sums, gbu, *ships = middle(
        attn, x_in, cotangent, w_out_all, w_up, w_down, vectors, n_dp
    )
    members = n_dp // 2
    moved = []
    for k, ship in enumerate(ships):
        route = [(d, 2 * ((d // 2 + k + 1) % members) + d % 2) for d in range(n_dp)]
        moved.append(lax.ppermute(ship, "dp", route))
    dqkv, grad_tables = attend_back(lengths, q0, q1b, k0, k1, vx, attn, grad_attn)
    grad_in, total, wd, wu, wq = final(
        lengths,
        dqkv,
        w_turned.reshape(-1, width),
        attn_in,
        tokens,
        stats,
        grad_one,
        dtot,
        usum,
        gwo,
        sums,
        gbu,
        grad_tables,
        moved,
        n_dp,
    )
    outs = list(
        finish(lengths, grad_in, tokens, stats, total, bn_gain, low, wd, wu, wq, heads, n_dp)
    )
    outs[4] = jnp.swapaxes(outs[4], 1, 2)
    outs[7] = jnp.swapaxes(outs[7], 0, 1)
    return tuple(outs)


def solution(mesh):
    rows = P(("dp", "head"), None)
    in_specs = (
        rows,
        P("dp", None),
        P(None, "dp"),
        P(),
        P(),
        P(None, None, "head"),
        P(None, "head"),
        P("head", None),
        P(None, "head", None),
        P("head", None),
        P(),
        P(),
        P(),
        P(None, "head"),
        P("head"),
        P("head", None),
        P(),
        P(),
        P(),
        rows,
    )
    out_specs = (
        rows,
        rows,
        P(),
        P(),
        P(None, None, "head"),
        P(None, "head"),
        P("head", None),
        P(None, "head", None),
        P("head", None),
        P(),
        P(),
        P(),
        P(None, "head"),
        P("head"),
        P("head", None),
        P(),
        P(),
        P(),
    )
    return jax.shard_map(
        functools.partial(body, mesh.shape["dp"]),
        mesh=mesh,
        in_specs=in_specs,
        out_specs=out_specs,
        check_vma=False,
    )
```
